32 devices in a mesh: expert: 16 (over z, y, x), dp: 2 (over core).
Axes of the slice: x: 2, y: 2, z: 4, core: 2. Of those that a mesh axis runs over, the one named last changes fastest.
Arguments:
- tokens: bfloat16 [4096, 2048], P(('expert', 'dp')), may hold values from -6 to 6
- routes: int32 [4096, 8], P(('expert', 'dp')), may hold values from 0 to 15, all different within a row; in each aligned block of 128 rows (0 to 127, 128 to 255, ...) at most 72 rows name the same one
- gates: float32 [4096, 8], P(('expert', 'dp')), may hold values from 0.05 to 1
- cotangent: bfloat16 [4096, 2048], P(('expert', 'dp')), may hold values from -6 to 6
- owner_before: int32 [16], replicated, may hold values from 0 to 15, each once
- owner_after: int32 [16], replicated, may hold values from 0 to 15, each once
- weights: bfloat16 [2, 16, 2048, 768], P(None, 'expert', 'dp'), may hold values from -6 to 6
- m_codes: bfloat16 [2, 16, 2048, 768], P(None, 'expert', 'dp'), may hold values from -7 to 7, as said below
- v_codes: bfloat16 [2, 16, 2048, 768], P(None, 'expert', 'dp'), may hold values from 1 to 7, as said below
- m_scales: bfloat16 [2, 16, 2048], P(None, 'expert', 'dp'), may hold values from 0.049804688 to 0.5
- v_scales: bfloat16 [2, 16, 2048], P(None, 'expert', 'dp'), may hold values from 0.019897461 to 0.19921875
- noise: bfloat16 [2, 16, 2048, 768], P(None, 'expert', 'dp'), may hold values from 0 to 1
Outputs:
- new_weights: bfloat16 [2, 16, 2048, 768], P(None, 'expert', 'dp')
- new_m_codes: bfloat16 [2, 16, 2048, 768], P(None, 'expert', 'dp')
- new_v_codes: bfloat16 [2, 16, 2048, 768], P(None, 'expert', 'dp')
- new_m_scales: bfloat16 [2, 16, 2048], P(None, 'expert', 'dp')
- new_v_scales: bfloat16 [2, 16, 2048], P(None, 'expert', 'dp')
The draws below stay inside these ranges and needn't reach their ends.
Inputs may be any that keep to these rules, and one draw needn't show every extreme that they name: `routes`: in the rows of one device no expert is chosen by more than 72 tokens; each token chooses 8 different experts. `owner_before`: A permutation of the slots. `owner_after`: A permutation of the slots. `m_codes`: whole numbers. `v_codes`: whole numbers.
All inputs are finite; a program needn't handle non-finite values. Where the reference program divides by a largest or mean magnitude, that divisor is 1e-20 or more.
Results may differ from the reference program's by a relative error of at most 0.022.
Values may be sent and summed in bfloat16 or wider, within the bound.
A program may use at most 128 MiB of HBM per device.

```python
import math
import jax
import jax.numpy as jnp
import numpy as np
from jax import lax

D = 2048
FF = 768
TOP = 8
LEVELS = 7
TOK_DEV = 128
CAP = 72
EXPERTS = 16
TOKENS = 4096
N_EXPERT = 16
N_DP = 2


def draw_m_codes(key, part):
    whole = jax.random.randint(jax.random.fold_in(key, 11), (2, EXPERTS, D, FF), -LEVELS, LEVELS + 1, dtype=jnp.int32)
    return whole.astype(jnp.float32).astype(jnp.bfloat16)


def draw_v_codes(key, part):
    whole = jax.random.randint(jax.random.fold_in(key, 23), (2, EXPERTS, D, FF), 1, LEVELS + 1, dtype=jnp.int32)
    return whole.astype(jnp.float32).astype(jnp.bfloat16)


def block_scale(stream_key, dims, pieces, smallest, largest):
    factor_of, own = 1.0, jax.random.fold_in(stream_key, 6)
    for axis_at, parts in pieces:
        steps = jnp.exp(jax.random.uniform(jax.random.fold_in(own, axis_at), (parts,), jnp.float32, smallest / len(pieces), largest / len(pieces)))
        factor_of = factor_of * jnp.repeat(steps, dims[axis_at] // parts).reshape([-1 if axis == axis_at else 1 for axis in range(len(dims))])
    return factor_of


def deal_out(key, own, number, rows, amount, top, reach, lean):
    sequence = jax.random.permutation(key, amount)
    packed, common = shares(amount, rows * top, reach, lean, True), shares(amount, rows * top, reach, lean, False)
    places = jnp.arange(amount)

    def named(lengths, offset_by):
        used = int((lengths > 0).sum())
        fixed = max(1, used // 4)
        moved = fixed + (places - fixed + offset_by * (used - fixed)) % max(1, amount - fixed)
        return jnp.zeros((amount,), jnp.int32).at[sequence[jnp.where(places < fixed, places, moved)]].set(jnp.asarray(lengths, jnp.int32))

    lengths = jnp.where(number % 4 == 0, named(packed, number // 4), named(common, number - number // 4 - 1))
    mixed = jax.random.permutation(jax.random.fold_in(own, 3), amount)
    donor, sink = mixed[0:amount // 2 * 2:2], mixed[1:amount // 2 * 2:2]
    margin = jnp.minimum(lengths[donor] - 1, reach - lengths[sink]) // 2
    margin = jnp.where((donor == sequence[0]) | (sink == sequence[0]) | (lengths[sink] == 0), 0, jnp.maximum(margin, 0))
    moved = jax.random.randint(jax.random.fold_in(own, 4), (amount // 2,), 0, 1 << 20) % (margin + 1)
    lengths = lengths.at[donor].add(-moved).at[sink].add(moved)
    members = jnp.searchsorted(jnp.cumsum(lengths), jnp.arange(rows * top), side="right").astype(jnp.int32)
    table = members.reshape(top, rows).T
    table = table[jax.random.permutation(jax.random.fold_in(own, 1), rows)]
    offset_by = jax.random.randint(jax.random.fold_in(own, 2), (rows, 1), 0, top)
    return jnp.take_along_axis(table, (jnp.arange(top)[None, :] + offset_by) % top, axis=1)


def shares(count, total, reach, skew, full):
    portions = [(1 << 20) // math.isqrt(standing ** skew) + 1 for standing in range(1, count + 1)]
    largest = reach if full else min(reach, max(-(-total // count), total * portions[0] // sum(portions)))
    least = 1 if total - largest >= count - 1 else 0
    counts, surplus = [largest] + [least] * (count - 1), total - largest - least * (count - 1)
    while surplus > 0:
        candidates = [i for i in range(1, count) if counts[i] < largest] or [i for i in range(1, count) if counts[i] < reach]
        mass, left = sum([portions[i] for i in candidates]), surplus
        for i in candidates:
            more = min(reach - counts[i], max(1, left * portions[i] // mass), surplus)
            counts[i] = counts[i] + more
            surplus = surplus - more
    return np.array(counts)


def normal_values(stream_key, dims, scale, most, pieces=(), kind=jnp.bfloat16):
    array = scale * jax.random.normal(stream_key, dims, jnp.float32)
    if pieces:
        array = array * block_scale(stream_key, dims, pieces, -0.22, 0.18)
    return jnp.clip(array, -most, most).astype(kind)


def setup_inputs(seed: int = 0) -> dict:
    key_of = jax.random.split(jax.random.key(seed), 13)
    tokens = normal_values(key_of[0], (TOKENS, D), 1.0, 6.0, ((0, 32),))
    routes_keys = jax.random.split(jax.random.fold_in(key_of[1], 1), TOKENS // TOK_DEV)
    routes_turns = jax.random.permutation(jax.random.fold_in(key_of[1], 3), TOKENS // TOK_DEV)
    routes = jax.vmap(lambda own, number: deal_out(jax.random.fold_in(key_of[1], 2), own, number, TOK_DEV, EXPERTS, TOP, CAP, 0))(routes_keys, routes_turns).reshape((TOKENS, TOP))
    gates = jnp.clip(jnp.exp(math.log(1.0) - 2.9957323 * jax.random.uniform(key_of[2], (TOKENS, TOP), jnp.float32) ** block_scale(key_of[2], (TOKENS, TOP), ((0, 32),), -0.2, 0.2)), 0.05, 1.0)
    cotangent = normal_values(key_of[3], (TOKENS, D), 1.0, 6.0, ((0, 32),))
    owner_before = jax.random.permutation(key_of[4], EXPERTS).astype(jnp.int32)
    owner_after = jax.random.permutation(key_of[5], EXPERTS).astype(jnp.int32)
    weights = normal_values(key_of[6], (2, EXPERTS, D, FF), 1.0, 6.0, ((1, 16), (2, 2)))
    m_codes = draw_m_codes(jax.random.fold_in(key_of[12], 71), 0)
    v_codes = draw_v_codes(jax.random.fold_in(key_of[12], 71), 0)
    m_scales = jnp.clip(jnp.exp(math.log(0.5) - 2.306499 * jax.random.uniform(key_of[9], (2, EXPERTS, D), jnp.float32) ** block_scale(key_of[9], (2, EXPERTS, D), ((1, 16), (2, 2)), -0.2, 0.2)), 0.049804688, 0.5).astype(jnp.bfloat16)
    v_scales = jnp.clip(jnp.exp(math.log(0.19921875) - 2.3038113 * jax.random.uniform(key_of[10], (2, EXPERTS, D), jnp.float32) ** block_scale(key_of[10], (2, EXPERTS, D), ((1, 16), (2, 2)), -0.2, 0.2)), 0.019897461, 0.19921875).astype(jnp.bfloat16)
    noise = jnp.clip(1.0 * jax.random.uniform(key_of[11], (2, EXPERTS, D, FF), jnp.float32) ** block_scale(key_of[11], (2, EXPERTS, D, FF), ((1, 16), (2, 2)), -0.2, 0.2), 0.0, 1.0).astype(jnp.bfloat16)
    return dict(tokens=tokens, routes=routes, gates=gates, cotangent=cotangent, owner_before=owner_before, owner_after=owner_after, weights=weights, m_codes=m_codes, v_codes=v_codes, m_scales=m_scales, v_scales=v_scales, noise=noise)


learn_rate = 0.1
beta_one = 0.9
beta_two = 0.95
adam_step = 20.0
adam_epsilon = 1e-08
scale_epsilon = 1e-06

def transposed_dot(left, right):
    return lax.dot_general(left, right, (((0,), (0,)), ((), ())), preferred_element_type=jnp.float32)

def slot_table(routes):
    device_count = N_EXPERT * N_DP
    entries = routes.reshape(device_count, TOK_DEV * TOP)
    expert_ids = jnp.arange(EXPERTS, dtype=jnp.int32)
    onehot = (entries[:, :, None] == expert_ids[None, None, :]).astype(jnp.int32)
    ranks = lax.optimization_barrier(jnp.sum((jnp.cumsum(onehot, axis=1) - 1) * onehot, axis=2)).astype(jnp.int32)
    sources = jnp.broadcast_to(jnp.arange(device_count, dtype=jnp.int32)[:, None], entries.shape)
    locals_ids = jnp.broadcast_to(jnp.arange(TOK_DEV * TOP, dtype=jnp.int32)[None, :], entries.shape)
    flat_ids = (sources * (TOK_DEV * TOP) + locals_ids).astype(jnp.int32)
    table = jnp.full((EXPERTS, device_count, CAP), -1, jnp.int32)
    return table.at[entries, sources, ranks].set(flat_ids)

def reference(tokens, routes, gates, cotangent, owner_before, owner_after, weights, m_codes, v_codes, m_scales, v_scales, noise):
    table = slot_table(routes)
    flat_gates = gates.reshape(-1)
    slot_ids = jnp.arange(EXPERTS, dtype=jnp.int32)
    holder = jnp.zeros((EXPERTS,), jnp.int32).at[owner_after].set(slot_ids)
    scale_model = D ** (-0.5)
    scale_hidden = FF ** (-0.5)

    def replica_grads(expert, replica, w_up, w_down):
        sources = (jnp.arange(N_EXPERT, dtype=jnp.int32) * N_DP + replica).astype(jnp.int32)
        entry = table[expert][sources].reshape(-1)
        live = entry >= 0
        safe = jnp.where(live, entry, 0).astype(jnp.int32)
        token_rows = (safe // TOP).astype(jnp.int32)
        token_block = jnp.where(live[:, None], tokens[token_rows], jnp.zeros((), tokens.dtype))
        gate_rows = jnp.where(live, flat_gates[safe], jnp.zeros((), flat_gates.dtype))
        gated_block = (gate_rows[:, None] * cotangent[token_rows].astype(jnp.float32)).astype(jnp.bfloat16)
        pre = jnp.dot(token_block, w_up, preferred_element_type=jnp.float32) * scale_model
        hidden = jax.nn.silu(pre).astype(jnp.bfloat16)
        back = jnp.dot(gated_block, w_down, preferred_element_type=jnp.float32) * scale_hidden
        sigmoid_pre = jax.nn.sigmoid(pre)
        pre_grad = (back * sigmoid_pre * (1.0 + pre * (1.0 - sigmoid_pre))).astype(jnp.bfloat16)
        up_part = transposed_dot(token_block, pre_grad) * scale_model
        down_part = transposed_dot(gated_block, hidden) * scale_hidden
        rounded = lax.optimization_barrier(jnp.stack([up_part, down_part]).astype(jnp.bfloat16))
        return rounded.astype(jnp.float32)

    def update_slot(slot):
        expert = holder[slot]
        old_slot = owner_before[expert]
        w_old = weights[:, old_slot]

        def add_replica(replica, total):
            return total + replica_grads(expert, replica, w_old[0], w_old[1])
        grads = lax.fori_loop(0, N_DP, add_replica, jnp.zeros((2, D, FF), jnp.float32))
        m_old = m_codes[:, old_slot].astype(jnp.float32) * m_scales[:, old_slot].astype(jnp.float32)[:, :, None] / LEVELS
        v_old = v_codes[:, old_slot].astype(jnp.float32) * v_scales[:, old_slot].astype(jnp.float32)[:, :, None] / LEVELS
        m_new = beta_one * m_old + (1.0 - beta_one) * grads
        v_new = beta_two * v_old + (1.0 - beta_two) * grads * grads
        direction = m_new / (1.0 - beta_one ** adam_step) / (jnp.sqrt(v_new / (1.0 - beta_two ** adam_step)) + adam_epsilon)
        new_w = (w_old.astype(jnp.float32) - learn_rate * direction).astype(jnp.bfloat16)
        new_ms = lax.optimization_barrier((lax.optimization_barrier(jnp.max(jnp.abs(m_new), axis=2)) + scale_epsilon).astype(jnp.bfloat16))
        new_vs = lax.optimization_barrier((lax.optimization_barrier(jnp.max(v_new, axis=2)) + scale_epsilon).astype(jnp.bfloat16))
        dither = noise[:, slot].astype(jnp.float32)
        m_value = LEVELS * m_new / new_ms.astype(jnp.float32)[:, :, None] + (dither - 0.5)
        v_value = LEVELS * v_new / new_vs.astype(jnp.float32)[:, :, None] + dither
        new_mc = jnp.clip(m_value, -1.0 * LEVELS, 1.0 * LEVELS).astype(jnp.bfloat16)
        new_vc = jnp.clip(v_value, 0.0, 1.0 * LEVELS).astype(jnp.bfloat16)
        return (new_w, new_mc, new_vc, new_ms, new_vs)
    results = lax.map(update_slot, slot_ids)
    return (jnp.moveaxis(results[0], 0, 1), jnp.moveaxis(results[1], 0, 1), jnp.moveaxis(results[2], 0, 1), jnp.moveaxis(results[3], 0, 1), jnp.moveaxis(results[4], 0, 1))
```

```python
import functools

import jax
import jax.numpy as jnp
from jax import lax
from jax.experimental import pallas as pl
from jax.experimental.pallas import tpu as pltpu
from jax.sharding import PartitionSpec as P

LEVELS = 7


learn_rate = 0.1
beta_one = 0.9
beta_two = 0.95
adam_step = 20.0
adam_epsilon = 1e-08
scale_epsilon = 1e-06

MESH = pl.DeviceIdType.MESH
ANY = pl.ANY
HALVES = 2
ROWS_AT_ONCE = 32


def transposed_dot(left, right):
    return lax.dot_general(
        left, right, (((0,), (0,)), ((), ())), preferred_element_type=jnp.float32
    )


def adam_kernel(parts, *refs):
    weight, m_code, v_code, m_scale, v_scale, noise, new_w, new_m, new_v, new_ms, new_vs = refs[parts:]
    grads = refs[0][...].astype(jnp.float32)
    for part in refs[1:parts]:
        grads += part[...].astype(jnp.float32)
    m_old = m_code[...].astype(jnp.float32) * (m_scale[...].astype(jnp.float32) / LEVELS)
    v_old = v_code[...].astype(jnp.float32) * (v_scale[...].astype(jnp.float32) / LEVELS)
    m_new = beta_one * m_old + (1.0 - beta_one) * grads
    v_new = beta_two * v_old + (1.0 - beta_two) * grads * grads
    direction = (
        m_new
        * (1.0 / (1.0 - beta_one**adam_step))
        / (jnp.sqrt(v_new * (1.0 / (1.0 - beta_two**adam_step))) + adam_epsilon)
    )
    new_w[...] = (weight[...].astype(jnp.float32) - learn_rate * direction).astype(jnp.bfloat16)
    m_top = (jnp.max(jnp.abs(m_new), axis=1, keepdims=True) + scale_epsilon).astype(jnp.bfloat16)
    v_top = (jnp.max(v_new, axis=1, keepdims=True) + scale_epsilon).astype(jnp.bfloat16)
    new_ms[...] = m_top
    new_vs[...] = v_top
    dither = noise[...].astype(jnp.float32)
    m_value = m_new * (LEVELS / m_top.astype(jnp.float32)) + (dither - 0.5)
    v_value = v_new * (LEVELS / v_top.astype(jnp.float32)) + dither
    new_m[...] = jnp.clip(m_value, -1.0 * LEVELS, 1.0 * LEVELS).astype(jnp.bfloat16)
    new_v[...] = jnp.clip(v_value, 0.0, 1.0 * LEVELS).astype(jnp.bfloat16)


def adam(grads, weight, m_code, v_code, m_scale, v_scale, noise):
    rows, width = weight.shape
    block = min(256, rows)
    wide = pl.BlockSpec((block, width), lambda i: (i, 0))
    thin = pl.BlockSpec((block, 1), lambda i: (i, 0))
    big = jax.ShapeDtypeStruct((rows, width), jnp.bfloat16)
    small = jax.ShapeDtypeStruct((rows, 1), jnp.bfloat16)
    return pl.pallas_call(
        functools.partial(adam_kernel, len(grads)),
        grid=(rows // block,),
        out_shape=(big, big, big, small, small),
        in_specs=[wide] * len(grads) + [wide, wide, wide, thin, thin, wide],
        out_specs=(wide, wide, wide, thin, thin),
        name="adam",
        cost_estimate=pl.CostEstimate(
            flops=30 * rows * width, bytes_accessed=16 * rows * width, transcendentals=2 * rows * width
        ),
    )(*grads, weight, m_code, v_code, m_scale, v_scale, noise)


def plan_kernel(line, inner, steps, dest_ref, dest_col_ref, moves_ref, last_ref, used_ref):
    count = line * inner
    lanes = dest_ref.shape[1]
    shape = (2 * line, lanes)
    lane = lax.broadcasted_iota(jnp.int32, shape, 1)
    row = lax.broadcasted_iota(jnp.int32, shape, 0)
    node, down = row // 2, row % 2
    dest = jnp.broadcast_to(dest_ref[...], shape)
    goal = dest // inner
    here = jnp.where(lane < count, lane // inner, -1)
    slot = lane % inner
    used = jnp.zeros((8, lanes), jnp.int32)
    far = jnp.abs(goal - node)
    wants = (goal - node) * (1 - 2 * down) > 0
    for step in range(steps):
        score = jnp.where((here == node) & wants, far * lanes + (lanes - 1 - lane), -1)
        best = jnp.max(score, axis=1, keepdims=True)
        chosen = (score == best) & (score >= 0)
        sent = jnp.max(jnp.where(chosen, slot, 0), axis=1, keepdims=True)
        moves_ref[step] = jnp.broadcast_to(sent, shape)
        move = jnp.sum(jnp.where(chosen, 1 - 2 * down, 0), axis=0, keepdims=True)
        move = jnp.broadcast_to(move, shape)
        here = here + move
        moved = move * move
        slot = slot * (1 - moved) + moved * (inner + 2 * step) + (moved - move) // 2
        any_sent = jnp.minimum(jnp.max(best, axis=0, keepdims=True) + 1, 1)
        used = jnp.maximum(used, jnp.broadcast_to(any_sent, used.shape) * (step + 1))
    used_ref[...] = used
    wanted = lax.broadcasted_iota(jnp.int32, (count, lanes), 0)
    slots = jnp.broadcast_to(slot[0:1, :], (count, lanes))
    hits = jnp.where(jnp.broadcast_to(dest_ref[...], (count, lanes)) == wanted, slots, 0)
    last_ref[...] = jnp.broadcast_to(jnp.sum(hits, axis=1, keepdims=True), (count, lanes))


def plan(dest, line, inner, steps):
    count, lanes = line * inner, 128
    wide = jnp.full((1, lanes), -1, jnp.int32)
    wide = lax.dynamic_update_slice(wide, dest[None, :], (0, 0))
    moves, last, used = pl.pallas_call(
        functools.partial(plan_kernel, line, inner, steps),
        out_shape=(
            jax.ShapeDtypeStruct((steps, 2 * line, lanes), jnp.int32),
            jax.ShapeDtypeStruct((count, lanes), jnp.int32),
            jax.ShapeDtypeStruct((8, lanes), jnp.int32),
        ),
        name="plan",
    )(wide, dest[:, None])
    table = jnp.concatenate([last[:, 0], moves[:, :, 0].reshape(-1)])
    return table, used[0, 0]


def move_kernel(line, inner, steps, table, tok_in, cot_in, small_in, *refs):
    arrays = 3
    chunks = arrays * HALVES
    own = (tok_in, cot_in, small_in)
    sources = refs[:arrays]
    moved = refs[arrays : 2 * arrays]
    gathered = refs[2 * arrays : 3 * arrays]
    rest = list(refs[3 * arrays :])
    slots = rest[:chunks]
    (b_buf, c_buf, a_send, a_recv, a_local, b_send, b_recv, credit, c_send, c_recv, c_local,
     z_send, z_recv, p_send, p_recv, o_local) = rest[chunks:]
    me = lax.axis_index("expert")
    z, p = me // inner, me % inner
    x, y = p % 2, p // 2
    mates = (y * 2 + (1 - x), (1 - y) * 2 + x, (1 - y) * 2 + (1 - x))
    rows = slots[0].shape[1]
    above, below = z < line - 1, z > 0

    def at(place):
        return {"expert": place}

    def remote(src, dst, send, recv, place):
        return pltpu.make_async_remote_copy(
            src_ref=src, dst_ref=dst, send_sem=send, recv_sem=recv,
            device_id=at(place), device_id_type=MESH,
        )

    barrier = pltpu.get_barrier_semaphore()
    for mate in mates:
        pl.semaphore_signal(barrier, inc=1, device_id=at(z * inner + mate), device_id_type=MESH)

    @pl.when(above)
    def _():
        pl.semaphore_signal(barrier, inc=1, device_id=at(me + inner), device_id_type=MESH)

    @pl.when(below)
    def _():
        pl.semaphore_signal(barrier, inc=1, device_id=at(me - inner), device_id_type=MESH)

    middle = above & below

    @pl.when(middle)
    def _():
        pl.semaphore_wait(barrier, len(mates) + 2)

    @pl.when(jnp.logical_not(middle))
    def _():
        pl.semaphore_wait(barrier, len(mates) + 1)

    def block(array, plane, place):
        return gathered[array].at[plane * inner + place]

    def line_copy(array, hop, down):
        if down:
            plane, place, = z + hop, me - inner
        else:
            plane, place = z - hop, me + inner
        src = own[array] if hop == 0 else block(array, plane, p)
        return remote(src, block(array, plane, p), z_send.at[array, down, hop], z_recv.at[array, down, hop], place)

    def line_has(hop, down):
        return (below & (z + hop < line)) if down else (above & (z - hop >= 0))

    def line_send(hop):
        for down in range(2):
            @pl.when(line_has(hop, down))
            def _():
                for array in range(arrays):
                    line_copy(array, hop, down).start()

    def line_drain(hop):
        for down in range(2):
            @pl.when(line_has(hop, down))
            def _():
                for array in range(arrays):
                    line_copy(array, hop, down).wait_send()

    def line_came(hop, down):
        return (z + hop + 1 < line) if down else (z - hop - 1 >= 0)

    def line_recv(hop):
        for down in range(2):
            @pl.when(line_came(hop, down))
            def _():
                plane = z + hop + 1 if down else z - hop - 1
                for array in range(arrays):
                    dst = block(array, plane, p)
                    remote(dst, dst, z_send.at[array, down, hop], z_recv.at[array, down, hop], me).wait_recv()

    def halves(array):
        size = own[array].shape[0] // 2
        return pl.ds(0, size), pl.ds(size, size)

    def plane_copy(array, plane, kind, first):
        sems = p_send.at[array, plane, kind], p_recv.at[array, plane, kind]
        if kind < 2:
            dst = block(array, plane, p)
            src = own[array] if first else dst
            return remote(src, dst, *sems, z * inner + mates[kind])
        near = mates[kind - 2]
        part = block(array, plane, near).at[halves(array)[kind - 2]]
        return remote(part, part, *sems, z * inner + mates[3 - kind])

    def plane_got(array, plane, kind):
        sems = p_send.at[array, plane, kind], p_recv.at[array, plane, kind]
        if kind < 2:
            dst = block(array, plane, mates[kind])
        else:
            dst = block(array, plane, mates[2]).at[halves(array)[kind - 2]]
        return remote(dst, dst, *sems, me)

    def plane_first(plane, first=False):
        for array in range(arrays):
            for kind in range(2):
                plane_copy(array, plane, kind, first).start()

    def plane_second(plane):
        for array in range(arrays):
            for kind in range(2):
                plane_got(array, plane, kind).wait_recv()
            for kind in range(2, 4):
                plane_copy(array, plane, kind, False).start()

    def plane_end(plane):
        for array in range(arrays):
            for kind in range(2, 4):
                plane_got(array, plane, kind).wait_recv()
            for kind in range(4):
                plane_copy(array, plane, kind, False).wait_send()

    def by_hop(hop, action):
        for down in range(2):
            @pl.when(line_came(hop, down))
            def _():
                action(z + hop + 1 if down else z - hop - 1)

    def source_piece(chunk, place):
        return sources[chunk // HALVES].at[place, pl.ds(chunk % HALVES * rows, rows)]

    def moved_piece(chunk, place):
        return moved[chunk // HALVES].at[place, pl.ds(chunk % HALVES * rows, rows)]

    def spread_copy(chunk, k):
        return remote(source_piece(chunk, mates[k]), slots[chunk].at[p],
                      a_send.at[chunk, k], a_recv.at[chunk, k], z * inner + mates[k])

    def spread_local(chunk):
        return pltpu.make_async_copy(source_piece(chunk, p), slots[chunk].at[p], a_local.at[chunk])

    def spread_start(chunk):
        for k in range(3):
            spread_copy(chunk, k).start()
        spread_local(chunk).start()

    def spread_wait(chunk):
        for k in range(3):
            dst = slots[chunk].at[mates[k]]
            remote(dst, dst, a_send.at[chunk, k], a_recv.at[chunk, k], me).wait_recv()
        spread_local(chunk).wait()

    def line_step_copy(chunk, step, down):
        place = me - inner if down else me + inner
        return remote(b_buf.at[chunk % 2, down], slots[chunk].at[inner + 2 * step + down],
                      b_send.at[chunk % 2, down], b_recv.at[chunk, down], place)

    def step_recv(chunk, step):
        for down in range(2):
            @pl.when(above if down else below)
            def _():
                dst = slots[chunk].at[inner + 2 * step + down]
                remote(dst, dst, b_send.at[chunk % 2, down], b_recv.at[chunk, down], me).wait_recv()

    def pick(chunk, index, dst):
        def body(i, carry):
            part = pl.ds(i * ROWS_AT_ONCE, ROWS_AT_ONCE)
            dst[part, :] = slots[chunk][index, part, :]
            return carry

        lax.fori_loop(0, rows // ROWS_AT_ONCE, body, 0)

    def step_drain(chunk, step):
        for down in range(2):
            @pl.when(below if down else above)
            def _():
                line_step_copy(chunk, step, down).wait_send()

    def step_send(chunk, step, before):
        if before is not None:
            step_drain(*before)
        for down in range(2):
            @pl.when(below if down else above)
            def _():
                index = table[line * inner + step * 2 * line + z * 2 + down]
                pick(chunk, index, b_buf.at[chunk % 2, down])
        for down in range(2):
            @pl.when(below if down else above)
            def _():
                pl.semaphore_signal(credit.at[chunk, 1 - down], inc=1,
                                    device_id=at(me - inner if down else me + inner), device_id_type=MESH)
        for down in range(2):
            @pl.when(below if down else above)
            def _():
                pl.semaphore_wait(credit.at[chunk, down], 1)
                line_step_copy(chunk, step, down).start()

    def collect_copy(chunk, k):
        return remote(c_buf.at[chunk % 2, k], moved_piece(chunk, p),
                      c_send.at[chunk, k], c_recv.at[chunk, k], z * inner + mates[k])

    def collect_local(chunk):
        return pltpu.make_async_copy(c_buf.at[chunk % 2, 3], moved_piece(chunk, p), c_local.at[chunk])

    def collect_drain(chunk):
        for k in range(3):
            collect_copy(chunk, k).wait_send()
        collect_local(chunk).wait()

    def collect_send(chunk):
        step_recv(chunk, steps - 1)
        if chunk >= 2:
            collect_drain(chunk - 2)
        for k in range(4):
            place = mates[k] if k < 3 else p
            pick(chunk, table[z * inner + place], c_buf.at[chunk % 2, k])
            if k < 3:
                collect_copy(chunk, k).start()
        collect_local(chunk).start()

    def collect_wait(chunk):
        for k in range(3):
            dst = moved_piece(chunk, mates[k])
            remote(dst, dst, c_send.at[chunk, k], c_recv.at[chunk, k], me).wait_recv()

    own_copies = [pltpu.make_async_copy(own[a], block(a, z, p), o_local.at[a]) for a in range(arrays)]
    for chunk in range(2):
        spread_start(chunk)
    line_send(0)
    for chunk in range(2, chunks):
        spread_start(chunk)
    for copy in own_copies:
        copy.start()
    plane_first(z, first=True)

    hooks = {}
    for hop in range(line - 1):
        hooks.setdefault(1 + 2 * hop, []).append(functools.partial(line_recv, hop))
        if hop + 1 < line - 1:
            hooks[1 + 2 * hop].append(functools.partial(line_send, hop + 1))
        hooks[1 + 2 * hop].append(functools.partial(by_hop, hop, plane_first))
    total = chunks * steps
    for hop in range(line - 1):
        hooks.setdefault(min(total - 1, 15 + 2 * hop), []).append(functools.partial(by_hop, hop, plane_second))
    hooks.setdefault(13 if total > 13 else total - 1, []).append(lambda: plane_second(z))

    previous = {}
    number = 0
    for pair in range(chunks // 2):
        for step in range(steps):
            for chunk in (2 * pair, 2 * pair + 1):
                if step == 0:
                    spread_wait(chunk)
                else:
                    step_recv(chunk, step - 1)
                step_send(chunk, step, previous.get(chunk % 2))
                previous[chunk % 2] = (chunk, step)
                if step == 0 and pair > 0:
                    collect_send(chunk - 2)
                for hook in hooks.get(number, []):
                    hook()
                number += 1
    for chunk in (chunks - 2, chunks - 1):
        collect_send(chunk)

    for chunk in (chunks - 2, chunks - 1):
        step_drain(*previous[chunk % 2])
        collect_drain(chunk)
    for chunk in range(chunks):
        for k in range(3):
            spread_copy(chunk, k).wait_send()
        collect_wait(chunk)
    for copy in own_copies:
        copy.wait()
    for hop in range(line - 1):
        line_drain(hop)
        by_hop(hop, plane_end)
    plane_end(z)


def move(line, inner, steps, number, table, tokens, cotangent, small, arrays):
    count = line * inner
    places, wide_rows, width = arrays[0].shape
    rows = wide_rows // HALVES
    chunks = len(arrays) * HALVES
    dma, regular = pltpu.SemaphoreType.DMA, pltpu.SemaphoreType.REGULAR
    gathers = (tokens, cotangent, small)
    vmem = pl.BlockSpec(memory_space=pltpu.VMEM)
    anywhere = pl.BlockSpec(memory_space=ANY)
    return pl.pallas_call(
        functools.partial(move_kernel, line, inner, steps),
        out_shape=tuple(jax.ShapeDtypeStruct(a.shape, a.dtype) for a in arrays)
        + tuple(jax.ShapeDtypeStruct((count,) + g.shape, g.dtype) for g in gathers),
        in_specs=[pl.BlockSpec(memory_space=pltpu.SMEM)] + [vmem] * 3 + [anywhere] * len(arrays),
        out_specs=tuple([anywhere] * (len(arrays) + 3)),
        scratch_shapes=[pltpu.VMEM((inner + 2 * steps, rows, width), jnp.bfloat16) for _ in range(chunks)]
        + [
            pltpu.VMEM((2, 2, rows, width), jnp.bfloat16),
            pltpu.VMEM((2, 4, rows, width), jnp.bfloat16),
            dma((chunks, 3)), dma((chunks, 3)), dma((chunks,)),
            dma((2, 2)), dma((chunks, 2)), regular((chunks, 2)),
            dma((chunks, 3)), dma((chunks, 3)), dma((chunks,)),
            dma((3, 2, line - 1)), dma((3, 2, line - 1)),
            dma((3, line, 4)), dma((3, line, 4)),
            dma((3,)),
        ],
        compiler_params=pltpu.CompilerParams(
            collective_id=number, has_side_effects=True, vmem_limit_bytes=60 * 1024 * 1024
        ),
        name="move%d" % steps,
    )(table, tokens, cotangent, small, *arrays)


def planes_on_device(
    tokens, routes, gates, cotangent, owner_before, owner_after,
    weights, m_codes, v_codes, m_scales, v_scales, noise, inner,
):
    expert_count = lax.axis_size("expert")
    dp_count = lax.axis_size("dp")
    me = lax.axis_index("expert")
    my_dp = lax.axis_index("dp")
    line = expert_count // inner
    most = 2 * inner
    slot_ids = jnp.arange(expert_count, dtype=jnp.int32)
    from_slot = (owner_before[None, :] == slot_ids[:, None]).astype(jnp.int32)
    dest = jnp.sum(from_slot * owner_after[None, :], axis=1)
    my_match = (owner_after == me).astype(jnp.int32)
    my_expert = jnp.sum(my_match * slot_ids)
    my_source = jnp.sum(my_match * owner_before)
    rows_dp = weights.shape[2]
    hidden_units = weights.shape[3]
    model_width = tokens.shape[1]
    token_count = tokens.shape[0]

    def shift(array, step):
        ring = [(i, (i + step) % dp_count) for i in range(dp_count)]
        return lax.ppermute(array, "dp", ring)

    dense_gates = jnp.sum(
        jnp.where(routes[:, :, None] == slot_ids[None, None, :], gates[:, :, None], 0.0), axis=1
    ).T
    scales = jnp.concatenate([m_scales.reshape(-1), v_scales.reshape(-1)]).astype(jnp.float32)
    small = jnp.concatenate([dense_gates, scales.reshape(-1, token_count)])

    table, used = plan(dest, line, inner, most)
    arrays = tuple(a.reshape(inner, 2 * rows_dp // inner, hidden_units) for a in (weights, m_codes, v_codes))
    sizes = [inner, inner + 1, most]
    branch = sum([(used > s).astype(jnp.int32) for s in sizes[:-1]])
    moved_weights, moved_m, moved_v, all_tokens, all_cotangent, all_small = lax.switch(
        branch,
        [functools.partial(move, line, inner, s, i) for i, s in enumerate(sizes)],
        table, tokens, cotangent, small, arrays,
    )
    moved_weights, moved_m, moved_v, all_tokens, all_cotangent, all_small = lax.optimization_barrier(
        (moved_weights, moved_m, moved_v, all_tokens, all_cotangent, all_small)
    )
    all_tokens = all_tokens.reshape(-1, model_width)
    all_cotangent = all_cotangent.reshape(-1, model_width)
    gate = lax.dynamic_index_in_dim(all_small, my_expert, axis=1, keepdims=False).reshape(-1)
    old_scales = lax.dynamic_index_in_dim(all_small, my_source, axis=0, keepdims=False)[expert_count:]
    old_scales = old_scales.reshape(2, 2 * rows_dp)

    own_rows = moved_weights.reshape(2, rows_dp, hidden_units)
    full_weights = jnp.zeros((2, dp_count * rows_dp, hidden_units), jnp.bfloat16)
    full_weights = lax.dynamic_update_slice(full_weights, own_rows, (0, my_dp * rows_dp, 0))
    for step in range(1, dp_count):
        start = (my_dp - step) % dp_count * rows_dp
        full_weights = lax.dynamic_update_slice(full_weights, shift(own_rows, step), (0, start, 0))
    gated = (gate[:, None] * all_cotangent.astype(jnp.float32)).astype(jnp.bfloat16)
    scale_model = model_width ** (-0.5)
    scale_hidden = hidden_units ** (-0.5)
    pre = jnp.dot(all_tokens, full_weights[0], preferred_element_type=jnp.float32) * scale_model
    back = jnp.dot(gated, full_weights[1], preferred_element_type=jnp.float32) * scale_hidden
    sigmoid_pre = jax.nn.sigmoid(pre)
    hidden = (pre * sigmoid_pre).astype(jnp.bfloat16)
    pre_grad = (back * sigmoid_pre * (1.0 + pre * (1.0 - sigmoid_pre))).astype(jnp.bfloat16)
    up_part = (transposed_dot(all_tokens, pre_grad) * scale_model).astype(jnp.bfloat16)
    down_part = (transposed_dot(gated, hidden) * scale_hidden).astype(jnp.bfloat16)
    part = jnp.stack([up_part, down_part])
    grads = []
    for step in range(dp_count):
        start = (my_dp + step) % dp_count * rows_dp
        mine = lax.dynamic_slice(part, (0, start, 0), (2, rows_dp, hidden_units))
        grads.append((shift(mine, step) if step else mine).reshape(2 * rows_dp, hidden_units))
    new_w, new_m, new_v, new_ms, new_vs = adam(
        grads,
        moved_weights.reshape(2 * rows_dp, hidden_units),
        moved_m.reshape(2 * rows_dp, hidden_units),
        moved_v.reshape(2 * rows_dp, hidden_units),
        old_scales[0][:, None],
        old_scales[1][:, None],
        noise.reshape(2 * rows_dp, hidden_units),
    )
    return (
        new_w.reshape(2, 1, rows_dp, hidden_units),
        new_m.reshape(2, 1, rows_dp, hidden_units),
        new_v.reshape(2, 1, rows_dp, hidden_units),
        new_ms.reshape(2, 1, rows_dp),
        new_vs.reshape(2, 1, rows_dp),
    )


def on_device(
    tokens,
    routes,
    gates,
    cotangent,
    owner_before,
    owner_after,
    weights,
    m_codes,
    v_codes,
    m_scales,
    v_scales,
    noise,
):
    expert_count = lax.axis_size("expert")
    me = lax.axis_index("expert")
    slot_ids = jnp.arange(expert_count, dtype=jnp.int32)
    matches = (owner_after[None, :] == slot_ids[:, None]).astype(jnp.int32)
    source_slot = jnp.sum(matches * owner_before[None, :], axis=1)
    my_match = (owner_after == me).astype(jnp.int32)
    my_expert = jnp.sum(my_match * slot_ids)
    my_source = jnp.sum(my_match * owner_before)
    rows_dp = weights.shape[2]
    hidden_units = weights.shape[3]
    model_width = tokens.shape[1]
    token_count = tokens.shape[0]
    piece = 2 * rows_dp // expert_count

    dp_count = lax.axis_size("dp")
    my_dp = lax.axis_index("dp")

    def spread(array):
        shaped = array.reshape(expert_count, piece, hidden_units)
        return lax.all_to_all(shaped, "expert", split_axis=0, concat_axis=0, tiled=True)

    def collect(array):
        return lax.all_to_all(array, "expert", split_axis=0, concat_axis=0, tiled=True)

    def regroup(array):
        return array.at[source_slot].get(mode="promise_in_bounds")

    def shift(array, step):
        ring = [(i, (i + step) % dp_count) for i in range(dp_count)]
        return lax.ppermute(array, "dp", ring)

    dense_gates = jnp.sum(
        jnp.where(routes[:, :, None] == slot_ids[None, None, :], gates[:, :, None], 0.0), axis=1
    ).T
    scales = jnp.concatenate([m_scales.reshape(-1), v_scales.reshape(-1)]).astype(jnp.float32)
    small = jnp.concatenate([dense_gates, scales.reshape(-1, token_count)])
    all_small = lax.all_gather(small, "expert", axis=0, tiled=False)
    inner = 1
    while inner * inner * 4 <= expert_count and expert_count % (inner * 2) == 0:
        inner *= 2
    outer = expert_count // inner
    lines = [[i + inner * k for k in range(outer)] for i in range(inner)]
    planes = [[inner * k + i for i in range(inner)] for k in range(outer)]

    def gather_line(array):
        return lax.all_gather(array, "expert", axis=0, tiled=True, axis_index_groups=lines)

    def gather_plane(array):
        return lax.all_gather(array, "expert", axis=0, tiled=True, axis_index_groups=planes)

    line_tokens, all_small = lax.optimization_barrier((gather_line(tokens), all_small))
    all_tokens = gather_plane(line_tokens)
    all_cotangent = gather_plane(gather_line(cotangent))

    weights_ready, all_small = lax.optimization_barrier((regroup(spread(weights)), all_small))
    gate = lax.dynamic_index_in_dim(all_small, my_expert, axis=1, keepdims=False)
    gate = gate.reshape(outer, inner, token_count).swapaxes(0, 1).reshape(-1)
    old_scales = lax.dynamic_index_in_dim(all_small, my_source, axis=0, keepdims=False)[expert_count:]
    old_scales = old_scales.reshape(2, 2 * rows_dp)
    moved_weights = collect(weights_ready)
    moved_weights, m_codes = lax.optimization_barrier((moved_weights, m_codes))
    m_spread = spread(m_codes)
    m_spread, v_codes = lax.optimization_barrier((m_spread, v_codes))
    v_spread = spread(v_codes)
    m_ready, v_spread = lax.optimization_barrier((regroup(m_spread), v_spread))
    moved_m = collect(m_ready)
    v_ready, moved_m = lax.optimization_barrier((regroup(v_spread), moved_m))
    moved_v = collect(v_ready)
    moved_m, all_cotangent = lax.optimization_barrier((moved_m, all_cotangent))

    own_rows = moved_weights.reshape(2, rows_dp, hidden_units)
    full_weights = jnp.zeros((2, dp_count * rows_dp, hidden_units), jnp.bfloat16)
    full_weights = lax.dynamic_update_slice(full_weights, own_rows, (0, my_dp * rows_dp, 0))
    for step in range(1, dp_count):
        start = (my_dp - step) % dp_count * rows_dp
        full_weights = lax.dynamic_update_slice(full_weights, shift(own_rows, step), (0, start, 0))
    gated = (gate[:, None] * all_cotangent.astype(jnp.float32)).astype(jnp.bfloat16)
    scale_model = model_width ** (-0.5)
    scale_hidden = hidden_units ** (-0.5)
    pre = jnp.dot(all_tokens, full_weights[0], preferred_element_type=jnp.float32) * scale_model
    back = jnp.dot(gated, full_weights[1], preferred_element_type=jnp.float32) * scale_hidden
    sigmoid_pre = jax.nn.sigmoid(pre)
    hidden = (pre * sigmoid_pre).astype(jnp.bfloat16)
    pre_grad = (back * sigmoid_pre * (1.0 + pre * (1.0 - sigmoid_pre))).astype(jnp.bfloat16)
    up_part = (transposed_dot(all_tokens, pre_grad) * scale_model).astype(jnp.bfloat16)
    down_part = (transposed_dot(gated, hidden) * scale_hidden).astype(jnp.bfloat16)
    part = jnp.stack([up_part, down_part])
    grads = []
    for step in range(dp_count):
        start = (my_dp + step) % dp_count * rows_dp
        mine = lax.dynamic_slice(part, (0, start, 0), (2, rows_dp, hidden_units))
        grads.append((shift(mine, step) if step else mine).reshape(2 * rows_dp, hidden_units))
    new_w, new_m, new_v, new_ms, new_vs = adam(
        grads,
        moved_weights.reshape(2 * rows_dp, hidden_units),
        moved_m.reshape(2 * rows_dp, hidden_units),
        moved_v.reshape(2 * rows_dp, hidden_units),
        old_scales[0][:, None],
        old_scales[1][:, None],
        noise.reshape(2 * rows_dp, hidden_units),
    )
    return (
        new_w.reshape(2, 1, rows_dp, hidden_units),
        new_m.reshape(2, 1, rows_dp, hidden_units),
        new_v.reshape(2, 1, rows_dp, hidden_units),
        new_ms.reshape(2, 1, rows_dp),
        new_vs.reshape(2, 1, rows_dp),
    )


def solution(mesh):
    placed = (
        P(("expert", "dp"), None),
        P(("expert", "dp"), None),
        P(("expert", "dp"), None),
        P(("expert", "dp"), None),
        P(),
        P(),
        P(None, "expert", "dp", None),
        P(None, "expert", "dp", None),
        P(None, "expert", "dp", None),
        P(None, "expert", "dp"),
        P(None, "expert", "dp"),
        P(None, "expert", "dp", None),
    )
    inner = 4
    line = mesh.shape["expert"] // inner
    in_planes = mesh.shape["dp"] == 2 and mesh.shape["expert"] == line * inner and 2 <= line <= 4
    program = functools.partial(planes_on_device, inner=inner) if in_planes else on_device
    return jax.shard_map(
        program,
        mesh=mesh,
        in_specs=placed,
        out_specs=(
            P(None, "expert", "dp", None),
            P(None, "expert", "dp", None),
            P(None, "expert", "dp", None),
            P(None, "expert", "dp"),
            P(None, "expert", "dp"),
        ),
        check_vma=False,
    )
```

```python
import functools

import jax
import jax.numpy as jnp
from jax import lax
from jax.experimental import pallas as pl
from jax.experimental.pallas import tpu as pltpu
from jax.sharding import PartitionSpec as P

LEVELS = 7


learn_rate = 0.1
beta_one = 0.9
beta_two = 0.95
adam_step = 20.0
adam_epsilon = 1e-08
scale_epsilon = 1e-06

MESH = pl.DeviceIdType.MESH
ANY = pl.ANY
HALVES = 2
ROWS_AT_ONCE = 32
COLUMNS = 512


def transposed_dot(left, right):
    return lax.dot_general(
        left, right, (((0,), (0,)), ((), ())), preferred_element_type=jnp.float32
    )


def adam_kernel(parts, *refs):
    weight, m_code, v_code, m_scale, v_scale, noise, new_w, new_m, new_v, new_ms, new_vs = refs[parts:]
    grads = refs[0][...].astype(jnp.float32)
    for part in refs[1:parts]:
        grads += part[...].astype(jnp.float32)
    m_old = m_code[...].astype(jnp.float32) * (m_scale[...].astype(jnp.float32) / LEVELS)
    v_old = v_code[...].astype(jnp.float32) * (v_scale[...].astype(jnp.float32) / LEVELS)
    m_new = beta_one * m_old + (1.0 - beta_one) * grads
    v_new = beta_two * v_old + (1.0 - beta_two) * grads * grads
    direction = (
        m_new
        * (1.0 / (1.0 - beta_one**adam_step))
        / (jnp.sqrt(v_new * (1.0 / (1.0 - beta_two**adam_step))) + adam_epsilon)
    )
    new_w[...] = (weight[...].astype(jnp.float32) - learn_rate * direction).astype(jnp.bfloat16)
    m_top = (jnp.max(jnp.abs(m_new), axis=1, keepdims=True) + scale_epsilon).astype(jnp.bfloat16)
    v_top = (jnp.max(v_new, axis=1, keepdims=True) + scale_epsilon).astype(jnp.bfloat16)
    new_ms[...] = m_top
    new_vs[...] = v_top
    dither = noise[...].astype(jnp.float32)
    m_value = m_new * (LEVELS / m_top.astype(jnp.float32)) + (dither - 0.5)
    v_value = v_new * (LEVELS / v_top.astype(jnp.float32)) + dither
    new_m[...] = jnp.clip(m_value, -1.0 * LEVELS, 1.0 * LEVELS).astype(jnp.bfloat16)
    new_v[...] = jnp.clip(v_value, 0.0, 1.0 * LEVELS).astype(jnp.bfloat16)


def adam(grads, weight, m_code, v_code, m_scale, v_scale, noise):
    rows, width = weight.shape
    block = min(256, rows)
    wide = pl.BlockSpec((block, width), lambda i: (i, 0))
    thin = pl.BlockSpec((block, 1), lambda i: (i, 0))
    big = jax.ShapeDtypeStruct((rows, width), jnp.bfloat16)
    small = jax.ShapeDtypeStruct((rows, 1), jnp.bfloat16)
    return pl.pallas_call(
        functools.partial(adam_kernel, len(grads)),
        grid=(rows // block,),
        out_shape=(big, big, big, small, small),
        in_specs=[wide] * len(grads) + [wide, wide, wide, thin, thin, wide],
        out_specs=(wide, wide, wide, thin, thin),
        name="adam",
        cost_estimate=pl.CostEstimate(
            flops=30 * rows * width, bytes_accessed=16 * rows * width, transcendentals=2 * rows * width
        ),
    )(*grads, weight, m_code, v_code, m_scale, v_scale, noise)


def adam_rows(my_dp, part, other, full, m_code, v_code, m_scale, v_scale, noise):
    rows, width = m_code.shape
    block = min(256, rows // 2)
    per = rows // 2 // block
    wide = pl.BlockSpec((block, width), lambda i, dp: (i, 0))
    held = pl.BlockSpec((block, width), lambda i, dp: (i // per * 2 * per + dp[0] * per + i % per, 0))
    thin = pl.BlockSpec((block, 1), lambda i, dp: (i, 0))
    big = jax.ShapeDtypeStruct((rows, width), jnp.bfloat16)
    small = jax.ShapeDtypeStruct((rows, 1), jnp.bfloat16)
    return pl.pallas_call(
        lambda dp, *refs: adam_kernel(2, *refs),
        grid_spec=pltpu.PrefetchScalarGridSpec(
            num_scalar_prefetch=1,
            grid=(rows // block,),
            in_specs=[held, wide, held, wide, wide, thin, thin, wide],
            out_specs=(wide, wide, wide, thin, thin),
        ),
        out_shape=(big, big, big, small, small),
        name="adam_rows",
        cost_estimate=pl.CostEstimate(
            flops=30 * rows * width, bytes_accessed=16 * rows * width, transcendentals=2 * rows * width
        ),
    )(my_dp, part, other, full, m_code, v_code, m_scale, v_scale, noise)


def plan_kernel(line, inner, steps, dest_ref, dest_col_ref, moves_ref, last_ref, used_ref):
    count = line * inner
    lanes = dest_ref.shape[1]
    shape = (2 * line, lanes)
    lane = lax.broadcasted_iota(jnp.int32, shape, 1)
    row = lax.broadcasted_iota(jnp.int32, shape, 0)
    node, down = row // 2, row % 2
    dest = jnp.broadcast_to(dest_ref[...], shape)
    goal = dest // inner
    here = jnp.where(lane < count, lane // inner, -1)
    slot = lane % inner
    used = jnp.zeros((8, lanes), jnp.int32)
    far = jnp.abs(goal - node)
    wants = (goal - node) * (1 - 2 * down) > 0
    for step in range(steps):
        score = jnp.where((here == node) & wants, far * lanes + (lanes - 1 - lane), -1)
        best = jnp.max(score, axis=1, keepdims=True)
        chosen = (score == best) & (score >= 0)
        sent = jnp.max(jnp.where(chosen, slot, 0), axis=1, keepdims=True)
        moves_ref[step] = jnp.broadcast_to(sent, shape)
        move = jnp.sum(jnp.where(chosen, 1 - 2 * down, 0), axis=0, keepdims=True)
        move = jnp.broadcast_to(move, shape)
        here = here + move
        moved = move * move
        slot = slot * (1 - moved) + moved * (inner + 2 * step) + (moved - move) // 2
        any_sent = jnp.minimum(jnp.max(best, axis=0, keepdims=True) + 1, 1)
        used = jnp.maximum(used, jnp.broadcast_to(any_sent, used.shape) * (step + 1))
    used_ref[...] = used
    wanted = lax.broadcasted_iota(jnp.int32, (count, lanes), 0)
    slots = jnp.broadcast_to(slot[0:1, :], (count, lanes))
    hits = jnp.where(jnp.broadcast_to(dest_ref[...], (count, lanes)) == wanted, slots, 0)
    last_ref[...] = jnp.broadcast_to(jnp.sum(hits, axis=1, keepdims=True), (count, lanes))


def plan(dest, line, inner, steps):
    count, lanes = line * inner, 128
    wide = jnp.full((1, lanes), -1, jnp.int32)
    wide = lax.dynamic_update_slice(wide, dest[None, :], (0, 0))
    moves, last, used = pl.pallas_call(
        functools.partial(plan_kernel, line, inner, steps),
        out_shape=(
            jax.ShapeDtypeStruct((steps, 2 * line, lanes), jnp.int32),
            jax.ShapeDtypeStruct((count, lanes), jnp.int32),
            jax.ShapeDtypeStruct((8, lanes), jnp.int32),
        ),
        name="plan",
    )(wide, dest[:, None])
    table = jnp.concatenate([last[:, 0], moves[:, :, 0].reshape(-1)])
    return table, used[0, 0]


def move_kernel(line, inner, steps, sets, table, tok_in, cot_in, small_in, *refs):
    arrays = 3
    chunks = arrays * HALVES
    own = (tok_in, cot_in, small_in)
    sources = refs[:arrays]
    moved = refs[arrays : 2 * arrays]
    packed = refs[2 * arrays : 2 * arrays + 2]
    all_small = refs[2 * arrays + 2]
    rest = list(refs[2 * arrays + 3 :])
    slots = rest[:chunks]
    held = rest[chunks : chunks + 3]
    (packs, b_buf, c_buf, a_send, a_recv, a_local, b_send, b_recv, credit, c_send, c_recv, c_local,
     z_send, z_recv, p_send, p_recv, p_local, x_send, x_recv, x_local, o_local, d_send, d_recv) = rest[chunks + 3 :]
    me = lax.axis_index("expert")
    my_dp = lax.axis_index("dp")
    z, p = me // inner, me % inner
    x, y = p % 2, p // 2
    mates = (y * 2 + (1 - x), (1 - y) * 2 + x, (1 - y) * 2 + (1 - x))
    experts = line * inner
    rows = slots[0].shape[1]
    piece = sources[0].shape[1]
    rows_dp = moved[1].shape[1]
    cap, width = packed[0].shape[1:]
    above, below = z < line - 1, z > 0

    def at(place):
        return {"expert": place}

    def remote(src, dst, send, recv, place):
        return pltpu.make_async_remote_copy(
            src_ref=src, dst_ref=dst, send_sem=send, recv_sem=recv,
            device_id=at(place), device_id_type=MESH,
        )

    barrier = pltpu.get_barrier_semaphore()
    for mate in mates:
        pl.semaphore_signal(barrier, inc=1, device_id=at(z * inner + mate), device_id_type=MESH)
    pl.semaphore_signal(barrier, inc=1, device_id={"dp": 1 - my_dp}, device_id_type=MESH)

    @pl.when(above)
    def _():
        pl.semaphore_signal(barrier, inc=1, device_id=at(me + inner), device_id_type=MESH)

    @pl.when(below)
    def _():
        pl.semaphore_signal(barrier, inc=1, device_id=at(me - inner), device_id_type=MESH)

    middle = above & below

    @pl.when(middle)
    def _():
        pl.semaphore_wait(barrier, len(mates) + 3)

    @pl.when(jnp.logical_not(middle))
    def _():
        pl.semaphore_wait(barrier, len(mates) + 2)

    def line_copy(array, hop, down):
        if down:
            plane, place = z + hop, me - inner
        else:
            plane, place = z - hop, me + inner
        src = own[array] if hop == 0 else held[array].at[plane]
        return remote(src, held[array].at[plane], z_send.at[array, down, hop], z_recv.at[array, down, hop], place)

    def line_has(hop, down):
        return (below & (z + hop < line)) if down else (above & (z - hop >= 0))

    def line_send(hop):
        for down in range(2):
            @pl.when(line_has(hop, down))
            def _():
                for array in range(3):
                    line_copy(array, hop, down).start()

    def line_drain(hop):
        for down in range(2):
            @pl.when(line_has(hop, down))
            def _():
                for array in range(3):
                    line_copy(array, hop, down).wait_send()

    def line_came(hop, down):
        return (z + hop + 1 < line) if down else (z - hop - 1 >= 0)

    def line_recv(hop):
        for down in range(2):
            @pl.when(line_came(hop, down))
            def _():
                plane = z + hop + 1 if down else z - hop - 1
                for array in range(3):
                    dst = held[array].at[plane]
                    remote(dst, dst, z_send.at[array, down, hop], z_recv.at[array, down, hop], me).wait_recv()

    def by_hop(hop, action):
        for down in range(2):
            @pl.when(line_came(hop, down))
            def _():
                action(z + hop + 1 if down else z - hop - 1)

    def table_copy(plane, k):
        return remote(held[2].at[plane], all_small.at[plane * inner + p],
                      p_send.at[plane, k], p_recv.at[plane, k], z * inner + mates[k])

    def table_local(plane):
        return pltpu.make_async_copy(held[2].at[plane], all_small.at[plane * inner + p], p_local.at[plane])

    def pack(plane, one):
        small = held[2].at[plane]

        def for_place(place, carry):
            expert = table[experts + 2 * line * steps_most(inner) + z * inner + place]
            chosen = lax.broadcasted_iota(jnp.int32, (experts, small.shape[1]), 0) == expert
            gate = jnp.sum(jnp.where(chosen, small[0:experts, :], 0.0), axis=0, keepdims=True)
            rank = jnp.sum(jnp.where(chosen, small[experts : 2 * experts, :], 0.0), axis=0, keepdims=True)
            count = lax.broadcasted_iota(jnp.int32, (cap, small.shape[1]), 0).astype(jnp.float32)
            hot = jnp.where(count == rank, 1.0, 0.0)
            gates = jnp.sum(hot * gate, axis=1, keepdims=True)
            hot = hot.astype(jnp.bfloat16)

            def for_columns(i, carry):
                part = pl.ds(pl.multiple_of(i * COLUMNS, COLUMNS), COLUMNS)
                packs[0, one, place, :, part] = jnp.dot(
                    hot, held[0][plane, :, part], preferred_element_type=jnp.float32
                ).astype(jnp.bfloat16)
                packs[1, one, place, :, part] = (gates * jnp.dot(
                    hot, held[1][plane, :, part], preferred_element_type=jnp.float32
                )).astype(jnp.bfloat16)
                return carry

            return lax.fori_loop(0, width // COLUMNS, for_columns, carry)

        lax.fori_loop(0, inner, for_place, 0)

    def pack_copy(array, plane, one, k):
        return remote(packs.at[array, one, mates[k]], packed[array].at[plane * inner + p],
                      x_send.at[array, plane, k], x_recv.at[array, plane, k], z * inner + mates[k])

    def pack_local(array, plane, one):
        return pltpu.make_async_copy(packs.at[array, one, p], packed[array].at[plane * inner + p], x_local.at[array, plane])

    def pack_start(plane, one):
        pack(plane, one)
        for array in range(2):
            for k in range(3):
                pack_copy(array, plane, one, k).start()
            pack_local(array, plane, one).start()
        for k in range(3):
            table_copy(plane, k).start()
        table_local(plane).start()

    def pack_drain(plane, one):
        for array in range(2):
            for k in range(3):
                pack_copy(array, plane, one, k).wait_send()
            pack_local(array, plane, one).wait()

    def pack_recv(plane):
        for k in range(3):
            for array in range(2):
                dst = packed[array].at[plane * inner + mates[k]]
                remote(dst, dst, x_send.at[array, plane, k], x_recv.at[array, plane, k], me).wait_recv()
            dst = all_small.at[plane * inner + mates[k]]
            remote(dst, dst, p_send.at[plane, k], p_recv.at[plane, k], me).wait_recv()
            table_copy(plane, k).wait_send()
        table_local(plane).wait()

    def source_piece(chunk, place):
        return sources[chunk // HALVES].at[place, pl.ds(chunk % HALVES * rows, rows)]

    def moved_piece(chunk, place):
        flat = place * piece + chunk % HALVES * rows
        offset = flat % rows_dp
        if chunk < HALVES:
            offset = offset + my_dp * rows_dp
        return moved[chunk // HALVES].at[flat // rows_dp, pl.ds(pl.multiple_of(offset, rows), rows)]

    def spread_copy(chunk, k):
        return remote(source_piece(chunk, mates[k]), slots[chunk].at[p],
                      a_send.at[chunk, k], a_recv.at[chunk, k], z * inner + mates[k])

    def spread_local(chunk):
        return pltpu.make_async_copy(source_piece(chunk, p), slots[chunk].at[p], a_local.at[chunk])

    def spread_start(chunk):
        for k in range(3):
            spread_copy(chunk, k).start()
        spread_local(chunk).start()

    def spread_wait(chunk):
        for k in range(3):
            dst = slots[chunk].at[mates[k]]
            remote(dst, dst, a_send.at[chunk, k], a_recv.at[chunk, k], me).wait_recv()
        spread_local(chunk).wait()

    def line_step_copy(chunk, step, down):
        place = me - inner if down else me + inner
        return remote(b_buf.at[chunk % 2, down], slots[chunk].at[inner + 2 * step + down],
                      b_send.at[chunk % 2, down], b_recv.at[chunk, down], place)

    def step_recv(chunk, step):
        for down in range(2):
            @pl.when(above if down else below)
            def _():
                dst = slots[chunk].at[inner + 2 * step + down]
                remote(dst, dst, b_send.at[chunk % 2, down], b_recv.at[chunk, down], me).wait_recv()

    def pick(chunk, index, dst):
        def body(i, carry):
            part = pl.ds(i * ROWS_AT_ONCE, ROWS_AT_ONCE)
            dst[part, :] = slots[chunk][index, part, :]
            return carry

        lax.fori_loop(0, rows // ROWS_AT_ONCE, body, 0)

    def step_drain(chunk, step):
        for down in range(2):
            @pl.when(below if down else above)
            def _():
                line_step_copy(chunk, step, down).wait_send()

    def step_send(chunk, step, before):
        if before is not None:
            step_drain(*before)
        for down in range(2):
            @pl.when(below if down else above)
            def _():
                index = table[experts + step * 2 * line + z * 2 + down]
                pick(chunk, index, b_buf.at[chunk % 2, down])
        for down in range(2):
            @pl.when(below if down else above)
            def _():
                pl.semaphore_signal(credit.at[chunk, 1 - down], inc=1,
                                    device_id=at(me - inner if down else me + inner), device_id_type=MESH)
        for down in range(2):
            @pl.when(below if down else above)
            def _():
                pl.semaphore_wait(credit.at[chunk, down], 1)
                line_step_copy(chunk, step, down).start()

    def collect_copy(chunk, k):
        return remote(c_buf.at[chunk % 2, k], moved_piece(chunk, p),
                      c_send.at[chunk, k], c_recv.at[chunk, k], z * inner + mates[k])

    def collect_local(chunk):
        return pltpu.make_async_copy(c_buf.at[chunk % 2, 3], moved_piece(chunk, p), c_local.at[chunk])

    def collect_drain(chunk):
        for k in range(3):
            collect_copy(chunk, k).wait_send()
        collect_local(chunk).wait()

    def collect_send(chunk):
        step_recv(chunk, steps - 1)
        if chunk >= 2:
            collect_drain(chunk - 2)
        for k in range(4):
            place = mates[k] if k < 3 else p
            pick(chunk, table[z * inner + place], c_buf.at[chunk % 2, k])
            if k < 3:
                collect_copy(chunk, k).start()
        collect_local(chunk).start()

    def collect_wait(chunk):
        for k in range(3):
            dst = moved_piece(chunk, mates[k])
            remote(dst, dst, c_send.at[chunk, k], c_recv.at[chunk, k], me).wait_recv()

    def share_copy(chunk, place):
        part = moved_piece(chunk, place)
        return pltpu.make_async_remote_copy(
            src_ref=part, dst_ref=part, send_sem=d_send.at[chunk, place], recv_sem=d_recv.at[chunk, place],
            device_id={"dp": 1 - my_dp}, device_id_type=MESH,
        )

    def share_got(chunk, place):
        flat = place * piece + chunk % HALVES * rows
        offset = pl.multiple_of(flat % rows_dp + (1 - my_dp) * rows_dp, rows)
        part = moved[0].at[flat // rows_dp, pl.ds(offset, rows)]
        return pltpu.make_async_remote_copy(
            src_ref=part, dst_ref=part, send_sem=d_send.at[chunk, place], recv_sem=d_recv.at[chunk, place],
            device_id={"dp": 1 - my_dp}, device_id_type=MESH,
        )

    own_copies = [pltpu.make_async_copy(own[a], held[a].at[z], o_local.at[a]) for a in range(3)]
    for copy in own_copies:
        copy.start()
    for chunk in range(2):
        spread_start(chunk)
    line_send(0)
    for chunk in range(2, 4):
        spread_start(chunk)
    for copy in own_copies:
        copy.wait()
    early = sets == line
    if early:
        pack_start(z, z)
    for chunk in range(4, chunks):
        spread_start(chunk)

    total = chunks * steps
    hooks = {}
    for hop in range(line - 1):
        todo = hooks.setdefault(1 + 2 * hop, [])
        todo.append(functools.partial(line_recv, hop))
        if hop + 1 < line - 1:
            todo.append(functools.partial(line_send, hop + 1))
        if early:
            todo.append(functools.partial(by_hop, hop, lambda plane: pack_start(plane, plane)))

    previous = {}
    number = 0
    for pair in range(chunks // 2):
        for step in range(steps):
            for chunk in (2 * pair, 2 * pair + 1):
                if step == 0:
                    spread_wait(chunk)
                else:
                    step_recv(chunk, step - 1)
                step_send(chunk, step, previous.get(chunk % 2))
                previous[chunk % 2] = (chunk, step)
                if step == 0 and pair > 0:
                    collect_send(chunk - 2)
                for hook in hooks.get(number, []):
                    hook()
                number += 1
    for chunk in range(HALVES):
        collect_wait(chunk)
        for place in range(inner):
            share_copy(chunk, place).start()
    for chunk in (chunks - 2, chunks - 1):
        collect_send(chunk)
    if not early:
        for plane in range(line):
            if plane >= sets:
                pack_drain(plane - sets, (plane - sets) % sets)
            pack_start(plane, plane % sets)

    for chunk in (chunks - 2, chunks - 1):
        step_drain(*previous[chunk % 2])
        collect_drain(chunk)
    for chunk in range(chunks):
        for k in range(3):
            spread_copy(chunk, k).wait_send()
        if chunk >= HALVES:
            collect_wait(chunk)
    for hop in range(line - 1):
        line_drain(hop)
    for plane in range(line):
        pack_recv(plane)
        if early or plane >= line - sets:
            pack_drain(plane, plane % sets)
    for chunk in range(HALVES):
        for place in range(inner):
            share_copy(chunk, place).wait_send()
            share_got(chunk, place).wait_recv()


def steps_most(inner):
    return 2 * inner


def move(line, inner, steps, number, cap, table, tokens, cotangent, small, arrays):
    count = line * inner
    places, wide_rows, width = arrays[0].shape
    rows = wide_rows // HALVES
    rows_dp = places * wide_rows // 2
    chunks = len(arrays) * HALVES
    sets = line if steps <= inner + 2 else 1
    dma, regular = pltpu.SemaphoreType.DMA, pltpu.SemaphoreType.REGULAR
    gathers = (tokens, cotangent, small)
    vmem = pl.BlockSpec(memory_space=pltpu.VMEM)
    anywhere = pl.BlockSpec(memory_space=ANY)
    packed = jax.ShapeDtypeStruct((count, cap, tokens.shape[1]), tokens.dtype)
    return pl.pallas_call(
        functools.partial(move_kernel, line, inner, steps, sets),
        out_shape=(
            jax.ShapeDtypeStruct((2, 2 * rows_dp, width), jnp.bfloat16),
            jax.ShapeDtypeStruct((2, rows_dp, width), jnp.bfloat16),
            jax.ShapeDtypeStruct((2, rows_dp, width), jnp.bfloat16),
            packed,
            packed,
            jax.ShapeDtypeStruct((count,) + small.shape, small.dtype),
        ),
        in_specs=[pl.BlockSpec(memory_space=pltpu.SMEM)] + [vmem] * 3 + [anywhere] * len(arrays),
        out_specs=tuple([anywhere] * (len(arrays) + 3)),
        scratch_shapes=[pltpu.VMEM((inner + 2 * steps, rows, width), jnp.bfloat16) for _ in range(chunks)]
        + [pltpu.VMEM((line,) + g.shape, g.dtype) for g in gathers]
        + [
            pltpu.VMEM((2, sets, inner, cap, tokens.shape[1]), jnp.bfloat16),
            pltpu.VMEM((2, 2, rows, width), jnp.bfloat16),
            pltpu.VMEM((2, 4, rows, width), jnp.bfloat16),
            dma((chunks, 3)), dma((chunks, 3)), dma((chunks,)),
            dma((2, 2)), dma((chunks, 2)), regular((chunks, 2)),
            dma((chunks, 3)), dma((chunks, 3)), dma((chunks,)),
            dma((3, 2, line - 1)), dma((3, 2, line - 1)),
            dma((line, 3)), dma((line, 3)), dma((line,)),
            dma((2, line, 3)), dma((2, line, 3)), dma((2, line)),
            dma((3,)),
            dma((HALVES, inner)), dma((HALVES, inner)),
        ],
        compiler_params=pltpu.CompilerParams(
            collective_id=number, has_side_effects=True, vmem_limit_bytes=61 * 1024 * 1024
        ),
        name="move%d" % steps,
    )(table, tokens, cotangent, small, *arrays)


def planes_on_device(
    tokens, routes, gates, cotangent, owner_before, owner_after,
    weights, m_codes, v_codes, m_scales, v_scales, noise, inner,
):
    expert_count = lax.axis_size("expert")
    dp_count = lax.axis_size("dp")
    me = lax.axis_index("expert")
    my_dp = lax.axis_index("dp")
    line = expert_count // inner
    most = steps_most(inner)
    slot_ids = jnp.arange(expert_count, dtype=jnp.int32)
    from_slot = (owner_before[None, :] == slot_ids[:, None]).astype(jnp.int32)
    dest = jnp.sum(from_slot * owner_after[None, :], axis=1)
    at_slot = (owner_after[None, :] == slot_ids[:, None]).astype(jnp.int32)
    holder = jnp.sum(at_slot * slot_ids[None, :], axis=1)
    my_source = jnp.sum((owner_after == me).astype(jnp.int32) * owner_before)
    rows_dp = weights.shape[2]
    hidden_units = weights.shape[3]
    model_width = tokens.shape[1]
    token_count = tokens.shape[0]
    cap = token_count * routes.shape[1] * 9 // (8 * expert_count)

    matches = routes[:, :, None] == slot_ids[None, None, :]
    dense_gates = jnp.sum(jnp.where(matches, gates[:, :, None], 0.0), axis=1).T
    named = jnp.sum(matches.astype(jnp.float32), axis=1).T
    order = jnp.arange(token_count, dtype=jnp.int32)
    earlier = (order[:, None] < order[None, :]).astype(jnp.float32)
    rank = jnp.where(named > 0, jnp.dot(named, earlier), -1.0)
    scales = jnp.concatenate([m_scales.reshape(-1), v_scales.reshape(-1)]).astype(jnp.float32)
    small = jnp.concatenate([dense_gates, rank, scales.reshape(-1, token_count)])

    table, used = plan(dest, line, inner, most)
    table = jnp.concatenate([table, holder])
    arrays = tuple(a.reshape(inner, 2 * rows_dp // inner, hidden_units) for a in (weights, m_codes, v_codes))
    sizes = [inner, inner + 1, most]
    branch = sum([(used > s).astype(jnp.int32) for s in sizes[:-1]])
    full_weights, moved_m, moved_v, all_tokens, gated, all_small = lax.optimization_barrier(
        lax.switch(
            branch,
            [functools.partial(move, line, inner, s, i, cap) for i, s in enumerate(sizes)],
            table, tokens, cotangent, small, arrays,
        )
    )
    all_tokens = all_tokens.reshape(-1, model_width)
    gated = gated.reshape(-1, model_width)
    old_scales = lax.dynamic_index_in_dim(all_small, my_source, axis=0, keepdims=False)[2 * expert_count :]
    old_scales = old_scales.reshape(2, 2 * rows_dp)

    scale_model = model_width ** (-0.5)
    scale_hidden = hidden_units ** (-0.5)
    pre = jnp.dot(all_tokens, full_weights[0], preferred_element_type=jnp.float32) * scale_model
    back = jnp.dot(gated, full_weights[1], preferred_element_type=jnp.float32) * scale_hidden
    sigmoid_pre = jax.nn.sigmoid(pre)
    hidden = (pre * sigmoid_pre).astype(jnp.bfloat16)
    pre_grad = (back * sigmoid_pre * (1.0 + pre * (1.0 - sigmoid_pre))).astype(jnp.bfloat16)
    up_part = (transposed_dot(all_tokens, pre_grad) * scale_model).astype(jnp.bfloat16)
    down_part = (transposed_dot(gated, hidden) * scale_hidden).astype(jnp.bfloat16)
    part = jnp.stack([up_part, down_part])
    theirs = lax.dynamic_slice(part, (0, (1 - my_dp) * rows_dp, 0), (2, rows_dp, hidden_units))
    other = lax.ppermute(theirs, "dp", [(i, (i + 1) % dp_count) for i in range(dp_count)])
    flat = (2 * rows_dp, hidden_units)
    new_w, new_m, new_v, new_ms, new_vs = adam_rows(
        my_dp[None].astype(jnp.int32),
        part.reshape(-1, hidden_units),
        other.reshape(flat),
        full_weights.reshape(-1, hidden_units),
        moved_m.reshape(flat),
        moved_v.reshape(flat),
        old_scales[0][:, None],
        old_scales[1][:, None],
        noise.reshape(flat),
    )
    return (
        new_w.reshape(2, 1, rows_dp, hidden_units),
        new_m.reshape(2, 1, rows_dp, hidden_units),
        new_v.reshape(2, 1, rows_dp, hidden_units),
        new_ms.reshape(2, 1, rows_dp),
        new_vs.reshape(2, 1, rows_dp),
    )


def on_device(
    tokens,
    routes,
    gates,
    cotangent,
    owner_before,
    owner_after,
    weights,
    m_codes,
    v_codes,
    m_scales,
    v_scales,
    noise,
):
    expert_count = lax.axis_size("expert")
    me = lax.axis_index("expert")
    slot_ids = jnp.arange(expert_count, dtype=jnp.int32)
    matches = (owner_after[None, :] == slot_ids[:, None]).astype(jnp.int32)
    source_slot = jnp.sum(matches * owner_before[None, :], axis=1)
    my_match = (owner_after == me).astype(jnp.int32)
    my_expert = jnp.sum(my_match * slot_ids)
    my_source = jnp.sum(my_match * owner_before)
    rows_dp = weights.shape[2]
    hidden_units = weights.shape[3]
    model_width = tokens.shape[1]
    token_count = tokens.shape[0]
    piece = 2 * rows_dp // expert_count

    dp_count = lax.axis_size("dp")
    my_dp = lax.axis_index("dp")

    def spread(array):
        shaped = array.reshape(expert_count, piece, hidden_units)
        return lax.all_to_all(shaped, "expert", split_axis=0, concat_axis=0, tiled=True)

    def collect(array):
        return lax.all_to_all(array, "expert", split_axis=0, concat_axis=0, tiled=True)

    def regroup(array):
        return array.at[source_slot].get(mode="promise_in_bounds")

    def shift(array, step):
        ring = [(i, (i + step) % dp_count) for i in range(dp_count)]
        return lax.ppermute(array, "dp", ring)

    dense_gates = jnp.sum(
        jnp.where(routes[:, :, None] == slot_ids[None, None, :], gates[:, :, None], 0.0), axis=1
    ).T
    scales = jnp.concatenate([m_scales.reshape(-1), v_scales.reshape(-1)]).astype(jnp.float32)
    small = jnp.concatenate([dense_gates, scales.reshape(-1, token_count)])
    all_small = lax.all_gather(small, "expert", axis=0, tiled=False)
    inner = 1
    while inner * inner * 4 <= expert_count and expert_count % (inner * 2) == 0:
        inner *= 2
    outer = expert_count // inner
    lines = [[i + inner * k for k in range(outer)] for i in range(inner)]
    planes = [[inner * k + i for i in range(inner)] for k in range(outer)]

    def gather_line(array):
        return lax.all_gather(array, "expert", axis=0, tiled=True, axis_index_groups=lines)

    def gather_plane(array):
        return lax.all_gather(array, "expert", axis=0, tiled=True, axis_index_groups=planes)

    line_tokens, all_small = lax.optimization_barrier((gather_line(tokens), all_small))
    all_tokens = gather_plane(line_tokens)
    all_cotangent = gather_plane(gather_line(cotangent))

    weights_ready, all_small = lax.optimization_barrier((regroup(spread(weights)), all_small))
    gate = lax.dynamic_index_in_dim(all_small, my_expert, axis=1, keepdims=False)
    gate = gate.reshape(outer, inner, token_count).swapaxes(0, 1).reshape(-1)
    old_scales = lax.dynamic_index_in_dim(all_small, my_source, axis=0, keepdims=False)[expert_count:]
    old_scales = old_scales.reshape(2, 2 * rows_dp)
    moved_weights = collect(weights_ready)
    moved_weights, m_codes = lax.optimization_barrier((moved_weights, m_codes))
    m_spread = spread(m_codes)
    m_spread, v_codes = lax.optimization_barrier((m_spread, v_codes))
    v_spread = spread(v_codes)
    m_ready, v_spread = lax.optimization_barrier((regroup(m_spread), v_spread))
    moved_m = collect(m_ready)
    v_ready, moved_m = lax.optimization_barrier((regroup(v_spread), moved_m))
    moved_v = collect(v_ready)
    moved_m, all_cotangent = lax.optimization_barrier((moved_m, all_cotangent))

    own_rows = moved_weights.reshape(2, rows_dp, hidden_units)
    full_weights = jnp.zeros((2, dp_count * rows_dp, hidden_units), jnp.bfloat16)
    full_weights = lax.dynamic_update_slice(full_weights, own_rows, (0, my_dp * rows_dp, 0))
    for step in range(1, dp_count):
        start = (my_dp - step) % dp_count * rows_dp
        full_weights = lax.dynamic_update_slice(full_weights, shift(own_rows, step), (0, start, 0))
    gated = (gate[:, None] * all_cotangent.astype(jnp.float32)).astype(jnp.bfloat16)
    scale_model = model_width ** (-0.5)
    scale_hidden = hidden_units ** (-0.5)
    pre = jnp.dot(all_tokens, full_weights[0], preferred_element_type=jnp.float32) * scale_model
    back = jnp.dot(gated, full_weights[1], preferred_element_type=jnp.float32) * scale_hidden
    sigmoid_pre = jax.nn.sigmoid(pre)
    hidden = (pre * sigmoid_pre).astype(jnp.bfloat16)
    pre_grad = (back * sigmoid_pre * (1.0 + pre * (1.0 - sigmoid_pre))).astype(jnp.bfloat16)
    up_part = (transposed_dot(all_tokens, pre_grad) * scale_model).astype(jnp.bfloat16)
    down_part = (transposed_dot(gated, hidden) * scale_hidden).astype(jnp.bfloat16)
    part = jnp.stack([up_part, down_part])
    grads = []
    for step in range(dp_count):
        start = (my_dp + step) % dp_count * rows_dp
        mine = lax.dynamic_slice(part, (0, start, 0), (2, rows_dp, hidden_units))
        grads.append((shift(mine, step) if step else mine).reshape(2 * rows_dp, hidden_units))
    new_w, new_m, new_v, new_ms, new_vs = adam(
        grads,
        moved_weights.reshape(2 * rows_dp, hidden_units),
        moved_m.reshape(2 * rows_dp, hidden_units),
        moved_v.reshape(2 * rows_dp, hidden_units),
        old_scales[0][:, None],
        old_scales[1][:, None],
        noise.reshape(2 * rows_dp, hidden_units),
    )
    return (
        new_w.reshape(2, 1, rows_dp, hidden_units),
        new_m.reshape(2, 1, rows_dp, hidden_units),
        new_v.reshape(2, 1, rows_dp, hidden_units),
        new_ms.reshape(2, 1, rows_dp),
        new_vs.reshape(2, 1, rows_dp),
    )


def solution(mesh):
    placed = (
        P(("expert", "dp"), None),
        P(("expert", "dp"), None),
        P(("expert", "dp"), None),
        P(("expert", "dp"), None),
        P(),
        P(),
        P(None, "expert", "dp", None),
        P(None, "expert", "dp", None),
        P(None, "expert", "dp", None),
        P(None, "expert", "dp"),
        P(None, "expert", "dp"),
        P(None, "expert", "dp", None),
    )
    inner = 4
    line = mesh.shape["expert"] // inner
    in_planes = mesh.shape["dp"] == 2 and mesh.shape["expert"] == line * inner and 2 <= line <= 4
    program = functools.partial(planes_on_device, inner=inner) if in_planes else on_device
    return jax.shard_map(
        program,
        mesh=mesh,
        in_specs=placed,
        out_specs=(
            P(None, "expert", "dp", None),
            P(None, "expert", "dp", None),
            P(None, "expert", "dp", None),
            P(None, "expert", "dp"),
            P(None, "expert", "dp"),
        ),
        check_vma=False,
    )
```

```python
import functools

import jax
import jax.numpy as jnp
from jax import lax
from jax.experimental import pallas as pl
from jax.experimental.pallas import tpu as pltpu
from jax.sharding import PartitionSpec as P

LEVELS = 7


learn_rate = 0.1
beta_one = 0.9
beta_two = 0.95
adam_step = 20.0
adam_epsilon = 1e-08
scale_epsilon = 1e-06

MESH = pl.DeviceIdType.MESH
ANY = pl.ANY
HALVES = 2
ROWS_AT_ONCE = 32
COLUMNS = 512


def transposed_dot(left, right):
    return lax.dot_general(
        left, right, (((0,), (0,)), ((), ())), preferred_element_type=jnp.float32
    )


def adam_kernel(parts, *refs):
    weight, m_code, v_code, m_scale, v_scale, noise, new_w, new_m, new_v, new_ms, new_vs = refs[parts:]
    grads = refs[0][...].astype(jnp.float32)
    for part in refs[1:parts]:
        grads += part[...].astype(jnp.float32)
    m_old = m_code[...].astype(jnp.float32) * (m_scale[...].astype(jnp.float32) / LEVELS)
    v_old = v_code[...].astype(jnp.float32) * (v_scale[...].astype(jnp.float32) / LEVELS)
    m_new = beta_one * m_old + (1.0 - beta_one) * grads
    v_new = beta_two * v_old + (1.0 - beta_two) * grads * grads
    direction = (
        m_new
        * (1.0 / (1.0 - beta_one**adam_step))
        / (jnp.sqrt(v_new * (1.0 / (1.0 - beta_two**adam_step))) + adam_epsilon)
    )
    new_w[...] = (weight[...].astype(jnp.float32) - learn_rate * direction).astype(jnp.bfloat16)
    m_top = (jnp.max(jnp.abs(m_new), axis=1, keepdims=True) + scale_epsilon).astype(jnp.bfloat16)
    v_top = (jnp.max(v_new, axis=1, keepdims=True) + scale_epsilon).astype(jnp.bfloat16)
    new_ms[...] = m_top
    new_vs[...] = v_top
    dither = noise[...].astype(jnp.float32)
    m_value = m_new * (LEVELS / m_top.astype(jnp.float32)) + (dither - 0.5)
    v_value = v_new * (LEVELS / v_top.astype(jnp.float32)) + dither
    new_m[...] = jnp.clip(m_value, -1.0 * LEVELS, 1.0 * LEVELS).astype(jnp.bfloat16)
    new_v[...] = jnp.clip(v_value, 0.0, 1.0 * LEVELS).astype(jnp.bfloat16)


def adam(grads, weight, m_code, v_code, m_scale, v_scale, noise):
    rows, width = weight.shape
    block = min(256, rows)
    wide = pl.BlockSpec((block, width), lambda i: (i, 0))
    thin = pl.BlockSpec((block, 1), lambda i: (i, 0))
    big = jax.ShapeDtypeStruct((rows, width), jnp.bfloat16)
    small = jax.ShapeDtypeStruct((rows, 1), jnp.bfloat16)
    return pl.pallas_call(
        functools.partial(adam_kernel, len(grads)),
        grid=(rows // block,),
        out_shape=(big, big, big, small, small),
        in_specs=[wide] * len(grads) + [wide, wide, wide, thin, thin, wide],
        out_specs=(wide, wide, wide, thin, thin),
        name="adam",
        cost_estimate=pl.CostEstimate(
            flops=30 * rows * width, bytes_accessed=16 * rows * width, transcendentals=2 * rows * width
        ),
    )(*grads, weight, m_code, v_code, m_scale, v_scale, noise)


def column(row):
    return jnp.transpose(jnp.broadcast_to(row, (128, row.shape[1])))[:, 0:1]


def adam_rows_kernel(per, dp, up, down, other_up, other_down, weight, m_code, v_code, scales, noise,
                     new_w, new_m, new_v, new_ms, new_vs):
    first = pl.program_id(0) < per
    grads = jnp.where(first, up[...], down[...]).astype(jnp.float32)
    grads += jnp.where(first, other_up[...], other_down[...]).astype(jnp.float32)
    m_scale, v_scale = column(scales[0, 0:1, :]), column(scales[0, 1:2, :])
    m_old = m_code[...].astype(jnp.float32) * (m_scale / LEVELS)
    v_old = v_code[...].astype(jnp.float32) * (v_scale / LEVELS)
    m_new = beta_one * m_old + (1.0 - beta_one) * grads
    v_new = beta_two * v_old + (1.0 - beta_two) * grads * grads
    direction = (
        m_new
        * (1.0 / (1.0 - beta_one**adam_step))
        / (jnp.sqrt(v_new * (1.0 / (1.0 - beta_two**adam_step))) + adam_epsilon)
    )
    new_w[...] = (weight[...].astype(jnp.float32) - learn_rate * direction).astype(jnp.bfloat16)
    m_top = (jnp.max(jnp.abs(m_new), axis=1, keepdims=True) + scale_epsilon).astype(jnp.bfloat16)
    v_top = (jnp.max(v_new, axis=1, keepdims=True) + scale_epsilon).astype(jnp.bfloat16)
    m_top, v_top = m_top.astype(jnp.float32), v_top.astype(jnp.float32)
    for top, out in ((m_top, new_ms), (v_top, new_vs)):
        lanes = jnp.transpose(jnp.broadcast_to(top, (top.shape[0], 128)))
        out[0] = lanes[0:1, :].astype(jnp.bfloat16)
    dither = noise[...].astype(jnp.float32)
    m_value = m_new * (LEVELS / m_top) + (dither - 0.5)
    v_value = v_new * (LEVELS / v_top) + dither
    new_m[...] = jnp.clip(m_value, -1.0 * LEVELS, 1.0 * LEVELS).astype(jnp.bfloat16)
    new_v[...] = jnp.clip(v_value, 0.0, 1.0 * LEVELS).astype(jnp.bfloat16)


def adam_rows(my_dp, up, down, other_up, other_down, full, m_code, v_code, scales, noise):
    rows, width = m_code.shape
    block = min(256, rows // 2)
    per = rows // 2 // block
    wide = pl.BlockSpec((block, width), lambda i, dp: (i, 0))
    held = pl.BlockSpec((block, width), lambda i, dp: (i // per * 2 * per + dp[0] * per + i % per, 0))
    ups = pl.BlockSpec((block, width), lambda i, dp: (dp[0] * per + jnp.minimum(i, per - 1), 0))
    downs = pl.BlockSpec((block, width), lambda i, dp: (dp[0] * per + jnp.maximum(i - per, 0), 0))
    other_ups = pl.BlockSpec((block, width), lambda i, dp: (jnp.minimum(i, per - 1), 0))
    other_downs = pl.BlockSpec((block, width), lambda i, dp: (jnp.maximum(i - per, 0), 0))
    thin = pl.BlockSpec((1, 2, block), lambda i, dp: (i, 0, 0))
    tops = pl.BlockSpec((1, 1, block), lambda i, dp: (i, 0, 0))
    big = jax.ShapeDtypeStruct((rows, width), jnp.bfloat16)
    small = jax.ShapeDtypeStruct((rows // block, 1, block), jnp.bfloat16)
    scales = scales.reshape(2, rows // block, block).swapaxes(0, 1)
    return pl.pallas_call(
        functools.partial(adam_rows_kernel, per),
        grid_spec=pltpu.PrefetchScalarGridSpec(
            num_scalar_prefetch=1,
            grid=(rows // block,),
            in_specs=[ups, downs, other_ups, other_downs, held, wide, wide, thin, wide],
            out_specs=(wide, wide, wide, tops, tops),
        ),
        out_shape=(big, big, big, small, small),
        name="adam_rows",
        cost_estimate=pl.CostEstimate(
            flops=30 * rows * width, bytes_accessed=16 * rows * width, transcendentals=2 * rows * width
        ),
    )(my_dp, up, down, other_up, other_down, full, m_code, v_code, scales, noise)


def plan_kernel(line, inner, steps, before, after, moves_ref, last_ref, used_ref):
    count = line * inner
    lanes = used_ref.shape[1]
    shape = (2 * line, lanes)
    lane = lax.broadcasted_iota(jnp.int32, shape, 1)
    row = lax.broadcasted_iota(jnp.int32, shape, 0)
    slot_row = lax.broadcasted_iota(jnp.int32, (count, lanes), 0)
    slot_lane = lax.broadcasted_iota(jnp.int32, (count, lanes), 1)
    dest = jnp.full(shape, -1, jnp.int32)
    wanted = jnp.full((count, lanes), -1, jnp.int32)
    holder = jnp.zeros((count, lanes), jnp.int32)
    for expert in range(count):
        dest = jnp.where(lane == before[expert], after[expert], dest)
        wanted = jnp.where(slot_lane == before[expert], after[expert], wanted)
        holder = jnp.where(slot_row == after[expert], expert, holder)
    node, down = row // 2, row % 2
    goal = dest // inner
    here = jnp.where(lane < count, lane // inner, -1)
    slot = lane % inner
    used = jnp.zeros((8, lanes), jnp.int32)
    far = jnp.abs(goal - node)
    wants = (goal - node) * (1 - 2 * down) > 0
    for step in range(steps):
        score = jnp.where((here == node) & wants, far * lanes + (lanes - 1 - lane), -1)
        best = jnp.max(score, axis=1, keepdims=True)
        chosen = (score == best) & (score >= 0)
        sent = jnp.max(jnp.where(chosen, slot, 0), axis=1, keepdims=True)
        moves_ref[step] = jnp.broadcast_to(sent, shape)
        move = jnp.sum(jnp.where(chosen, 1 - 2 * down, 0), axis=0, keepdims=True)
        move = jnp.broadcast_to(move, shape)
        here = here + move
        moved = move * move
        slot = slot * (1 - moved) + moved * (inner + 2 * step) + (moved - move) // 2
        any_sent = jnp.minimum(jnp.max(best, axis=0, keepdims=True) + 1, 1)
        used = jnp.maximum(used, jnp.broadcast_to(any_sent, used.shape) * (step + 1))
    used_ref[...] = used
    slots = jnp.broadcast_to(slot[0:1, :], (count, lanes))
    hits = jnp.where(wanted == slot_row, slots, 0)
    last_ref[0] = jnp.broadcast_to(jnp.sum(hits, axis=1, keepdims=True), (count, lanes))
    last_ref[1] = holder


def plan(before, after, line, inner, steps):
    count, lanes = line * inner, 128
    scalars = pl.BlockSpec(memory_space=pltpu.SMEM)
    moves, last, used = pl.pallas_call(
        functools.partial(plan_kernel, line, inner, steps),
        out_shape=(
            jax.ShapeDtypeStruct((steps, 2 * line, lanes), jnp.int32),
            jax.ShapeDtypeStruct((2, count, lanes), jnp.int32),
            jax.ShapeDtypeStruct((8, lanes), jnp.int32),
        ),
        in_specs=[scalars, scalars],
        name="plan",
    )(before, after)
    return moves, last, used[0, 0]


def move_kernel(line, inner, steps, sets, moves, last, tok_in, cot_in, small_in, *refs):
    arrays = 3
    chunks = arrays * HALVES
    own = (tok_in, cot_in, small_in)
    sources = refs[:arrays]
    moved = refs[arrays : 2 * arrays]
    packed = refs[2 * arrays : 2 * arrays + 2]
    all_small = refs[2 * arrays + 2]
    rest = list(refs[2 * arrays + 3 :])
    slots = rest[:chunks]
    held = rest[chunks : chunks + 3]
    (packs, b_buf, c_buf, a_send, a_recv, a_local, b_send, b_recv, credit, c_send, c_recv, c_local,
     z_send, z_recv, p_send, p_recv, p_local, x_send, x_recv, x_local, o_local, d_send, d_recv) = rest[chunks + 3 :]
    me = lax.axis_index("expert")
    my_dp = lax.axis_index("dp")
    z, p = me // inner, me % inner
    x, y = p % 2, p // 2
    mates = (y * 2 + (1 - x), (1 - y) * 2 + x, (1 - y) * 2 + (1 - x))
    experts = line * inner
    rows = slots[0].shape[1]
    piece = sources[0].shape[1]
    rows_dp = moved[1].shape[1]
    cap, width = packed[0].shape[1:]
    c_sets = c_buf.shape[0]
    above, below = z < line - 1, z > 0

    def at(place):
        return {"expert": place}

    def remote(src, dst, send, recv, place):
        return pltpu.make_async_remote_copy(
            src_ref=src, dst_ref=dst, send_sem=send, recv_sem=recv,
            device_id=at(place), device_id_type=MESH,
        )

    barrier = pltpu.get_barrier_semaphore()
    for mate in mates:
        pl.semaphore_signal(barrier, inc=1, device_id=at(z * inner + mate), device_id_type=MESH)
    pl.semaphore_signal(barrier, inc=1, device_id={"dp": 1 - my_dp}, device_id_type=MESH)

    @pl.when(above)
    def _():
        pl.semaphore_signal(barrier, inc=1, device_id=at(me + inner), device_id_type=MESH)

    @pl.when(below)
    def _():
        pl.semaphore_signal(barrier, inc=1, device_id=at(me - inner), device_id_type=MESH)

    middle = above & below

    @pl.when(middle)
    def _():
        pl.semaphore_wait(barrier, len(mates) + 3)

    @pl.when(jnp.logical_not(middle))
    def _():
        pl.semaphore_wait(barrier, len(mates) + 2)

    def line_copy(array, hop, down):
        if down:
            plane, place = z + hop, me - inner
        else:
            plane, place = z - hop, me + inner
        src = own[array] if hop == 0 else held[array].at[plane]
        return remote(src, held[array].at[plane], z_send.at[array, down, hop], z_recv.at[array, down, hop], place)

    def line_has(hop, down):
        return (below & (z + hop < line)) if down else (above & (z - hop >= 0))

    def line_send(hop):
        for down in range(2):
            @pl.when(line_has(hop, down))
            def _():
                for array in range(3):
                    line_copy(array, hop, down).start()

    def line_drain(hop):
        for down in range(2):
            @pl.when(line_has(hop, down))
            def _():
                for array in range(3):
                    line_copy(array, hop, down).wait_send()

    def line_came(hop, down):
        return (z + hop + 1 < line) if down else (z - hop - 1 >= 0)

    def line_recv(hop):
        for down in range(2):
            @pl.when(line_came(hop, down))
            def _():
                plane = z + hop + 1 if down else z - hop - 1
                for array in range(3):
                    dst = held[array].at[plane]
                    remote(dst, dst, z_send.at[array, down, hop], z_recv.at[array, down, hop], me).wait_recv()

    def by_hop(hop, action):
        for down in range(2):
            @pl.when(line_came(hop, down))
            def _():
                action(z + hop + 1 if down else z - hop - 1)

    def table_copy(plane, k):
        return remote(held[2].at[plane], all_small.at[plane * inner + p],
                      p_send.at[plane, k], p_recv.at[plane, k], z * inner + mates[k])

    def table_local(plane):
        return pltpu.make_async_copy(held[2].at[plane], all_small.at[plane * inner + p], p_local.at[plane])

    def pack(plane, one):
        small = held[2].at[plane]

        def for_place(place, carry):
            expert = last[1, z * inner + place, 0]
            chosen = lax.broadcasted_iota(jnp.int32, (experts, small.shape[1]), 0) == expert
            gate = jnp.sum(jnp.where(chosen, small[0:experts, :], 0.0), axis=0, keepdims=True)
            rank = jnp.sum(jnp.where(chosen, small[experts : 2 * experts, :], 0.0), axis=0, keepdims=True)
            count = lax.broadcasted_iota(jnp.int32, (cap, small.shape[1]), 0).astype(jnp.float32)
            hot = jnp.where(count == rank, 1.0, 0.0)
            gates = jnp.sum(hot * gate, axis=1, keepdims=True)
            hot = hot.astype(jnp.bfloat16)

            def for_columns(i, carry):
                part = pl.ds(pl.multiple_of(i * COLUMNS, COLUMNS), COLUMNS)
                packs[0, one, place, :, part] = jnp.dot(
                    hot, held[0][plane, :, part], preferred_element_type=jnp.float32
                ).astype(jnp.bfloat16)
                packs[1, one, place, :, part] = (gates * jnp.dot(
                    hot, held[1][plane, :, part], preferred_element_type=jnp.float32
                )).astype(jnp.bfloat16)
                return carry

            return lax.fori_loop(0, width // COLUMNS, for_columns, carry)

        lax.fori_loop(0, inner, for_place, 0)

    def pack_copy(array, plane, one, k):
        return remote(packs.at[array, one, mates[k]], packed[array].at[plane * inner + p],
                      x_send.at[array, plane, k], x_recv.at[array, plane, k], z * inner + mates[k])

    def pack_local(array, plane, one):
        return pltpu.make_async_copy(packs.at[array, one, p], packed[array].at[plane * inner + p], x_local.at[array, plane])

    def pack_start(plane, one):
        pack(plane, one)
        for array in range(2):
            for k in range(3):
                pack_copy(array, plane, one, k).start()
            pack_local(array, plane, one).start()
        for k in range(3):
            table_copy(plane, k).start()
        table_local(plane).start()

    def pack_drain(plane, one):
        for array in range(2):
            for k in range(3):
                pack_copy(array, plane, one, k).wait_send()
            pack_local(array, plane, one).wait()

    def pack_recv(plane):
        for k in range(3):
            for array in range(2):
                dst = packed[array].at[plane * inner + mates[k]]
                remote(dst, dst, x_send.at[array, plane, k], x_recv.at[array, plane, k], me).wait_recv()
            dst = all_small.at[plane * inner + mates[k]]
            remote(dst, dst, p_send.at[plane, k], p_recv.at[plane, k], me).wait_recv()
            table_copy(plane, k).wait_send()
        table_local(plane).wait()

    def source_piece(chunk, place):
        return sources[chunk // HALVES].at[place, pl.ds(chunk % HALVES * rows, rows)]

    def moved_piece(chunk, place):
        flat = place * piece + chunk % HALVES * rows
        offset = flat % rows_dp
        if chunk < HALVES:
            offset = offset + my_dp * rows_dp
        return moved[chunk // HALVES].at[flat // rows_dp, pl.ds(pl.multiple_of(offset, rows), rows)]

    def spread_copy(chunk, k):
        return remote(source_piece(chunk, mates[k]), slots[chunk].at[p],
                      a_send.at[chunk, k], a_recv.at[chunk, k], z * inner + mates[k])

    def spread_local(chunk):
        return pltpu.make_async_copy(source_piece(chunk, p), slots[chunk].at[p], a_local.at[chunk])

    def spread_start(chunk):
        for k in range(3):
            spread_copy(chunk, k).start()
        spread_local(chunk).start()

    def spread_wait(chunk):
        for k in range(3):
            dst = slots[chunk].at[mates[k]]
            remote(dst, dst, a_send.at[chunk, k], a_recv.at[chunk, k], me).wait_recv()
        spread_local(chunk).wait()

    def line_step_copy(chunk, step, down):
        place = me - inner if down else me + inner
        return remote(b_buf.at[chunk % 2, down], slots[chunk].at[inner + 2 * step + down],
                      b_send.at[chunk % 2, down], b_recv.at[chunk, down], place)

    def step_recv(chunk, step):
        for down in range(2):
            @pl.when(above if down else below)
            def _():
                dst = slots[chunk].at[inner + 2 * step + down]
                remote(dst, dst, b_send.at[chunk % 2, down], b_recv.at[chunk, down], me).wait_recv()

    def pick(chunk, index, dst):
        def body(i, carry):
            part = pl.ds(i * ROWS_AT_ONCE, ROWS_AT_ONCE)
            dst[part, :] = slots[chunk][index, part, :]
            return carry

        lax.fori_loop(0, rows // ROWS_AT_ONCE, body, 0)

    def step_drain(chunk, step):
        for down in range(2):
            @pl.when(below if down else above)
            def _():
                line_step_copy(chunk, step, down).wait_send()

    def step_send(chunk, step, before):
        if before is not None:
            step_drain(*before)
        for down in range(2):
            @pl.when(below if down else above)
            def _():
                index = moves[step, z * 2 + down, 0]
                pick(chunk, index, b_buf.at[chunk % 2, down])
        for down in range(2):
            @pl.when(below if down else above)
            def _():
                pl.semaphore_signal(credit.at[chunk, 1 - down], inc=1,
                                    device_id=at(me - inner if down else me + inner), device_id_type=MESH)
        for down in range(2):
            @pl.when(below if down else above)
            def _():
                pl.semaphore_wait(credit.at[chunk, down], 1)
                line_step_copy(chunk, step, down).start()

    def collect_copy(chunk, k):
        return remote(c_buf.at[chunk % c_sets, k], moved_piece(chunk, p),
                      c_send.at[chunk, k], c_recv.at[chunk, k], z * inner + mates[k])

    def collect_local(chunk):
        return pltpu.make_async_copy(c_buf.at[chunk % c_sets, 3], moved_piece(chunk, p), c_local.at[chunk])

    def collect_drain(chunk):
        for k in range(3):
            collect_copy(chunk, k).wait_send()
        if c_sets < chunks or chunk >= HALVES:
            collect_local(chunk).wait()

    def collect_send(chunk):
        step_recv(chunk, steps - 1)
        if chunk >= c_sets:
            collect_drain(chunk - c_sets)
        for k in range(4):
            place = mates[k] if k < 3 else p
            pick(chunk, last[0, z * inner + place, 0], c_buf.at[chunk % c_sets, k])
            if k < 3:
                collect_copy(chunk, k).start()
        collect_local(chunk).start()

    def collect_wait(chunk):
        for k in range(3):
            dst = moved_piece(chunk, mates[k])
            remote(dst, dst, c_send.at[chunk, k], c_recv.at[chunk, k], me).wait_recv()

    def share_copy(chunk, place):
        part = moved_piece(chunk, place)
        return pltpu.make_async_remote_copy(
            src_ref=part, dst_ref=part, send_sem=d_send.at[chunk, place], recv_sem=d_recv.at[chunk, place],
            device_id={"dp": 1 - my_dp}, device_id_type=MESH,
        )

    def share_got(chunk, place):
        flat = place * piece + chunk % HALVES * rows
        offset = pl.multiple_of(flat % rows_dp + (1 - my_dp) * rows_dp, rows)
        part = moved[0].at[flat // rows_dp, pl.ds(offset, rows)]
        return pltpu.make_async_remote_copy(
            src_ref=part, dst_ref=part, send_sem=d_send.at[chunk, place], recv_sem=d_recv.at[chunk, place],
            device_id={"dp": 1 - my_dp}, device_id_type=MESH,
        )

    own_copies = [pltpu.make_async_copy(own[a], held[a].at[z], o_local.at[a]) for a in range(3)]
    for copy in own_copies:
        copy.start()
    for chunk in range(2):
        spread_start(chunk)
    line_send(0)
    for chunk in range(2, 4):
        spread_start(chunk)
    for copy in own_copies:
        copy.wait()
    early = sets == line
    if early:
        pack_start(z, z)
    for chunk in range(4, chunks):
        spread_start(chunk)

    total = chunks * steps
    hooks = {}
    for hop in range(line - 1):
        todo = hooks.setdefault(1 + 2 * hop, [])
        todo.append(functools.partial(line_recv, hop))
        if hop + 1 < line - 1:
            todo.append(functools.partial(line_send, hop + 1))
        if early:
            todo.append(functools.partial(by_hop, hop, lambda plane: pack_start(plane, plane)))

    previous = {}
    number = 0
    for pair in range(chunks // 2):
        for step in range(steps):
            for chunk in (2 * pair, 2 * pair + 1):
                if step == 0:
                    spread_wait(chunk)
                else:
                    step_recv(chunk, step - 1)
                step_send(chunk, step, previous.get(chunk % 2))
                previous[chunk % 2] = (chunk, step)
                if step == 0 and pair > 0:
                    collect_send(chunk - 2)
                for hook in hooks.get(number, []):
                    hook()
                number += 1
    for chunk in range(HALVES):
        collect_wait(chunk)
        if c_sets == chunks:
            collect_local(chunk).wait()
        for place in range(inner):
            share_copy(chunk, place).start()
    for chunk in (chunks - 2, chunks - 1):
        collect_send(chunk)
    if not early:
        for plane in range(line):
            if plane >= sets:
                pack_drain(plane - sets, (plane - sets) % sets)
            pack_start(plane, plane % sets)

    for chunk in (chunks - 2, chunks - 1):
        step_drain(*previous[chunk % 2])
    for chunk in range(chunks - c_sets, chunks):
        collect_drain(chunk)
    for chunk in range(chunks):
        for k in range(3):
            spread_copy(chunk, k).wait_send()
        if chunk >= HALVES:
            collect_wait(chunk)
    for hop in range(line - 1):
        line_drain(hop)
    for plane in range(line):
        pack_recv(plane)
        if early or plane >= line - sets:
            pack_drain(plane, plane % sets)
    for chunk in range(HALVES):
        for place in range(inner):
            share_copy(chunk, place).wait_send()
            share_got(chunk, place).wait_recv()


def steps_most(inner):
    return 2 * inner


def move(line, inner, steps, number, cap, moves, last, tokens, cotangent, small, arrays):
    count = line * inner
    places, wide_rows, width = arrays[0].shape
    rows = wide_rows // HALVES
    rows_dp = places * wide_rows // 2
    chunks = len(arrays) * HALVES
    sets = line if steps <= inner + 1 else 1
    c_sets = chunks if steps <= inner + 1 else 2
    dma, regular = pltpu.SemaphoreType.DMA, pltpu.SemaphoreType.REGULAR
    gathers = (tokens, cotangent, small)
    vmem = pl.BlockSpec(memory_space=pltpu.VMEM)
    anywhere = pl.BlockSpec(memory_space=ANY)
    packed = jax.ShapeDtypeStruct((count, cap, tokens.shape[1]), tokens.dtype)
    return pl.pallas_call(
        functools.partial(move_kernel, line, inner, steps, sets),
        out_shape=(
            jax.ShapeDtypeStruct((2, 2 * rows_dp, width), jnp.bfloat16),
            jax.ShapeDtypeStruct((2, rows_dp, width), jnp.bfloat16),
            jax.ShapeDtypeStruct((2, rows_dp, width), jnp.bfloat16),
            packed,
            packed,
            jax.ShapeDtypeStruct((count,) + small.shape, small.dtype),
        ),
        in_specs=[pl.BlockSpec(memory_space=pltpu.SMEM)] * 2 + [vmem] * 3 + [anywhere] * len(arrays),
        out_specs=tuple([anywhere] * (len(arrays) + 3)),
        scratch_shapes=[pltpu.VMEM((inner + 2 * steps, rows, width), jnp.bfloat16) for _ in range(chunks)]
        + [pltpu.VMEM((line,) + g.shape, g.dtype) for g in gathers]
        + [
            pltpu.VMEM((2, sets, inner, cap, tokens.shape[1]), jnp.bfloat16),
            pltpu.VMEM((2, 2, rows, width), jnp.bfloat16),
            pltpu.VMEM((c_sets, 4, rows, width), jnp.bfloat16),
            dma((chunks, 3)), dma((chunks, 3)), dma((chunks,)),
            dma((2, 2)), dma((chunks, 2)), regular((chunks, 2)),
            dma((chunks, 3)), dma((chunks, 3)), dma((chunks,)),
            dma((3, 2, line - 1)), dma((3, 2, line - 1)),
            dma((line, 3)), dma((line, 3)), dma((line,)),
            dma((2, line, 3)), dma((2, line, 3)), dma((2, line)),
            dma((3,)),
            dma((HALVES, inner)), dma((HALVES, inner)),
        ],
        compiler_params=pltpu.CompilerParams(
            collective_id=number, has_side_effects=True, vmem_limit_bytes=61 * 1024 * 1024
        ),
        name="move%d" % steps,
    )(moves, last, tokens, cotangent, small, *arrays)


def planes_on_device(
    tokens, routes, gates, cotangent, owner_before, owner_after,
    weights, m_codes, v_codes, m_scales, v_scales, noise, inner,
):
    expert_count = lax.axis_size("expert")
    dp_count = lax.axis_size("dp")
    me = lax.axis_index("expert")
    my_dp = lax.axis_index("dp")
    line = expert_count // inner
    most = steps_most(inner)
    slot_ids = jnp.arange(expert_count, dtype=jnp.int32)
    my_source = jnp.sum((owner_after == me).astype(jnp.int32) * owner_before)
    rows_dp = weights.shape[2]
    hidden_units = weights.shape[3]
    model_width = tokens.shape[1]
    token_count = tokens.shape[0]
    cap = token_count * routes.shape[1] * 9 // (8 * expert_count)

    matches = routes[:, :, None] == slot_ids[None, None, :]
    dense_gates = jnp.sum(jnp.where(matches, gates[:, :, None], 0.0), axis=1).T
    named = jnp.sum(matches.astype(jnp.float32), axis=1).T
    order = jnp.arange(token_count, dtype=jnp.int32)
    earlier = (order[:, None] < order[None, :]).astype(jnp.float32)
    rank = jnp.where(named > 0, jnp.dot(named, earlier), -1.0)
    scales = jnp.concatenate([m_scales.reshape(-1), v_scales.reshape(-1)]).astype(jnp.float32)
    small = jnp.concatenate([dense_gates, rank, scales.reshape(-1, token_count)])

    moves, last, used = plan(owner_before, owner_after, line, inner, most)
    arrays = tuple(a.reshape(inner, 2 * rows_dp // inner, hidden_units) for a in (weights, m_codes, v_codes))
    sizes = [inner, inner + 1, most]
    branch = sum([(used > s).astype(jnp.int32) for s in sizes[:-1]])
    full_weights, moved_m, moved_v, all_tokens, gated, all_small = lax.optimization_barrier(
        lax.switch(
            branch,
            [functools.partial(move, line, inner, s, i, cap) for i, s in enumerate(sizes)],
            moves, last, tokens, cotangent, small, arrays,
        )
    )
    all_tokens = all_tokens.reshape(-1, model_width)
    gated = gated.reshape(-1, model_width)
    old_scales = lax.dynamic_index_in_dim(all_small, my_source, axis=0, keepdims=False)[2 * expert_count :]
    old_scales = old_scales.reshape(2, 2 * rows_dp)

    scale_model = model_width ** (-0.5)
    scale_hidden = hidden_units ** (-0.5)
    pre = jnp.dot(all_tokens, full_weights[0], preferred_element_type=jnp.float32) * scale_model
    back = jnp.dot(gated, full_weights[1], preferred_element_type=jnp.float32) * scale_hidden
    sigmoid_pre = jax.nn.sigmoid(pre)
    hidden = (pre * sigmoid_pre).astype(jnp.bfloat16)
    pre_grad = (back * sigmoid_pre * (1.0 + pre * (1.0 - sigmoid_pre))).astype(jnp.bfloat16)
    up_part = (transposed_dot(all_tokens, pre_grad) * scale_model).astype(jnp.bfloat16)
    down_part = (transposed_dot(gated, hidden) * scale_hidden).astype(jnp.bfloat16)
    swap = [(i, (i + 1) % dp_count) for i in range(dp_count)]

    def theirs(part):
        return lax.ppermute(lax.dynamic_slice(part, ((1 - my_dp) * rows_dp, 0), (rows_dp, hidden_units)), "dp", swap)

    other_up, other_down = theirs(up_part), theirs(down_part)
    flat = (2 * rows_dp, hidden_units)
    new_w, new_m, new_v, new_ms, new_vs = adam_rows(
        my_dp[None].astype(jnp.int32),
        up_part,
        down_part,
        other_up,
        other_down,
        full_weights.reshape(-1, hidden_units),
        moved_m.reshape(flat),
        moved_v.reshape(flat),
        old_scales,
        noise.reshape(flat),
    )
    return (
        new_w.reshape(2, 1, rows_dp, hidden_units),
        new_m.reshape(2, 1, rows_dp, hidden_units),
        new_v.reshape(2, 1, rows_dp, hidden_units),
        new_ms.reshape(2, 1, rows_dp),
        new_vs.reshape(2, 1, rows_dp),
    )


def on_device(
    tokens,
    routes,
    gates,
    cotangent,
    owner_before,
    owner_after,
    weights,
    m_codes,
    v_codes,
    m_scales,
    v_scales,
    noise,
):
    expert_count = lax.axis_size("expert")
    me = lax.axis_index("expert")
    slot_ids = jnp.arange(expert_count, dtype=jnp.int32)
    matches = (owner_after[None, :] == slot_ids[:, None]).astype(jnp.int32)
    source_slot = jnp.sum(matches * owner_before[None, :], axis=1)
    my_match = (owner_after == me).astype(jnp.int32)
    my_expert = jnp.sum(my_match * slot_ids)
    my_source = jnp.sum(my_match * owner_before)
    rows_dp = weights.shape[2]
    hidden_units = weights.shape[3]
    model_width = tokens.shape[1]
    token_count = tokens.shape[0]
    piece = 2 * rows_dp // expert_count

    dp_count = lax.axis_size("dp")
    my_dp = lax.axis_index("dp")

    def spread(array):
        shaped = array.reshape(expert_count, piece, hidden_units)
        return lax.all_to_all(shaped, "expert", split_axis=0, concat_axis=0, tiled=True)

    def collect(array):
        return lax.all_to_all(array, "expert", split_axis=0, concat_axis=0, tiled=True)

    def regroup(array):
        return array.at[source_slot].get(mode="promise_in_bounds")

    def shift(array, step):
        ring = [(i, (i + step) % dp_count) for i in range(dp_count)]
        return lax.ppermute(array, "dp", ring)

    dense_gates = jnp.sum(
        jnp.where(routes[:, :, None] == slot_ids[None, None, :], gates[:, :, None], 0.0), axis=1
    ).T
    scales = jnp.concatenate([m_scales.reshape(-1), v_scales.reshape(-1)]).astype(jnp.float32)
    small = jnp.concatenate([dense_gates, scales.reshape(-1, token_count)])
    all_small = lax.all_gather(small, "expert", axis=0, tiled=False)
    inner = 1
    while inner * inner * 4 <= expert_count and expert_count % (inner * 2) == 0:
        inner *= 2
    outer = expert_count // inner
    lines = [[i + inner * k for k in range(outer)] for i in range(inner)]
    planes = [[inner * k + i for i in range(inner)] for k in range(outer)]

    def gather_line(array):
        return lax.all_gather(array, "expert", axis=0, tiled=True, axis_index_groups=lines)

    def gather_plane(array):
        return lax.all_gather(array, "expert", axis=0, tiled=True, axis_index_groups=planes)

    line_tokens, all_small = lax.optimization_barrier((gather_line(tokens), all_small))
    all_tokens = gather_plane(line_tokens)
    all_cotangent = gather_plane(gather_line(cotangent))

    weights_ready, all_small = lax.optimization_barrier((regroup(spread(weights)), all_small))
    gate = lax.dynamic_index_in_dim(all_small, my_expert, axis=1, keepdims=False)
    gate = gate.reshape(outer, inner, token_count).swapaxes(0, 1).reshape(-1)
    old_scales = lax.dynamic_index_in_dim(all_small, my_source, axis=0, keepdims=False)[expert_count:]
    old_scales = old_scales.reshape(2, 2 * rows_dp)
    moved_weights = collect(weights_ready)
    moved_weights, m_codes = lax.optimization_barrier((moved_weights, m_codes))
    m_spread = spread(m_codes)
    m_spread, v_codes = lax.optimization_barrier((m_spread, v_codes))
    v_spread = spread(v_codes)
    m_ready, v_spread = lax.optimization_barrier((regroup(m_spread), v_spread))
    moved_m = collect(m_ready)
    v_ready, moved_m = lax.optimization_barrier((regroup(v_spread), moved_m))
    moved_v = collect(v_ready)
    moved_m, all_cotangent = lax.optimization_barrier((moved_m, all_cotangent))

    own_rows = moved_weights.reshape(2, rows_dp, hidden_units)
    full_weights = jnp.zeros((2, dp_count * rows_dp, hidden_units), jnp.bfloat16)
    full_weights = lax.dynamic_update_slice(full_weights, own_rows, (0, my_dp * rows_dp, 0))
    for step in range(1, dp_count):
        start = (my_dp - step) % dp_count * rows_dp
        full_weights = lax.dynamic_update_slice(full_weights, shift(own_rows, step), (0, start, 0))
    gated = (gate[:, None] * all_cotangent.astype(jnp.float32)).astype(jnp.bfloat16)
    scale_model = model_width ** (-0.5)
    scale_hidden = hidden_units ** (-0.5)
    pre = jnp.dot(all_tokens, full_weights[0], preferred_element_type=jnp.float32) * scale_model
    back = jnp.dot(gated, full_weights[1], preferred_element_type=jnp.float32) * scale_hidden
    sigmoid_pre = jax.nn.sigmoid(pre)
    hidden = (pre * sigmoid_pre).astype(jnp.bfloat16)
    pre_grad = (back * sigmoid_pre * (1.0 + pre * (1.0 - sigmoid_pre))).astype(jnp.bfloat16)
    up_part = (transposed_dot(all_tokens, pre_grad) * scale_model).astype(jnp.bfloat16)
    down_part = (transposed_dot(gated, hidden) * scale_hidden).astype(jnp.bfloat16)
    part = jnp.stack([up_part, down_part])
    grads = []
    for step in range(dp_count):
        start = (my_dp + step) % dp_count * rows_dp
        mine = lax.dynamic_slice(part, (0, start, 0), (2, rows_dp, hidden_units))
        grads.append((shift(mine, step) if step else mine).reshape(2 * rows_dp, hidden_units))
    new_w, new_m, new_v, new_ms, new_vs = adam(
        grads,
        moved_weights.reshape(2 * rows_dp, hidden_units),
        moved_m.reshape(2 * rows_dp, hidden_units),
        moved_v.reshape(2 * rows_dp, hidden_units),
        old_scales[0][:, None],
        old_scales[1][:, None],
        noise.reshape(2 * rows_dp, hidden_units),
    )
    return (
        new_w.reshape(2, 1, rows_dp, hidden_units),
        new_m.reshape(2, 1, rows_dp, hidden_units),
        new_v.reshape(2, 1, rows_dp, hidden_units),
        new_ms.reshape(2, 1, rows_dp),
        new_vs.reshape(2, 1, rows_dp),
    )


def solution(mesh):
    placed = (
        P(("expert", "dp"), None),
        P(("expert", "dp"), None),
        P(("expert", "dp"), None),
        P(("expert", "dp"), None),
        P(),
        P(),
        P(None, "expert", "dp", None),
        P(None, "expert", "dp", None),
        P(None, "expert", "dp", None),
        P(None, "expert", "dp"),
        P(None, "expert", "dp"),
        P(None, "expert", "dp", None),
    )
    inner = 4
    line = mesh.shape["expert"] // inner
    in_planes = mesh.shape["dp"] == 2 and mesh.shape["expert"] == line * inner and 2 <= line <= 4
    program = functools.partial(planes_on_device, inner=inner) if in_planes else on_device
    return jax.shard_map(
        program,
        mesh=mesh,
        in_specs=placed,
        out_specs=(
            P(None, "expert", "dp", None),
            P(None, "expert", "dp", None),
            P(None, "expert", "dp", None),
            P(None, "expert", "dp"),
            P(None, "expert", "dp"),
        ),
        check_vma=False,
    )
```

```python
import functools

import jax
import jax.numpy as jnp
from jax import lax
from jax.experimental import pallas as pl
from jax.experimental.pallas import tpu as pltpu
from jax.sharding import PartitionSpec as P

LEVELS = 7


learn_rate = 0.1
beta_one = 0.9
beta_two = 0.95
adam_step = 20.0
adam_epsilon = 1e-08
scale_epsilon = 1e-06

MESH = pl.DeviceIdType.MESH
ANY = pl.ANY
HALVES = 2
ROWS_AT_ONCE = 32
COLUMNS = 512


def transposed_dot(left, right):
    return lax.dot_general(
        left, right, (((0,), (0,)), ((), ())), preferred_element_type=jnp.float32
    )


def adam_kernel(parts, *refs):
    weight, m_code, v_code, m_scale, v_scale, noise, new_w, new_m, new_v, new_ms, new_vs = refs[parts:]
    grads = refs[0][...].astype(jnp.float32)
    for part in refs[1:parts]:
        grads += part[...].astype(jnp.float32)
    m_old = m_code[...].astype(jnp.float32) * (m_scale[...].astype(jnp.float32) / LEVELS)
    v_old = v_code[...].astype(jnp.float32) * (v_scale[...].astype(jnp.float32) / LEVELS)
    m_new = beta_one * m_old + (1.0 - beta_one) * grads
    v_new = beta_two * v_old + (1.0 - beta_two) * grads * grads
    direction = (
        m_new
        * (1.0 / (1.0 - beta_one**adam_step))
        / (jnp.sqrt(v_new * (1.0 / (1.0 - beta_two**adam_step))) + adam_epsilon)
    )
    new_w[...] = (weight[...].astype(jnp.float32) - learn_rate * direction).astype(jnp.bfloat16)
    m_top = (jnp.max(jnp.abs(m_new), axis=1, keepdims=True) + scale_epsilon).astype(jnp.bfloat16)
    v_top = (jnp.max(v_new, axis=1, keepdims=True) + scale_epsilon).astype(jnp.bfloat16)
    new_ms[...] = m_top
    new_vs[...] = v_top
    dither = noise[...].astype(jnp.float32)
    m_value = m_new * (LEVELS / m_top.astype(jnp.float32)) + (dither - 0.5)
    v_value = v_new * (LEVELS / v_top.astype(jnp.float32)) + dither
    new_m[...] = jnp.clip(m_value, -1.0 * LEVELS, 1.0 * LEVELS).astype(jnp.bfloat16)
    new_v[...] = jnp.clip(v_value, 0.0, 1.0 * LEVELS).astype(jnp.bfloat16)


def adam(grads, weight, m_code, v_code, m_scale, v_scale, noise):
    rows, width = weight.shape
    block = min(256, rows)
    wide = pl.BlockSpec((block, width), lambda i: (i, 0))
    thin = pl.BlockSpec((block, 1), lambda i: (i, 0))
    big = jax.ShapeDtypeStruct((rows, width), jnp.bfloat16)
    small = jax.ShapeDtypeStruct((rows, 1), jnp.bfloat16)
    return pl.pallas_call(
        functools.partial(adam_kernel, len(grads)),
        grid=(rows // block,),
        out_shape=(big, big, big, small, small),
        in_specs=[wide] * len(grads) + [wide, wide, wide, thin, thin, wide],
        out_specs=(wide, wide, wide, thin, thin),
        name="adam",
        cost_estimate=pl.CostEstimate(
            flops=30 * rows * width, bytes_accessed=16 * rows * width, transcendentals=2 * rows * width
        ),
    )(*grads, weight, m_code, v_code, m_scale, v_scale, noise)


def column(row):
    return jnp.transpose(jnp.broadcast_to(row, (128, row.shape[1])))[:, 0:1]


def adam_rows_kernel(dp, own, other, weight, m_code, v_code, scales, noise,
                     new_w, new_m, new_v, new_ms, new_vs):
    grads = own[...].astype(jnp.float32) + other[...].astype(jnp.float32)
    m_scale = column(scales[0, 0:1, :]) * (beta_one / LEVELS)
    v_scale = column(scales[0, 1:2, :]) * (beta_two / LEVELS)
    m_new = m_code[...].astype(jnp.float32) * m_scale + (1.0 - beta_one) * grads
    v_new = v_code[...].astype(jnp.float32) * v_scale + (1.0 - beta_two) * grads * grads
    root = (1.0 - beta_two**adam_step) ** 0.5
    rate = learn_rate * root / (1.0 - beta_one**adam_step)
    change = (rate * m_new) / (jnp.sqrt(v_new) + adam_epsilon * root)
    new_w[...] = (weight[...].astype(jnp.float32) - change).astype(jnp.bfloat16)
    m_top = (jnp.max(jnp.abs(m_new), axis=1, keepdims=True) + scale_epsilon).astype(jnp.bfloat16)
    v_top = (jnp.max(v_new, axis=1, keepdims=True) + scale_epsilon).astype(jnp.bfloat16)
    m_top, v_top = m_top.astype(jnp.float32), v_top.astype(jnp.float32)
    for top, out in ((m_top, new_ms), (v_top, new_vs)):
        lanes = jnp.transpose(jnp.broadcast_to(top, (top.shape[0], 128)))
        out[0] = lanes[0:1, :].astype(jnp.bfloat16)
    dither = noise[...].astype(jnp.float32)
    m_value = m_new * (LEVELS / m_top) + (dither - 0.5)
    v_value = v_new * (LEVELS / v_top) + dither
    new_m[...] = jnp.clip(m_value, -1.0 * LEVELS, 1.0 * LEVELS).astype(jnp.bfloat16)
    new_v[...] = jnp.clip(v_value, 0.0, 1.0 * LEVELS).astype(jnp.bfloat16)


def adam_rows(my_dp, own, other, full, m_code, v_code, scales, noise):
    rows, width = m_code.shape
    block = min(256, rows // 2)
    per = rows // 2 // block
    wide = pl.BlockSpec((block, width), lambda i, dp: (i, 0))
    held = pl.BlockSpec((block, width), lambda i, dp: (i // per * 2 * per + dp[0] * per + i % per, 0))
    thin = pl.BlockSpec((1, 2, block), lambda i, dp: (i, 0, 0))
    tops = pl.BlockSpec((1, 1, block), lambda i, dp: (i, 0, 0))
    big = jax.ShapeDtypeStruct((rows, width), jnp.bfloat16)
    small = jax.ShapeDtypeStruct((rows // block, 1, block), jnp.bfloat16)
    scales = scales.reshape(2, rows // block, block).swapaxes(0, 1)
    return pl.pallas_call(
        adam_rows_kernel,
        grid_spec=pltpu.PrefetchScalarGridSpec(
            num_scalar_prefetch=1,
            grid=(rows // block,),
            in_specs=[wide, wide, held, wide, wide, thin, wide],
            out_specs=(wide, wide, wide, tops, tops),
        ),
        out_shape=(big, big, big, small, small),
        name="adam_rows",
        cost_estimate=pl.CostEstimate(
            flops=30 * rows * width, bytes_accessed=16 * rows * width, transcendentals=2 * rows * width
        ),
    )(my_dp, own, other, full, m_code, v_code, scales, noise)


def plan_kernel(line, inner, steps, before, after, moves_ref, last_ref, used_ref):
    count = line * inner
    lanes = used_ref.shape[1]
    shape = (2 * line, lanes)
    lane = lax.broadcasted_iota(jnp.int32, shape, 1)
    row = lax.broadcasted_iota(jnp.int32, shape, 0)
    slot_row = lax.broadcasted_iota(jnp.int32, (count, lanes), 0)
    slot_lane = lax.broadcasted_iota(jnp.int32, (count, lanes), 1)
    dest = jnp.full(shape, -1, jnp.int32)
    wanted = jnp.full((count, lanes), -1, jnp.int32)
    holder = jnp.zeros((count, lanes), jnp.int32)
    for expert in range(count):
        dest = jnp.where(lane == before[expert], after[expert], dest)
        wanted = jnp.where(slot_lane == before[expert], after[expert], wanted)
        holder = jnp.where(slot_row == after[expert], expert, holder)
    node, down = row // 2, row % 2
    goal = dest // inner
    here = jnp.where(lane < count, lane // inner, -1)
    slot = lane % inner
    used = jnp.zeros((8, lanes), jnp.int32)
    far = jnp.abs(goal - node)
    wants = (goal - node) * (1 - 2 * down) > 0
    for step in range(steps):
        score = jnp.where((here == node) & wants, far * lanes + (lanes - 1 - lane), -1)
        best = jnp.max(score, axis=1, keepdims=True)
        chosen = (score == best) & (score >= 0)
        sent = jnp.max(jnp.where(chosen, slot, 0), axis=1, keepdims=True)
        moves_ref[step] = jnp.broadcast_to(sent, shape)
        move = jnp.sum(jnp.where(chosen, 1 - 2 * down, 0), axis=0, keepdims=True)
        move = jnp.broadcast_to(move, shape)
        here = here + move
        moved = move * move
        slot = slot * (1 - moved) + moved * (inner + 2 * step) + (moved - move) // 2
        any_sent = jnp.minimum(jnp.max(best, axis=0, keepdims=True) + 1, 1)
        used = jnp.maximum(used, jnp.broadcast_to(any_sent, used.shape) * (step + 1))
    used_ref[...] = used
    slots = jnp.broadcast_to(slot[0:1, :], (count, lanes))
    hits = jnp.where(wanted == slot_row, slots, 0)
    last_ref[0] = jnp.broadcast_to(jnp.sum(hits, axis=1, keepdims=True), (count, lanes))
    last_ref[1] = holder


def plan(before, after, line, inner, steps):
    count, lanes = line * inner, 128
    scalars = pl.BlockSpec(memory_space=pltpu.SMEM)
    moves, last, used = pl.pallas_call(
        functools.partial(plan_kernel, line, inner, steps),
        out_shape=(
            jax.ShapeDtypeStruct((steps, 2 * line, lanes), jnp.int32),
            jax.ShapeDtypeStruct((2, count, lanes), jnp.int32),
            jax.ShapeDtypeStruct((8, lanes), jnp.int32),
        ),
        in_specs=[scalars, scalars],
        name="plan",
    )(before, after)
    return moves, last, used[0, 0]


def move_kernel(line, inner, steps, sets, moves, last, tok_in, cot_in, small_in, *refs):
    arrays = 3
    chunks = arrays * HALVES
    own = (tok_in, cot_in, small_in)
    sources = refs[:arrays]
    moved = refs[arrays : 2 * arrays]
    packed = refs[2 * arrays : 2 * arrays + 2]
    all_small = refs[2 * arrays + 2]
    mine, other = refs[2 * arrays + 3 : 2 * arrays + 5]
    rest = list(refs[2 * arrays + 5 :])
    slots = rest[:chunks]
    held = rest[chunks : chunks + 3]
    (packs, b_buf, c_buf, a_send, a_recv, a_local, b_send, b_recv, credit, c_send, c_recv, c_local,
     z_send, z_recv, p_send, p_recv, p_local, x_send, x_recv, x_local, o_local, d_send, d_recv) = rest[chunks + 3 : chunks + 26]
    me = lax.axis_index("expert")
    my_dp = lax.axis_index("dp")
    z, p = me // inner, me % inner
    x, y = p % 2, p // 2
    mates = (y * 2 + (1 - x), (1 - y) * 2 + x, (1 - y) * 2 + (1 - x))
    experts = line * inner
    rows = slots[0].shape[1]
    piece = sources[0].shape[1]
    rows_dp = moved[1].shape[1]
    cap, width = packs.shape[3:]
    c_sets = c_buf.shape[0]
    above, below = z < line - 1, z > 0

    def at(place):
        return {"expert": place}

    def remote(src, dst, send, recv, place):
        return pltpu.make_async_remote_copy(
            src_ref=src, dst_ref=dst, send_sem=send, recv_sem=recv,
            device_id=at(place), device_id_type=MESH,
        )

    barrier = pltpu.get_barrier_semaphore()
    for mate in mates:
        pl.semaphore_signal(barrier, inc=1, device_id=at(z * inner + mate), device_id_type=MESH)
    pl.semaphore_signal(barrier, inc=1, device_id={"dp": 1 - my_dp}, device_id_type=MESH)

    @pl.when(above)
    def _():
        pl.semaphore_signal(barrier, inc=1, device_id=at(me + inner), device_id_type=MESH)

    @pl.when(below)
    def _():
        pl.semaphore_signal(barrier, inc=1, device_id=at(me - inner), device_id_type=MESH)

    middle = above & below

    @pl.when(middle)
    def _():
        pl.semaphore_wait(barrier, len(mates) + 3)

    @pl.when(jnp.logical_not(middle))
    def _():
        pl.semaphore_wait(barrier, len(mates) + 2)

    def line_copy(array, hop, down):
        if down:
            plane, place = z + hop, me - inner
        else:
            plane, place = z - hop, me + inner
        return remote(held[array].at[plane], held[array].at[plane], z_send.at[array, down, hop], z_recv.at[array, down, hop], place)

    def line_has(hop, down):
        return (below & (z + hop < line)) if down else (above & (z - hop >= 0))

    def line_send(hop):
        for down in range(2):
            @pl.when(line_has(hop, down))
            def _():
                for array in range(3):
                    line_copy(array, hop, down).start()

    def line_drain(hop):
        for down in range(2):
            @pl.when(line_has(hop, down))
            def _():
                for array in range(3):
                    line_copy(array, hop, down).wait_send()

    def line_came(hop, down):
        return (z + hop + 1 < line) if down else (z - hop - 1 >= 0)

    def line_recv(hop):
        for down in range(2):
            @pl.when(line_came(hop, down))
            def _():
                plane = z + hop + 1 if down else z - hop - 1
                for array in range(3):
                    dst = held[array].at[plane]
                    remote(dst, dst, z_send.at[array, down, hop], z_recv.at[array, down, hop], me).wait_recv()

    def by_hop(hop, action):
        for down in range(2):
            @pl.when(line_came(hop, down))
            def _():
                action(z + hop + 1 if down else z - hop - 1)

    def table_copy(plane, k):
        return remote(held[2].at[plane], all_small.at[plane * inner + p],
                      p_send.at[plane, k], p_recv.at[plane, k], z * inner + mates[k])

    def table_local(plane):
        return pltpu.make_async_copy(held[2].at[plane], all_small.at[plane * inner + p], p_local.at[plane])

    def pack(plane, one):
        small = held[2].at[plane]

        def for_place(place, carry):
            expert = last[1, z * inner + place, 0]
            chosen = lax.broadcasted_iota(jnp.int32, (experts, small.shape[1]), 0) == expert
            gate = jnp.sum(jnp.where(chosen, small[0:experts, :], 0.0), axis=0, keepdims=True)
            rank = jnp.sum(jnp.where(chosen, small[experts : 2 * experts, :], 0.0), axis=0, keepdims=True)
            count = lax.broadcasted_iota(jnp.int32, (cap, small.shape[1]), 0).astype(jnp.float32)
            hot = jnp.where(count == rank, 1.0, 0.0)
            gates = jnp.sum(hot * gate, axis=1, keepdims=True)
            hot = hot.astype(jnp.bfloat16)

            def for_columns(i, carry):
                part = pl.ds(pl.multiple_of(i * COLUMNS, COLUMNS), COLUMNS)
                packs[0, one, place, :, part] = jnp.dot(
                    hot, held[0][plane, :, part], preferred_element_type=jnp.float32
                ).astype(jnp.bfloat16)
                packs[1, one, place, :, part] = (gates * jnp.dot(
                    hot, held[1][plane, :, part], preferred_element_type=jnp.float32
                )).astype(jnp.bfloat16)
                return carry

            return lax.fori_loop(0, width // COLUMNS, for_columns, carry)

        lax.fori_loop(0, inner, for_place, 0)

    def packed_block(array, plane, place):
        return packed[array].at[pl.ds(pl.multiple_of((plane * inner + place) * cap, 8), cap)]

    def pack_copy(array, plane, one, k):
        return remote(packs.at[array, one, mates[k]], packed_block(array, plane, p),
                      x_send.at[array, plane, k], x_recv.at[array, plane, k], z * inner + mates[k])

    def pack_local(array, plane, one):
        return pltpu.make_async_copy(packs.at[array, one, p], packed_block(array, plane, p), x_local.at[array, plane])

    def pack_start(plane, one):
        pack(plane, one)
        for array in range(2):
            for k in range(3):
                pack_copy(array, plane, one, k).start()
            pack_local(array, plane, one).start()
        for k in range(3):
            table_copy(plane, k).start()
        table_local(plane).start()

    def pack_drain(plane, one):
        for array in range(2):
            for k in range(3):
                pack_copy(array, plane, one, k).wait_send()
            pack_local(array, plane, one).wait()

    def pack_recv(plane):
        for k in range(3):
            for array in range(2):
                dst = packed_block(array, plane, mates[k])
                remote(dst, dst, x_send.at[array, plane, k], x_recv.at[array, plane, k], me).wait_recv()
            dst = all_small.at[plane * inner + mates[k]]
            remote(dst, dst, p_send.at[plane, k], p_recv.at[plane, k], me).wait_recv()
            table_copy(plane, k).wait_send()
        table_local(plane).wait()

    def source_piece(chunk, place):
        return sources[chunk // HALVES].at[place, pl.ds(chunk % HALVES * rows, rows)]

    def moved_piece(chunk, place):
        flat = place * piece + chunk % HALVES * rows
        offset = flat % rows_dp
        if chunk < HALVES:
            offset = offset + my_dp * rows_dp
        return moved[chunk // HALVES].at[flat // rows_dp, pl.ds(pl.multiple_of(offset, rows), rows)]

    def spread_copy(chunk, k):
        return remote(source_piece(chunk, mates[k]), slots[chunk].at[p],
                      a_send.at[chunk, k], a_recv.at[chunk, k], z * inner + mates[k])

    def spread_local(chunk):
        return pltpu.make_async_copy(source_piece(chunk, p), slots[chunk].at[p], a_local.at[chunk])

    def spread_start(chunk):
        for k in range(3):
            spread_copy(chunk, k).start()
        spread_local(chunk).start()

    def spread_wait(chunk):
        for k in range(3):
            dst = slots[chunk].at[mates[k]]
            remote(dst, dst, a_send.at[chunk, k], a_recv.at[chunk, k], me).wait_recv()
        spread_local(chunk).wait()

    def line_step_copy(chunk, step, down):
        place = me - inner if down else me + inner
        return remote(b_buf.at[chunk % 2, down], slots[chunk].at[inner + 2 * step + down],
                      b_send.at[chunk % 2, down], b_recv.at[chunk, down], place)

    def step_recv(chunk, step):
        for down in range(2):
            @pl.when(above if down else below)
            def _():
                dst = slots[chunk].at[inner + 2 * step + down]
                remote(dst, dst, b_send.at[chunk % 2, down], b_recv.at[chunk, down], me).wait_recv()

    def pick(chunk, index, dst):
        def body(i, carry):
            part = pl.ds(i * ROWS_AT_ONCE, ROWS_AT_ONCE)
            dst[part, :] = slots[chunk][index, part, :]
            return carry

        lax.fori_loop(0, rows // ROWS_AT_ONCE, body, 0)

    def step_drain(chunk, step):
        for down in range(2):
            @pl.when(below if down else above)
            def _():
                line_step_copy(chunk, step, down).wait_send()

    def step_send(chunk, step, before):
        if before is not None:
            step_drain(*before)
        for down in range(2):
            @pl.when(below if down else above)
            def _():
                index = moves[step, z * 2 + down, 0]
                pick(chunk, index, b_buf.at[chunk % 2, down])
        for down in range(2):
            @pl.when(below if down else above)
            def _():
                pl.semaphore_signal(credit.at[chunk, 1 - down], inc=1,
                                    device_id=at(me - inner if down else me + inner), device_id_type=MESH)
        for down in range(2):
            @pl.when(below if down else above)
            def _():
                pl.semaphore_wait(credit.at[chunk, down], 1)
                line_step_copy(chunk, step, down).start()

    def collect_copy(chunk, k):
        return remote(c_buf.at[chunk % c_sets, k], moved_piece(chunk, p),
                      c_send.at[chunk, k], c_recv.at[chunk, k], z * inner + mates[k])

    def collect_local(chunk):
        return pltpu.make_async_copy(c_buf.at[chunk % c_sets, 3], moved_piece(chunk, p), c_local.at[chunk])

    def collect_drain(chunk):
        for k in range(3):
            collect_copy(chunk, k).wait_send()
        if c_sets < chunks or chunk >= HALVES:
            collect_local(chunk).wait()

    def collect_send(chunk):
        step_recv(chunk, steps - 1)
        if chunk >= c_sets:
            collect_drain(chunk - c_sets)
        for k in range(4):
            place = mates[k] if k < 3 else p
            pick(chunk, last[0, z * inner + place, 0], c_buf.at[chunk % c_sets, k])
            if k < 3:
                collect_copy(chunk, k).start()
        collect_local(chunk).start()

    def collect_wait(chunk):
        for k in range(3):
            dst = moved_piece(chunk, mates[k])
            remote(dst, dst, c_send.at[chunk, k], c_recv.at[chunk, k], me).wait_recv()

    def share_copy(chunk, place):
        part = moved_piece(chunk, place)
        return pltpu.make_async_remote_copy(
            src_ref=part, dst_ref=part, send_sem=d_send.at[chunk, place], recv_sem=d_recv.at[chunk, place],
            device_id={"dp": 1 - my_dp}, device_id_type=MESH,
        )

    def share_got(chunk, place):
        flat = place * piece + chunk % HALVES * rows
        offset = pl.multiple_of(flat % rows_dp + (1 - my_dp) * rows_dp, rows)
        part = moved[0].at[flat // rows_dp, pl.ds(offset, rows)]
        return pltpu.make_async_remote_copy(
            src_ref=part, dst_ref=part, send_sem=d_send.at[chunk, place], recv_sem=d_recv.at[chunk, place],
            device_id={"dp": 1 - my_dp}, device_id_type=MESH,
        )

    own_copies = [pltpu.make_async_copy(own[a], held[a].at[z], o_local.at[a]) for a in range(3)]
    for copy in own_copies:
        copy.start()
    for chunk in range(2):
        spread_start(chunk)
    for copy in own_copies:
        copy.wait()
    line_send(0)
    for chunk in range(2, 4):
        spread_start(chunk)
    early = sets == line
    if early:
        pack_start(z, z)
    for chunk in range(4, chunks):
        spread_start(chunk)

    total = chunks * steps
    hooks = {}
    for hop in range(line - 1):
        todo = hooks.setdefault(1 + 2 * hop, [])
        todo.append(functools.partial(line_recv, hop))
        if hop + 1 < line - 1:
            todo.append(functools.partial(line_send, hop + 1))
        if early:
            todo.append(functools.partial(by_hop, hop, lambda plane: pack_start(plane, plane)))

    previous = {}
    number = 0
    for pair in range(chunks // 2):
        for step in range(steps):
            for chunk in (2 * pair, 2 * pair + 1):
                if step == 0:
                    spread_wait(chunk)
                else:
                    step_recv(chunk, step - 1)
                step_send(chunk, step, previous.get(chunk % 2))
                previous[chunk % 2] = (chunk, step)
                if step == 0 and pair > 0:
                    collect_send(chunk - 2)
                for hook in hooks.get(number, []):
                    hook()
                number += 1
    for chunk in (chunks - 2, chunks - 1):
        collect_send(chunk)
    for chunk in range(HALVES):
        collect_wait(chunk)
        if c_sets == chunks:
            collect_local(chunk).wait()
        for place in range(inner):
            share_copy(chunk, place).start()
    if not early:
        for plane in range(line):
            if plane >= sets:
                pack_drain(plane - sets, (plane - sets) % sets)
            pack_start(plane, plane % sets)
    for hop in range(line - 1):
        line_drain(hop)
    for plane in range(line):
        pack_recv(plane)
        if early or plane >= line - sets:
            pack_drain(plane, plane % sets)
    for chunk in range(HALVES):
        for place in range(inner):
            share_copy(chunk, place).wait_send()
            share_got(chunk, place).wait_recv()
    gradients(moved[0], packed, mine, other, slots[:2], held[:2], my_dp, *rest[chunks + 26 :])

    for chunk in (chunks - 2, chunks - 1):
        step_drain(*previous[chunk % 2])
    for chunk in range(chunks - c_sets, chunks):
        collect_drain(chunk)
    for chunk in range(chunks):
        for k in range(3):
            spread_copy(chunk, k).wait_send()
        if chunk >= HALVES:
            collect_wait(chunk)


def gradients(full, packed, mine, other, tiles, lines, my_dp,
              hidden_ref, grad_ref, columns_ref, out_ref, w_sem, m_sem, k_sem, g_send, g_recv, g_local):
    total, hidden_units = hidden_ref.shape
    model_width = lines[0].shape[2]
    depth, height = lines[0].shape[:2]
    deep = tiles[0].shape[1]
    count = total // height
    scale_model = model_width ** (-0.5)
    scale_hidden = hidden_units ** (-0.5)
    wide = min(256, hidden_units)

    def weight_copy(matrix, k):
        return pltpu.make_async_copy(full.at[matrix, pl.ds(k * deep, deep)], tiles[matrix].at[k], w_sem.at[matrix, k])

    def row_copy(array, tile):
        rows = pl.ds(pl.multiple_of(tile * height, height), height)
        return pltpu.make_async_copy(packed[array].at[rows], lines[array].at[tile % depth], m_sem.at[array, tile % depth])

    part = columns_ref.shape[2]
    pieces = model_width // part

    def column_copy(array, i):
        one = i % 2
        return pltpu.make_async_copy(packed[array].at[:, pl.ds(pl.multiple_of(i * part, part), part)], columns_ref.at[one], k_sem.at[one])

    for k in range(model_width // deep):
        for matrix in range(2):
            weight_copy(matrix, k).start()
    for tile in range(min(depth, count)):
        for array in range(2):
            row_copy(array, tile).start()
    column_copy(0, 0).start()
    for k in range(model_width // deep):
        for matrix in range(2):
            weight_copy(matrix, k).wait()

    def for_tile(tile, carry):
        one = tile % depth
        for array in range(2):
            row_copy(array, tile).wait()

        def for_width(n, carry):
            cols = pl.ds(pl.multiple_of(n * wide, wide), wide)

            def product(array):
                out = jnp.zeros((height, wide), jnp.float32)
                for k in range(model_width // deep):
                    out += jnp.dot(
                        lines[array][one, :, k * deep : (k + 1) * deep], tiles[array][k, :, cols],
                        preferred_element_type=jnp.float32,
                    )
                return out

            pre = product(0) * scale_model
            back = product(1) * scale_hidden
            sigmoid_pre = 1.0 / (1.0 + jnp.exp(-pre))
            rows = pl.ds(pl.multiple_of(tile * height, height), height)
            hidden_ref[rows, cols] = (pre * sigmoid_pre).astype(jnp.bfloat16)
            grad_ref[rows, cols] = (back * sigmoid_pre * (1.0 + pre * (1.0 - sigmoid_pre))).astype(jnp.bfloat16)
            return carry

        lax.fori_loop(0, hidden_units // wide, for_width, 0)

        @pl.when(tile + depth < count)
        def _():
            for array in range(2):
                row_copy(array, tile + depth).start()

        return carry

    lax.fori_loop(0, count, for_tile, 0)

    half = model_width // 2
    sub = min(256, part)

    def keep(array, i, one):
        rows = pl.ds(pl.multiple_of(i * part % half, part), part)
        return pltpu.make_async_copy(out_ref.at[one], mine.at[array, rows], g_local.at[array, i])

    def give(array, i, one):
        rows = pl.ds(pl.multiple_of(i * part % half, part), part)
        return pltpu.make_async_remote_copy(
            src_ref=out_ref.at[one], dst_ref=other.at[array, rows], send_sem=g_send.at[array, i],
            recv_sem=g_recv.at[array, i], device_id={"dp": 1 - my_dp}, device_id_type=MESH,
        )

    def settle(array, i, one):
        is_mine = my_dp == i * part // half

        @pl.when(is_mine)
        def _():
            keep(array, i, one).wait()

        @pl.when(jnp.logical_not(is_mine))
        def _():
            give(array, i, one).wait_send()

    for array in range(2):
        right = (grad_ref, hidden_ref)[array]
        scale = (scale_model, scale_hidden)[array]

        def for_piece(i, carry):
            one = i % 2
            column_copy(array, i).wait()

            @pl.when(i + 1 < pieces)
            def _():
                column_copy(array, i + 1).start()

            if array == 0:
                @pl.when(i + 1 == pieces)
                def _():
                    column_copy(1, 0).start()

            @pl.when(i >= 2)
            def _():
                settle(array, i - 2, one)

            if array == 1:
                @pl.when(i < 2)
                def _():
                    settle(0, pieces - 2 + i, one)

            def for_part(j, carry):
                cols = pl.ds(pl.multiple_of(j * sub, sub), sub)
                out = transposed_dot(columns_ref[one, :, cols], right[...]) * scale
                out_ref[one, cols, :] = out.astype(jnp.bfloat16)
                return carry

            lax.fori_loop(0, part // sub, for_part, 0)
            is_mine = my_dp == i * part // half

            @pl.when(is_mine)
            def _():
                keep(array, i, one).start()

            @pl.when(jnp.logical_not(is_mine))
            def _():
                give(array, i, one).start()

            return carry

        lax.fori_loop(0, pieces, for_piece, 0)

    for number in range(2 * pieces - 2, 2 * pieces):
        settle(number // pieces, number % pieces, number % 2)
    for array in range(2):
        for i in range(pieces):
            @pl.when(my_dp == i * part // half)
            def _():
                give(array, i, 0).wait_recv()


def steps_most(inner):
    return 2 * inner


def move(line, inner, steps, number, cap, moves, last, tokens, cotangent, small, arrays):
    count = line * inner
    places, wide_rows, width = arrays[0].shape
    rows = wide_rows // HALVES
    rows_dp = places * wide_rows // 2
    chunks = len(arrays) * HALVES
    sets = line if steps <= inner + 2 else 1
    c_sets = chunks if steps <= inner + 1 else 2
    dma, regular = pltpu.SemaphoreType.DMA, pltpu.SemaphoreType.REGULAR
    gathers = (tokens, cotangent, small)
    anywhere = pl.BlockSpec(memory_space=ANY)
    model_width = tokens.shape[1]
    packed = jax.ShapeDtypeStruct((count * cap, model_width), tokens.dtype)
    half = jax.ShapeDtypeStruct((2, rows_dp, width), jnp.bfloat16)
    part = min(512, model_width // 2)
    extra = [
        pltpu.VMEM((count * cap, width), jnp.bfloat16),
        pltpu.VMEM((count * cap, width), jnp.bfloat16),
        pltpu.VMEM((2, count * cap, part), jnp.bfloat16),
        pltpu.VMEM((2, part, width), jnp.bfloat16),
        dma((2, model_width // rows)), dma((2, line)), dma((2,)),
        dma((2, model_width // part)), dma((2, model_width // part)), dma((2, model_width // part)),
    ]
    return pl.pallas_call(
        functools.partial(move_kernel, line, inner, steps, sets),
        out_shape=(
            jax.ShapeDtypeStruct((2, 2 * rows_dp, width), jnp.bfloat16),
            jax.ShapeDtypeStruct((2, rows_dp, width), jnp.bfloat16),
            jax.ShapeDtypeStruct((2, rows_dp, width), jnp.bfloat16),
            packed,
            packed,
            jax.ShapeDtypeStruct((count,) + small.shape, small.dtype),
        ) + (half, half),
        in_specs=[pl.BlockSpec(memory_space=pltpu.SMEM)] * 2 + [anywhere] * (3 + len(arrays)),
        out_specs=tuple([anywhere] * (len(arrays) + 5)),
        scratch_shapes=[pltpu.VMEM((inner + 2 * steps, rows, width), jnp.bfloat16) for _ in range(chunks)]
        + [pltpu.VMEM((line,) + g.shape, g.dtype) for g in gathers]
        + [
            pltpu.VMEM((2, sets, inner, cap, tokens.shape[1]), jnp.bfloat16),
            pltpu.VMEM((2, 2, rows, width), jnp.bfloat16),
            pltpu.VMEM((c_sets, 4, rows, width), jnp.bfloat16),
            dma((chunks, 3)), dma((chunks, 3)), dma((chunks,)),
            dma((2, 2)), dma((chunks, 2)), regular((chunks, 2)),
            dma((chunks, 3)), dma((chunks, 3)), dma((chunks,)),
            dma((3, 2, line - 1)), dma((3, 2, line - 1)),
            dma((line, 3)), dma((line, 3)), dma((line,)),
            dma((2, line, 3)), dma((2, line, 3)), dma((2, line)),
            dma((3,)),
            dma((HALVES, inner)), dma((HALVES, inner)),
        ]
        + extra,
        compiler_params=pltpu.CompilerParams(
            collective_id=number, has_side_effects=True, vmem_limit_bytes=67043328
        ),
        name="move%d" % steps,
    )(moves, last, tokens, cotangent, small, *arrays)


def planes_on_device(
    tokens, routes, gates, cotangent, owner_before, owner_after,
    weights, m_codes, v_codes, m_scales, v_scales, noise, inner,
):
    expert_count = lax.axis_size("expert")
    dp_count = lax.axis_size("dp")
    me = lax.axis_index("expert")
    my_dp = lax.axis_index("dp")
    line = expert_count // inner
    most = steps_most(inner)
    slot_ids = jnp.arange(expert_count, dtype=jnp.int32)
    my_source = jnp.sum((owner_after == me).astype(jnp.int32) * owner_before)
    rows_dp = weights.shape[2]
    hidden_units = weights.shape[3]
    model_width = tokens.shape[1]
    token_count = tokens.shape[0]
    cap = token_count * routes.shape[1] * 9 // (8 * expert_count)

    matches = routes[:, :, None] == slot_ids[None, None, :]
    dense_gates = jnp.sum(jnp.where(matches, gates[:, :, None], 0.0), axis=1).T
    named = jnp.sum(matches.astype(jnp.float32), axis=1).T
    order = jnp.arange(token_count, dtype=jnp.int32)
    earlier = (order[:, None] < order[None, :]).astype(jnp.float32)
    rank = jnp.where(named > 0, jnp.dot(named, earlier), -1.0)
    scales = jnp.concatenate([m_scales.reshape(-1), v_scales.reshape(-1)]).astype(jnp.float32)
    small = jnp.concatenate([dense_gates, rank, scales.reshape(-1, token_count)])

    moves, last, used = plan(owner_before, owner_after, line, inner, most)
    arrays = tuple(a.reshape(inner, 2 * rows_dp // inner, hidden_units) for a in (weights, m_codes, v_codes))
    sizes = [inner, inner + 1, inner + 2, most]
    branch = sum([(used > s).astype(jnp.int32) for s in sizes[:-1]])
    full_weights, moved_m, moved_v, _, _, all_small, own, other = lax.optimization_barrier(
        lax.switch(
            branch,
            [functools.partial(move, line, inner, s, i, cap) for i, s in enumerate(sizes)],
            moves, last, tokens, cotangent, small, arrays,
        )
    )
    old_scales = lax.dynamic_index_in_dim(all_small, my_source, axis=0, keepdims=False)[2 * expert_count :]
    old_scales = old_scales.reshape(2, 2 * rows_dp)
    flat = (2 * rows_dp, hidden_units)
    new_w, new_m, new_v, new_ms, new_vs = adam_rows(
        my_dp[None].astype(jnp.int32),
        own.reshape(flat),
        other.reshape(flat),
        full_weights.reshape(-1, hidden_units),
        moved_m.reshape(flat),
        moved_v.reshape(flat),
        old_scales,
        noise.reshape(flat),
    )
    return (
        new_w.reshape(2, 1, rows_dp, hidden_units),
        new_m.reshape(2, 1, rows_dp, hidden_units),
        new_v.reshape(2, 1, rows_dp, hidden_units),
        new_ms.reshape(2, 1, rows_dp),
        new_vs.reshape(2, 1, rows_dp),
    )


def on_device(
    tokens,
    routes,
    gates,
    cotangent,
    owner_before,
    owner_after,
    weights,
    m_codes,
    v_codes,
    m_scales,
    v_scales,
    noise,
):
    expert_count = lax.axis_size("expert")
    me = lax.axis_index("expert")
    slot_ids = jnp.arange(expert_count, dtype=jnp.int32)
    matches = (owner_after[None, :] == slot_ids[:, None]).astype(jnp.int32)
    source_slot = jnp.sum(matches * owner_before[None, :], axis=1)
    my_match = (owner_after == me).astype(jnp.int32)
    my_expert = jnp.sum(my_match * slot_ids)
    my_source = jnp.sum(my_match * owner_before)
    rows_dp = weights.shape[2]
    hidden_units = weights.shape[3]
    model_width = tokens.shape[1]
    token_count = tokens.shape[0]
    piece = 2 * rows_dp // expert_count

    dp_count = lax.axis_size("dp")
    my_dp = lax.axis_index("dp")

    def spread(array):
        shaped = array.reshape(expert_count, piece, hidden_units)
        return lax.all_to_all(shaped, "expert", split_axis=0, concat_axis=0, tiled=True)

    def collect(array):
        return lax.all_to_all(array, "expert", split_axis=0, concat_axis=0, tiled=True)

    def regroup(array):
        return array.at[source_slot].get(mode="promise_in_bounds")

    def shift(array, step):
        ring = [(i, (i + step) % dp_count) for i in range(dp_count)]
        return lax.ppermute(array, "dp", ring)

    dense_gates = jnp.sum(
        jnp.where(routes[:, :, None] == slot_ids[None, None, :], gates[:, :, None], 0.0), axis=1
    ).T
    scales = jnp.concatenate([m_scales.reshape(-1), v_scales.reshape(-1)]).astype(jnp.float32)
    small = jnp.concatenate([dense_gates, scales.reshape(-1, token_count)])
    all_small = lax.all_gather(small, "expert", axis=0, tiled=False)
    inner = 1
    while inner * inner * 4 <= expert_count and expert_count % (inner * 2) == 0:
        inner *= 2
    outer = expert_count // inner
    lines = [[i + inner * k for k in range(outer)] for i in range(inner)]
    planes = [[inner * k + i for i in range(inner)] for k in range(outer)]

    def gather_line(array):
        return lax.all_gather(array, "expert", axis=0, tiled=True, axis_index_groups=lines)

    def gather_plane(array):
        return lax.all_gather(array, "expert", axis=0, tiled=True, axis_index_groups=planes)

    line_tokens, all_small = lax.optimization_barrier((gather_line(tokens), all_small))
    all_tokens = gather_plane(line_tokens)
    all_cotangent = gather_plane(gather_line(cotangent))

    weights_ready, all_small = lax.optimization_barrier((regroup(spread(weights)), all_small))
    gate = lax.dynamic_index_in_dim(all_small, my_expert, axis=1, keepdims=False)
    gate = gate.reshape(outer, inner, token_count).swapaxes(0, 1).reshape(-1)
    old_scales = lax.dynamic_index_in_dim(all_small, my_source, axis=0, keepdims=False)[expert_count:]
    old_scales = old_scales.reshape(2, 2 * rows_dp)
    moved_weights = collect(weights_ready)
    moved_weights, m_codes = lax.optimization_barrier((moved_weights, m_codes))
    m_spread = spread(m_codes)
    m_spread, v_codes = lax.optimization_barrier((m_spread, v_codes))
    v_spread = spread(v_codes)
    m_ready, v_spread = lax.optimization_barrier((regroup(m_spread), v_spread))
    moved_m = collect(m_ready)
    v_ready, moved_m = lax.optimization_barrier((regroup(v_spread), moved_m))
    moved_v = collect(v_ready)
    moved_m, all_cotangent = lax.optimization_barrier((moved_m, all_cotangent))

    own_rows = moved_weights.reshape(2, rows_dp, hidden_units)
    full_weights = jnp.zeros((2, dp_count * rows_dp, hidden_units), jnp.bfloat16)
    full_weights = lax.dynamic_update_slice(full_weights, own_rows, (0, my_dp * rows_dp, 0))
    for step in range(1, dp_count):
        start = (my_dp - step) % dp_count * rows_dp
        full_weights = lax.dynamic_update_slice(full_weights, shift(own_rows, step), (0, start, 0))
    gated = (gate[:, None] * all_cotangent.astype(jnp.float32)).astype(jnp.bfloat16)
    scale_model = model_width ** (-0.5)
    scale_hidden = hidden_units ** (-0.5)
    pre = jnp.dot(all_tokens, full_weights[0], preferred_element_type=jnp.float32) * scale_model
    back = jnp.dot(gated, full_weights[1], preferred_element_type=jnp.float32) * scale_hidden
    sigmoid_pre = jax.nn.sigmoid(pre)
    hidden = (pre * sigmoid_pre).astype(jnp.bfloat16)
    pre_grad = (back * sigmoid_pre * (1.0 + pre * (1.0 - sigmoid_pre))).astype(jnp.bfloat16)
    up_part = (transposed_dot(all_tokens, pre_grad) * scale_model).astype(jnp.bfloat16)
    down_part = (transposed_dot(gated, hidden) * scale_hidden).astype(jnp.bfloat16)
    part = jnp.stack([up_part, down_part])
    grads = []
    for step in range(dp_count):
        start = (my_dp + step) % dp_count * rows_dp
        mine = lax.dynamic_slice(part, (0, start, 0), (2, rows_dp, hidden_units))
        grads.append((shift(mine, step) if step else mine).reshape(2 * rows_dp, hidden_units))
    new_w, new_m, new_v, new_ms, new_vs = adam(
        grads,
        moved_weights.reshape(2 * rows_dp, hidden_units),
        moved_m.reshape(2 * rows_dp, hidden_units),
        moved_v.reshape(2 * rows_dp, hidden_units),
        old_scales[0][:, None],
        old_scales[1][:, None],
        noise.reshape(2 * rows_dp, hidden_units),
    )
    return (
        new_w.reshape(2, 1, rows_dp, hidden_units),
        new_m.reshape(2, 1, rows_dp, hidden_units),
        new_v.reshape(2, 1, rows_dp, hidden_units),
        new_ms.reshape(2, 1, rows_dp),
        new_vs.reshape(2, 1, rows_dp),
    )


def solution(mesh):
    placed = (
        P(("expert", "dp"), None),
        P(("expert", "dp"), None),
        P(("expert", "dp"), None),
        P(("expert", "dp"), None),
        P(),
        P(),
        P(None, "expert", "dp", None),
        P(None, "expert", "dp", None),
        P(None, "expert", "dp", None),
        P(None, "expert", "dp"),
        P(None, "expert", "dp"),
        P(None, "expert", "dp", None),
    )
    inner = 4
    line = mesh.shape["expert"] // inner
    in_planes = mesh.shape["dp"] == 2 and mesh.shape["expert"] == line * inner and 2 <= line <= 4
    program = functools.partial(planes_on_device, inner=inner) if in_planes else on_device
    return jax.shard_map(
        program,
        mesh=mesh,
        in_specs=placed,
        out_specs=(
            P(None, "expert", "dp", None),
            P(None, "expert", "dp", None),
            P(None, "expert", "dp", None),
            P(None, "expert", "dp"),
            P(None, "expert", "dp"),
        ),
        check_vma=False,
    )
```

```python
import functools

import jax
import jax.numpy as jnp
from jax import lax
from jax.experimental import pallas as pl
from jax.experimental.pallas import tpu as pltpu
from jax.sharding import PartitionSpec as P

LEVELS = 7


learn_rate = 0.1
beta_one = 0.9
beta_two = 0.95
adam_step = 20.0
adam_epsilon = 1e-08
scale_epsilon = 1e-06

MESH = pl.DeviceIdType.MESH
ANY = pl.ANY
HALVES = 2
ROWS_AT_ONCE = 32
COLUMNS = 512


def transposed_dot(left, right):
    return lax.dot_general(
        left, right, (((0,), (0,)), ((), ())), preferred_element_type=jnp.float32
    )


def adam_kernel(parts, *refs):
    weight, m_code, v_code, m_scale, v_scale, noise, new_w, new_m, new_v, new_ms, new_vs = refs[parts:]
    grads = refs[0][...].astype(jnp.float32)
    for part in refs[1:parts]:
        grads += part[...].astype(jnp.float32)
    m_old = m_code[...].astype(jnp.float32) * (m_scale[...].astype(jnp.float32) / LEVELS)
    v_old = v_code[...].astype(jnp.float32) * (v_scale[...].astype(jnp.float32) / LEVELS)
    m_new = beta_one * m_old + (1.0 - beta_one) * grads
    v_new = beta_two * v_old + (1.0 - beta_two) * grads * grads
    direction = (
        m_new
        * (1.0 / (1.0 - beta_one**adam_step))
        / (jnp.sqrt(v_new * (1.0 / (1.0 - beta_two**adam_step))) + adam_epsilon)
    )
    new_w[...] = (weight[...].astype(jnp.float32) - learn_rate * direction).astype(jnp.bfloat16)
    m_top = (jnp.max(jnp.abs(m_new), axis=1, keepdims=True) + scale_epsilon).astype(jnp.bfloat16)
    v_top = (jnp.max(v_new, axis=1, keepdims=True) + scale_epsilon).astype(jnp.bfloat16)
    new_ms[...] = m_top
    new_vs[...] = v_top
    dither = noise[...].astype(jnp.float32)
    m_value = m_new * (LEVELS / m_top.astype(jnp.float32)) + (dither - 0.5)
    v_value = v_new * (LEVELS / v_top.astype(jnp.float32)) + dither
    new_m[...] = jnp.clip(m_value, -1.0 * LEVELS, 1.0 * LEVELS).astype(jnp.bfloat16)
    new_v[...] = jnp.clip(v_value, 0.0, 1.0 * LEVELS).astype(jnp.bfloat16)


def adam(grads, weight, m_code, v_code, m_scale, v_scale, noise):
    rows, width = weight.shape
    block = min(256, rows)
    wide = pl.BlockSpec((block, width), lambda i: (i, 0))
    thin = pl.BlockSpec((block, 1), lambda i: (i, 0))
    big = jax.ShapeDtypeStruct((rows, width), jnp.bfloat16)
    small = jax.ShapeDtypeStruct((rows, 1), jnp.bfloat16)
    return pl.pallas_call(
        functools.partial(adam_kernel, len(grads)),
        grid=(rows // block,),
        out_shape=(big, big, big, small, small),
        in_specs=[wide] * len(grads) + [wide, wide, wide, thin, thin, wide],
        out_specs=(wide, wide, wide, thin, thin),
        name="adam",
        cost_estimate=pl.CostEstimate(
            flops=30 * rows * width, bytes_accessed=16 * rows * width, transcendentals=2 * rows * width
        ),
    )(*grads, weight, m_code, v_code, m_scale, v_scale, noise)


def column(rows):
    parts = [jnp.transpose(jnp.broadcast_to(rows[i : i + 1, :], (128, rows.shape[1])))[:, 0:1] for i in range(rows.shape[0])]
    return jnp.concatenate(parts, axis=0)


def adam_rows_kernel(per, first, who, own, other, weight, m_code, v_code, scales, noise,
                     new_w, new_m, new_v, new_ms, new_vs, m_tops, v_tops):
    grads = own[...].astype(jnp.float32) + other[...].astype(jnp.float32)
    number = pl.program_id(0)
    block = own.shape[0]
    lines = block // scales.shape[2]
    m_row = first + number * lines
    m_scale = column(scales[0, pl.ds(m_row, lines), :]) * (beta_one / LEVELS)
    v_scale = column(scales[0, pl.ds(m_row + 2 * per * lines, lines), :]) * (beta_two / LEVELS)
    m_new = m_code[...].astype(jnp.float32) * m_scale + (1.0 - beta_one) * grads
    v_new = v_code[...].astype(jnp.float32) * v_scale + (1.0 - beta_two) * grads * grads
    root = (1.0 - beta_two**adam_step) ** 0.5
    rate = learn_rate * root / (1.0 - beta_one**adam_step)
    change = (rate * m_new) / (jnp.sqrt(v_new) + adam_epsilon * root)
    new_w[...] = (weight[...].astype(jnp.float32) - change).astype(jnp.bfloat16)
    m_top = (jnp.max(jnp.abs(m_new), axis=1, keepdims=True) + scale_epsilon).astype(jnp.bfloat16)
    v_top = (jnp.max(v_new, axis=1, keepdims=True) + scale_epsilon).astype(jnp.bfloat16)
    m_top, v_top = m_top.astype(jnp.float32), v_top.astype(jnp.float32)
    for top, tops in ((m_top, m_tops), (v_top, v_tops)):
        lanes = jnp.transpose(jnp.broadcast_to(top, (block, 128)))
        tops[pl.ds(number // per, 1), pl.ds(pl.multiple_of(number % per * block, block), block)] = lanes[0:1, :]

    @pl.when(number == 2 * per - 1)
    def _():
        new_ms[...] = m_tops[...].astype(jnp.bfloat16)
        new_vs[...] = v_tops[...].astype(jnp.bfloat16)

    dither = noise[...].astype(jnp.float32)
    m_value = m_new * (LEVELS / m_top) + (dither - 0.5)
    v_value = v_new * (LEVELS / v_top) + dither
    new_m[...] = jnp.clip(m_value, -1.0 * LEVELS, 1.0 * LEVELS).astype(jnp.bfloat16)
    new_v[...] = jnp.clip(v_value, 0.0, 1.0 * LEVELS).astype(jnp.bfloat16)


def adam_rows(who, first, own, other, full, m_code, v_code, scales, noise):
    rows, width = m_code.shape
    block = min(256, rows // 2)
    per = rows // 2 // block
    wide = pl.BlockSpec((block, width), lambda i, who: (i, 0))
    held = pl.BlockSpec((block, width), lambda i, who: (i // per * 2 * per + who[0] * per + i % per, 0))
    table = pl.BlockSpec((1,) + scales.shape[1:], lambda i, who: (who[1], 0, 0))
    tops = pl.BlockSpec((2, rows // 2), lambda i, who: (0, 0))
    big = jax.ShapeDtypeStruct((rows, width), jnp.bfloat16)
    small = jax.ShapeDtypeStruct((2, rows // 2), jnp.bfloat16)
    return pl.pallas_call(
        functools.partial(adam_rows_kernel, per, first),
        grid_spec=pltpu.PrefetchScalarGridSpec(
            num_scalar_prefetch=1,
            grid=(rows // block,),
            in_specs=[wide, wide, held, wide, wide, table, wide],
            out_specs=(wide, wide, wide, tops, tops),
            scratch_shapes=[pltpu.VMEM((2, rows // 2), jnp.float32)] * 2,
        ),
        out_shape=(big, big, big, small, small),
        name="adam_rows",
        cost_estimate=pl.CostEstimate(
            flops=30 * rows * width, bytes_accessed=16 * rows * width, transcendentals=2 * rows * width
        ),
    )(who, own, other, full, m_code, v_code, scales, noise)


def plan_kernel(line, inner, steps, before, after, moves_ref, last_ref, used_ref, who_ref):
    count = line * inner
    lanes = used_ref.shape[1]
    shape = (2 * line, lanes)
    lane = lax.broadcasted_iota(jnp.int32, shape, 1)
    row = lax.broadcasted_iota(jnp.int32, shape, 0)
    slot_row = lax.broadcasted_iota(jnp.int32, (count, lanes), 0)
    slot_lane = lax.broadcasted_iota(jnp.int32, (count, lanes), 1)
    dest = jnp.full(shape, -1, jnp.int32)
    wanted = jnp.full((count, lanes), -1, jnp.int32)
    holder = jnp.zeros((count, lanes), jnp.int32)
    for expert in range(count):
        dest = jnp.where(lane == before[expert], after[expert], dest)
        wanted = jnp.where(slot_lane == before[expert], after[expert], wanted)
        holder = jnp.where(slot_row == after[expert], expert, holder)
    node, down = row // 2, row % 2
    goal = dest // inner
    here = jnp.where(lane < count, lane // inner, -1)
    slot = lane % inner
    used = jnp.zeros((8, lanes), jnp.int32)
    far = jnp.abs(goal - node)
    wants = (goal - node) * (1 - 2 * down) > 0
    for step in range(steps):
        score = jnp.where((here == node) & wants, far * lanes + (lanes - 1 - lane), -1)
        best = jnp.max(score, axis=1, keepdims=True)
        chosen = (score == best) & (score >= 0)
        sent = jnp.max(jnp.where(chosen, slot, 0), axis=1, keepdims=True)
        moves_ref[step] = jnp.broadcast_to(sent, shape)
        move = jnp.sum(jnp.where(chosen, 1 - 2 * down, 0), axis=0, keepdims=True)
        move = jnp.broadcast_to(move, shape)
        here = here + move
        moved = move * move
        slot = slot * (1 - moved) + moved * (inner + 2 * step) + (moved - move) // 2
        any_sent = jnp.minimum(jnp.max(best, axis=0, keepdims=True) + 1, 1)
        used = jnp.maximum(used, jnp.broadcast_to(any_sent, used.shape) * (step + 1))
    used_ref[...] = used
    slots = jnp.broadcast_to(slot[0:1, :], (count, lanes))
    hits = jnp.where(wanted == slot_row, slots, 0)
    last_ref[0] = jnp.broadcast_to(jnp.sum(hits, axis=1, keepdims=True), (count, lanes))
    last_ref[1] = holder
    me = lax.axis_index("expert")
    source = 0
    for expert in range(count):
        source = jnp.where(after[expert] == me, before[expert], source)
    who_ref[0] = lax.axis_index("dp")
    who_ref[1] = source


def plan(before, after, line, inner, steps):
    count, lanes = line * inner, 128
    scalars = pl.BlockSpec(memory_space=pltpu.SMEM)
    whole = pl.BlockSpec(memory_space=pltpu.VMEM)
    moves, last, used, who = pl.pallas_call(
        functools.partial(plan_kernel, line, inner, steps),
        out_shape=(
            jax.ShapeDtypeStruct((steps, 2 * line, lanes), jnp.int32),
            jax.ShapeDtypeStruct((2, count, lanes), jnp.int32),
            jax.ShapeDtypeStruct((8, lanes), jnp.int32),
            jax.ShapeDtypeStruct((2,), jnp.int32),
        ),
        in_specs=[scalars, scalars],
        out_specs=(whole, whole, whole, scalars),
        name="plan",
    )(before, after)
    return moves, last, used[0, 0], who


def move_kernel(line, inner, steps, sets, moves, last, tok_in, cot_in, small_in, *refs):
    arrays = 3
    chunks = arrays * HALVES
    own = (tok_in, cot_in, small_in)
    sources = refs[:arrays]
    moved = refs[arrays : 2 * arrays]
    packed = refs[2 * arrays : 2 * arrays + 2]
    all_small = refs[2 * arrays + 2]
    mine, other = refs[2 * arrays + 3 : 2 * arrays + 5]
    rest = list(refs[2 * arrays + 5 :])
    slots = rest[:chunks]
    held = rest[chunks : chunks + 3]
    (packs, b_buf, c_buf, a_send, a_recv, a_local, b_send, b_recv, credit, c_send, c_recv, c_local,
     z_send, z_recv, p_send, p_recv, p_local, x_send, x_recv, x_local, o_local, d_send, d_recv) = rest[chunks + 3 : chunks + 26]
    me = lax.axis_index("expert")
    my_dp = lax.axis_index("dp")
    z, p = me // inner, me % inner
    x, y = p % 2, p // 2
    mates = (y * 2 + (1 - x), (1 - y) * 2 + x, (1 - y) * 2 + (1 - x))
    experts = line * inner
    rows = slots[0].shape[1]
    piece = sources[0].shape[1]
    rows_dp = moved[1].shape[1]
    cap, width = packs.shape[3:]
    c_sets = c_buf.shape[0]
    above, below = z < line - 1, z > 0

    def at(place):
        return {"expert": place}

    def remote(src, dst, send, recv, place):
        return pltpu.make_async_remote_copy(
            src_ref=src, dst_ref=dst, send_sem=send, recv_sem=recv,
            device_id=at(place), device_id_type=MESH,
        )

    barrier = pltpu.get_barrier_semaphore()
    for mate in mates:
        pl.semaphore_signal(barrier, inc=1, device_id=at(z * inner + mate), device_id_type=MESH)
    pl.semaphore_signal(barrier, inc=1, device_id={"dp": 1 - my_dp}, device_id_type=MESH)

    @pl.when(above)
    def _():
        pl.semaphore_signal(barrier, inc=1, device_id=at(me + inner), device_id_type=MESH)

    @pl.when(below)
    def _():
        pl.semaphore_signal(barrier, inc=1, device_id=at(me - inner), device_id_type=MESH)

    middle = above & below

    @pl.when(middle)
    def _():
        pl.semaphore_wait(barrier, len(mates) + 3)

    @pl.when(jnp.logical_not(middle))
    def _():
        pl.semaphore_wait(barrier, len(mates) + 2)

    def line_copy(array, hop, down):
        if down:
            plane, place = z + hop, me - inner
        else:
            plane, place = z - hop, me + inner
        return remote(held[array].at[plane], held[array].at[plane], z_send.at[array, down, hop], z_recv.at[array, down, hop], place)

    def line_has(hop, down):
        return (below & (z + hop < line)) if down else (above & (z - hop >= 0))

    def line_send(hop):
        for down in range(2):
            @pl.when(line_has(hop, down))
            def _():
                for array in range(3):
                    line_copy(array, hop, down).start()

    def line_drain(hop):
        for down in range(2):
            @pl.when(line_has(hop, down))
            def _():
                for array in range(3):
                    line_copy(array, hop, down).wait_send()

    def line_came(hop, down):
        return (z + hop + 1 < line) if down else (z - hop - 1 >= 0)

    def line_recv(hop):
        for down in range(2):
            @pl.when(line_came(hop, down))
            def _():
                plane = z + hop + 1 if down else z - hop - 1
                for array in range(3):
                    dst = held[array].at[plane]
                    remote(dst, dst, z_send.at[array, down, hop], z_recv.at[array, down, hop], me).wait_recv()

    def by_hop(hop, action):
        for down in range(2):
            @pl.when(line_came(hop, down))
            def _():
                action(z + hop + 1 if down else z - hop - 1)

    def table_copy(plane, k):
        return remote(held[2].at[plane], all_small.at[plane * inner + p],
                      p_send.at[plane, k], p_recv.at[plane, k], z * inner + mates[k])

    def table_local(plane):
        return pltpu.make_async_copy(held[2].at[plane], all_small.at[plane * inner + p], p_local.at[plane])

    def pack(plane, one):
        small = held[2].at[plane]

        def for_place(place, carry):
            expert = last[1, z * inner + place, 0]
            chosen = lax.broadcasted_iota(jnp.int32, (experts, small.shape[1]), 0) == expert
            gate = jnp.sum(jnp.where(chosen, small[0:experts, :], 0.0), axis=0, keepdims=True)
            rank = jnp.sum(jnp.where(chosen, small[experts : 2 * experts, :], 0.0), axis=0, keepdims=True)
            count = lax.broadcasted_iota(jnp.int32, (cap, small.shape[1]), 0).astype(jnp.float32)
            hot = jnp.where(count == rank, 1.0, 0.0)
            gates = jnp.sum(hot * gate, axis=1, keepdims=True)
            hot = hot.astype(jnp.bfloat16)

            def for_columns(i, carry):
                part = pl.ds(pl.multiple_of(i * COLUMNS, COLUMNS), COLUMNS)
                packs[0, one, place, :, part] = jnp.dot(
                    hot, held[0][plane, :, part], preferred_element_type=jnp.float32
                ).astype(jnp.bfloat16)
                packs[1, one, place, :, part] = (gates * jnp.dot(
                    hot, held[1][plane, :, part], preferred_element_type=jnp.float32
                )).astype(jnp.bfloat16)
                return carry

            return lax.fori_loop(0, width // COLUMNS, for_columns, carry)

        lax.fori_loop(0, inner, for_place, 0)

    def packed_block(array, plane, place):
        return packed[array].at[pl.ds(pl.multiple_of((plane * inner + place) * cap, 8), cap)]

    def pack_copy(array, plane, one, k):
        return remote(packs.at[array, one, mates[k]], packed_block(array, plane, p),
                      x_send.at[array, plane, k], x_recv.at[array, plane, k], z * inner + mates[k])

    def pack_local(array, plane, one):
        return pltpu.make_async_copy(packs.at[array, one, p], packed_block(array, plane, p), x_local.at[array, plane])

    def pack_start(plane, one):
        pack(plane, one)
        for array in range(2):
            for k in range(3):
                pack_copy(array, plane, one, k).start()
            pack_local(array, plane, one).start()
        for k in range(3):
            table_copy(plane, k).start()
        table_local(plane).start()

    def pack_drain(plane, one):
        for array in range(2):
            for k in range(3):
                pack_copy(array, plane, one, k).wait_send()
            pack_local(array, plane, one).wait()

    def pack_recv(plane):
        for k in range(3):
            for array in range(2):
                dst = packed_block(array, plane, mates[k])
                remote(dst, dst, x_send.at[array, plane, k], x_recv.at[array, plane, k], me).wait_recv()
            dst = all_small.at[plane * inner + mates[k]]
            remote(dst, dst, p_send.at[plane, k], p_recv.at[plane, k], me).wait_recv()
            table_copy(plane, k).wait_send()
        table_local(plane).wait()

    def source_piece(chunk, place):
        return sources[chunk // HALVES].at[place, pl.ds(chunk % HALVES * rows, rows)]

    def moved_piece(chunk, place):
        flat = place * piece + chunk % HALVES * rows
        offset = flat % rows_dp
        if chunk < HALVES:
            offset = offset + my_dp * rows_dp
        return moved[chunk // HALVES].at[flat // rows_dp, pl.ds(pl.multiple_of(offset, rows), rows)]

    def spread_copy(chunk, k):
        return remote(source_piece(chunk, mates[k]), slots[chunk].at[p],
                      a_send.at[chunk, k], a_recv.at[chunk, k], z * inner + mates[k])

    def spread_local(chunk):
        return pltpu.make_async_copy(source_piece(chunk, p), slots[chunk].at[p], a_local.at[chunk])

    def spread_start(chunk):
        for k in range(3):
            spread_copy(chunk, k).start()
        spread_local(chunk).start()

    def spread_wait(chunk):
        for k in range(3):
            dst = slots[chunk].at[mates[k]]
            remote(dst, dst, a_send.at[chunk, k], a_recv.at[chunk, k], me).wait_recv()
        spread_local(chunk).wait()

    def line_step_copy(chunk, step, down):
        place = me - inner if down else me + inner
        return remote(b_buf.at[chunk % 2, down], slots[chunk].at[inner + 2 * step + down],
                      b_send.at[chunk % 2, down], b_recv.at[chunk, down], place)

    def step_recv(chunk, step):
        for down in range(2):
            @pl.when(above if down else below)
            def _():
                dst = slots[chunk].at[inner + 2 * step + down]
                remote(dst, dst, b_send.at[chunk % 2, down], b_recv.at[chunk, down], me).wait_recv()

    def pick(chunk, index, dst):
        def body(i, carry):
            part = pl.ds(i * ROWS_AT_ONCE, ROWS_AT_ONCE)
            dst[part, :] = slots[chunk][index, part, :]
            return carry

        lax.fori_loop(0, rows // ROWS_AT_ONCE, body, 0)

    def step_drain(chunk, step):
        for down in range(2):
            @pl.when(below if down else above)
            def _():
                line_step_copy(chunk, step, down).wait_send()

    def step_send(chunk, step, before):
        if before is not None:
            step_drain(*before)
        for down in range(2):
            @pl.when(below if down else above)
            def _():
                index = moves[step, z * 2 + down, 0]
                pick(chunk, index, b_buf.at[chunk % 2, down])
        for down in range(2):
            @pl.when(below if down else above)
            def _():
                pl.semaphore_signal(credit.at[chunk, 1 - down], inc=1,
                                    device_id=at(me - inner if down else me + inner), device_id_type=MESH)
        for down in range(2):
            @pl.when(below if down else above)
            def _():
                pl.semaphore_wait(credit.at[chunk, down], 1)
                line_step_copy(chunk, step, down).start()

    def collect_copy(chunk, k):
        return remote(c_buf.at[chunk % c_sets, k], moved_piece(chunk, p),
                      c_send.at[chunk, k], c_recv.at[chunk, k], z * inner + mates[k])

    def collect_local(chunk):
        return pltpu.make_async_copy(c_buf.at[chunk % c_sets, 3], moved_piece(chunk, p), c_local.at[chunk])

    settled = set()

    def collect_settle(chunk):
        if chunk not in settled:
            settled.add(chunk)
            collect_local(chunk).wait()

    def collect_drain(chunk):
        for k in range(3):
            collect_copy(chunk, k).wait_send()
        collect_settle(chunk)

    def collect_send(chunk):
        step_recv(chunk, steps - 1)
        if chunk >= c_sets:
            collect_drain(chunk - c_sets)
        for k in range(4):
            place = mates[k] if k < 3 else p
            pick(chunk, last[0, z * inner + place, 0], c_buf.at[chunk % c_sets, k])
            if k < 3:
                collect_copy(chunk, k).start()
        collect_local(chunk).start()

    def collect_wait(chunk):
        for k in range(3):
            dst = moved_piece(chunk, mates[k])
            remote(dst, dst, c_send.at[chunk, k], c_recv.at[chunk, k], me).wait_recv()

    def share_copy(chunk, place):
        part = moved_piece(chunk, place)
        return pltpu.make_async_remote_copy(
            src_ref=part, dst_ref=part, send_sem=d_send.at[chunk, place], recv_sem=d_recv.at[chunk, place],
            device_id={"dp": 1 - my_dp}, device_id_type=MESH,
        )

    def share_got(chunk, place):
        flat = place * piece + chunk % HALVES * rows
        offset = pl.multiple_of(flat % rows_dp + (1 - my_dp) * rows_dp, rows)
        part = moved[0].at[flat // rows_dp, pl.ds(offset, rows)]
        return pltpu.make_async_remote_copy(
            src_ref=part, dst_ref=part, send_sem=d_send.at[chunk, place], recv_sem=d_recv.at[chunk, place],
            device_id={"dp": 1 - my_dp}, device_id_type=MESH,
        )

    own_copies = [pltpu.make_async_copy(own[a], held[a].at[z], o_local.at[a]) for a in range(3)]
    for copy in own_copies:
        copy.start()
    for chunk in range(2):
        spread_start(chunk)
    for copy in own_copies:
        copy.wait()
    line_send(0)
    for chunk in range(2, 4):
        spread_start(chunk)
    early = sets == line
    if early:
        pack_start(z, z)
    for chunk in range(4, chunks):
        spread_start(chunk)

    total = chunks * steps
    hooks = {}
    for hop in range(line - 1):
        todo = hooks.setdefault(1 + 2 * hop, [])
        todo.append(functools.partial(line_recv, hop))
        if hop + 1 < line - 1:
            todo.append(functools.partial(line_send, hop + 1))
        if early:
            todo.append(functools.partial(by_hop, hop, lambda plane: pack_start(plane, plane)))

    def share():
        for chunk in range(HALVES):
            collect_wait(chunk)
            collect_settle(chunk)
            for place in range(inner):
                share_copy(chunk, place).start()

    def ready():
        if not early:
            for plane in range(line):
                if plane >= sets:
                    pack_drain(plane - sets, (plane - sets) % sets)
                pack_start(plane, plane % sets)
        for hop in range(line - 1):
            line_drain(hop)
        for plane in range(line):
            pack_recv(plane)
            if early or plane >= line - sets:
                pack_drain(plane, plane % sets)
        for chunk in range(HALVES):
            for place in range(inner):
                share_copy(chunk, place).wait_send()
                share_got(chunk, place).wait_recv()

    stages = [share, ready] + gradients(
        moved[0], packed, mine, other, slots[:2], held[:2], my_dp, *rest[chunks + 26 :]
    )
    if inner < steps <= inner + 2:
        for number in range(total - 8, total - 1):
            hooks.setdefault(number, []).append(stages.pop(0))

    lead = steps // 2
    lanes = [[(chunk, step) for chunk in range(lane, chunks, 2) for step in range(steps)] for lane in range(2)]
    units = lanes[0][:lead]
    for i, unit in enumerate(lanes[1]):
        units.append(unit)
        units.extend(lanes[0][lead + i : lead + i + 1])
    previous = {}
    for number, (chunk, step) in enumerate(units):
        if step == 0:
            spread_wait(chunk)
        else:
            step_recv(chunk, step - 1)
        step_send(chunk, step, previous.get(chunk % 2))
        previous[chunk % 2] = (chunk, step)
        if step == 0 and chunk >= 2:
            collect_send(chunk - 2)
        if (chunk, step) == (chunks - 1, steps - lead):
            collect_send(chunks - 2)
        for hook in hooks.get(number, []):
            hook()
    collect_send(chunks - 1)
    for stage in stages:
        stage()

    for chunk in (chunks - 2, chunks - 1):
        step_drain(*previous[chunk % 2])
    for chunk in range(chunks - c_sets, chunks):
        collect_drain(chunk)
    for chunk in range(chunks):
        for k in range(3):
            spread_copy(chunk, k).wait_send()
        if chunk >= HALVES:
            collect_wait(chunk)


def gradients(full, packed, mine, other, tiles, lines, my_dp,
              hidden_ref, grad_ref, columns_ref, out_ref, w_sem, m_sem, k_sem, g_send, g_recv, g_local):
    total, hidden_units = hidden_ref.shape
    model_width = lines[0].shape[2]
    depth, height = lines[0].shape[:2]
    deep = tiles[0].shape[1]
    count = total // height
    scale_model = model_width ** (-0.5)
    scale_hidden = hidden_units ** (-0.5)
    wide = min(256, hidden_units)

    def weight_copy(matrix, k):
        return pltpu.make_async_copy(full.at[matrix, pl.ds(k * deep, deep)], tiles[matrix].at[k], w_sem.at[matrix, k])

    def row_copy(array, tile):
        rows = pl.ds(pl.multiple_of(tile * height, height), height)
        return pltpu.make_async_copy(packed[array].at[rows], lines[array].at[tile % depth], m_sem.at[array, tile % depth])

    part = columns_ref.shape[2]
    pieces = model_width // part

    def column_copy(array, i):
        one = i % 2
        return pltpu.make_async_copy(packed[array].at[:, pl.ds(pl.multiple_of(i * part, part), part)], columns_ref.at[one], k_sem.at[one])

    def load():
        for k in range(model_width // deep):
            for matrix in range(2):
                weight_copy(matrix, k).start()
        for tile in range(min(depth, count)):
            for array in range(2):
                row_copy(array, tile).start()
        column_copy(0, 0).start()
        for k in range(model_width // deep):
            for matrix in range(2):
                weight_copy(matrix, k).wait()

    def for_tile(tile, carry):
        one = tile % depth
        for array in range(2):
            row_copy(array, tile).wait()

        def for_width(n, carry):
            cols = pl.ds(pl.multiple_of(n * wide, wide), wide)

            def product(array):
                out = jnp.zeros((height, wide), jnp.float32)
                for k in range(model_width // deep):
                    out += jnp.dot(
                        lines[array][one, :, k * deep : (k + 1) * deep], tiles[array][k, :, cols],
                        preferred_element_type=jnp.float32,
                    )
                return out

            pre = product(0) * scale_model
            back = product(1) * scale_hidden
            sigmoid_pre = 1.0 / (1.0 + jnp.exp(-pre))
            rows = pl.ds(pl.multiple_of(tile * height, height), height)
            hidden_ref[rows, cols] = (pre * sigmoid_pre).astype(jnp.bfloat16)
            grad_ref[rows, cols] = (back * sigmoid_pre * (1.0 + pre * (1.0 - sigmoid_pre))).astype(jnp.bfloat16)
            return carry

        lax.fori_loop(0, hidden_units // wide, for_width, 0)

        @pl.when(tile + depth < count)
        def _():
            for array in range(2):
                row_copy(array, tile + depth).start()

        return carry

    def tiles_between(first, stop):
        lax.fori_loop(first, stop, for_tile, 0)

    half = model_width // 2
    sub = min(256, part)

    def keep(array, i, one):
        rows = pl.ds(pl.multiple_of(i * part % half, part), part)
        return pltpu.make_async_copy(out_ref.at[one], mine.at[array, rows], g_local.at[array, i])

    def give(array, i, one):
        rows = pl.ds(pl.multiple_of(i * part % half, part), part)
        return pltpu.make_async_remote_copy(
            src_ref=out_ref.at[one], dst_ref=other.at[array, rows], send_sem=g_send.at[array, i],
            recv_sem=g_recv.at[array, i], device_id={"dp": 1 - my_dp}, device_id_type=MESH,
        )

    def settle(array, i, one):
        is_mine = my_dp == i * part // half

        @pl.when(is_mine)
        def _():
            keep(array, i, one).wait()

        @pl.when(jnp.logical_not(is_mine))
        def _():
            give(array, i, one).wait_send()

    def pieces_between(array, first, stop):
        right = (grad_ref, hidden_ref)[array]
        scale = (scale_model, scale_hidden)[array]

        def for_piece(i, carry):
            one = i % 2
            column_copy(array, i).wait()

            @pl.when(i + 1 < pieces)
            def _():
                column_copy(array, i + 1).start()

            if array == 0:
                @pl.when(i + 1 == pieces)
                def _():
                    column_copy(1, 0).start()

            @pl.when(i >= 2)
            def _():
                settle(array, i - 2, one)

            if array == 1:
                @pl.when(i < 2)
                def _():
                    settle(0, pieces - 2 + i, one)

            def for_part(j, carry):
                cols = pl.ds(pl.multiple_of(j * sub, sub), sub)
                out = transposed_dot(columns_ref[one, :, cols], right[...]) * scale
                out_ref[one, cols, :] = out.astype(jnp.bfloat16)
                return carry

            lax.fori_loop(0, part // sub, for_part, 0)
            is_mine = my_dp == i * part // half

            @pl.when(is_mine)
            def _():
                keep(array, i, one).start()

            @pl.when(jnp.logical_not(is_mine))
            def _():
                give(array, i, one).start()

            return carry

        lax.fori_loop(first, stop, for_piece, 0)

    def finish():
        for number in range(2 * pieces - 2, 2 * pieces):
            settle(number // pieces, number % pieces, number % 2)
        for array in range(2):
            for i in range(pieces):
                @pl.when(my_dp == i * part // half)
                def _():
                    give(array, i, 0).wait_recv()

    third = -(-count // 3)
    stages = [load]
    for first in range(0, count, third):
        stages.append(functools.partial(tiles_between, first, min(count, first + third)))
    for array in range(2):
        for first in range(0, pieces, 2):
            stages.append(functools.partial(pieces_between, array, first, min(pieces, first + 2)))
    return stages + [finish]


def steps_most(inner):
    return 2 * inner


def move(line, inner, steps, number, cap, moves, last, tokens, cotangent, small, arrays):
    count = line * inner
    places, wide_rows, width = arrays[0].shape
    rows = wide_rows // HALVES
    rows_dp = places * wide_rows // 2
    chunks = len(arrays) * HALVES
    sets = line if steps <= inner + 2 else 1
    c_sets = chunks if steps <= inner + 1 else 3 if steps == inner + 2 else 2
    dma, regular = pltpu.SemaphoreType.DMA, pltpu.SemaphoreType.REGULAR
    gathers = (tokens, cotangent, small)
    anywhere = pl.BlockSpec(memory_space=ANY)
    model_width = tokens.shape[1]
    packed = jax.ShapeDtypeStruct((count * cap, model_width), tokens.dtype)
    half = jax.ShapeDtypeStruct((2, rows_dp, width), jnp.bfloat16)
    part = min(512, model_width // 2)
    extra = [
        pltpu.VMEM((count * cap, width), jnp.bfloat16),
        pltpu.VMEM((count * cap, width), jnp.bfloat16),
        pltpu.VMEM((2, count * cap, part), jnp.bfloat16),
        pltpu.VMEM((2, part, width), jnp.bfloat16),
        dma((2, model_width // rows)), dma((2, line)), dma((2,)),
        dma((2, model_width // part)), dma((2, model_width // part)), dma((2, model_width // part)),
    ]
    return pl.pallas_call(
        functools.partial(move_kernel, line, inner, steps, sets),
        out_shape=(
            jax.ShapeDtypeStruct((2, 2 * rows_dp, width), jnp.bfloat16),
            jax.ShapeDtypeStruct((2, rows_dp, width), jnp.bfloat16),
            jax.ShapeDtypeStruct((2, rows_dp, width), jnp.bfloat16),
            packed,
            packed,
            jax.ShapeDtypeStruct((count,) + small.shape, small.dtype),
        ) + (half, half),
        in_specs=[pl.BlockSpec(memory_space=pltpu.SMEM)] * 2 + [anywhere] * (3 + len(arrays)),
        out_specs=tuple([anywhere] * (len(arrays) + 5)),
        scratch_shapes=[pltpu.VMEM((inner + 2 * steps, rows, width), jnp.bfloat16) for _ in range(chunks)]
        + [pltpu.VMEM((line,) + g.shape, g.dtype) for g in gathers]
        + [
            pltpu.VMEM((2, sets, inner, cap, tokens.shape[1]), jnp.bfloat16),
            pltpu.VMEM((2, 2, rows, width), jnp.bfloat16),
            pltpu.VMEM((c_sets, 4, rows, width), jnp.bfloat16),
            dma((chunks, 3)), dma((chunks, 3)), dma((chunks,)),
            dma((2, 2)), dma((chunks, 2)), regular((chunks, 2)),
            dma((chunks, 3)), dma((chunks, 3)), dma((chunks,)),
            dma((3, 2, line - 1)), dma((3, 2, line - 1)),
            dma((line, 3)), dma((line, 3)), dma((line,)),
            dma((2, line, 3)), dma((2, line, 3)), dma((2, line)),
            dma((3,)),
            dma((HALVES, inner)), dma((HALVES, inner)),
        ]
        + extra,
        compiler_params=pltpu.CompilerParams(
            collective_id=number, has_side_effects=True, vmem_limit_bytes=67043328
        ),
        name="move%d" % steps,
    )(moves, last, tokens, cotangent, small, *arrays)


def planes_on_device(
    tokens, routes, gates, cotangent, owner_before, owner_after,
    weights, m_codes, v_codes, m_scales, v_scales, noise, inner,
):
    expert_count = lax.axis_size("expert")
    dp_count = lax.axis_size("dp")
    me = lax.axis_index("expert")
    my_dp = lax.axis_index("dp")
    line = expert_count // inner
    most = steps_most(inner)
    slot_ids = jnp.arange(expert_count, dtype=jnp.int32)
    rows_dp = weights.shape[2]
    hidden_units = weights.shape[3]
    model_width = tokens.shape[1]
    token_count = tokens.shape[0]
    cap = token_count * routes.shape[1] * 9 // (8 * expert_count)

    matches = routes[:, :, None] == slot_ids[None, None, :]
    dense_gates = jnp.sum(jnp.where(matches, gates[:, :, None], 0.0), axis=1).T
    named = jnp.sum(matches.astype(jnp.float32), axis=1).T
    order = jnp.arange(token_count, dtype=jnp.int32)
    earlier = (order[:, None] < order[None, :]).astype(jnp.float32)
    rank = jnp.where(named > 0, jnp.dot(named, earlier), -1.0)
    scales = jnp.concatenate([m_scales.reshape(-1), v_scales.reshape(-1)]).astype(jnp.float32)
    small = jnp.concatenate([dense_gates, rank, scales.reshape(-1, token_count)])

    moves, last, used, who = plan(owner_before, owner_after, line, inner, most)
    arrays = tuple(a.reshape(inner, 2 * rows_dp // inner, hidden_units) for a in (weights, m_codes, v_codes))
    sizes = [inner, inner + 1, inner + 2, most]
    branch = sum([(used > s).astype(jnp.int32) for s in sizes[:-1]])
    full_weights, moved_m, moved_v, _, _, all_small, own, other = lax.optimization_barrier(
        lax.switch(
            branch,
            [functools.partial(move, line, inner, s, i, cap) for i, s in enumerate(sizes)],
            moves, last, tokens, cotangent, small, arrays,
        )
    )
    flat = (2 * rows_dp, hidden_units)
    new_w, new_m, new_v, new_ms, new_vs = adam_rows(
        who,
        2 * expert_count,
        own.reshape(flat),
        other.reshape(flat),
        full_weights.reshape(-1, hidden_units),
        moved_m.reshape(flat),
        moved_v.reshape(flat),
        all_small,
        noise.reshape(flat),
    )
    return (
        new_w.reshape(2, 1, rows_dp, hidden_units),
        new_m.reshape(2, 1, rows_dp, hidden_units),
        new_v.reshape(2, 1, rows_dp, hidden_units),
        new_ms.reshape(2, 1, rows_dp),
        new_vs.reshape(2, 1, rows_dp),
    )


def on_device(
    tokens,
    routes,
    gates,
    cotangent,
    owner_before,
    owner_after,
    weights,
    m_codes,
    v_codes,
    m_scales,
    v_scales,
    noise,
):
    expert_count = lax.axis_size("expert")
    me = lax.axis_index("expert")
    slot_ids = jnp.arange(expert_count, dtype=jnp.int32)
    matches = (owner_after[None, :] == slot_ids[:, None]).astype(jnp.int32)
    source_slot = jnp.sum(matches * owner_before[None, :], axis=1)
    my_match = (owner_after == me).astype(jnp.int32)
    my_expert = jnp.sum(my_match * slot_ids)
    my_source = jnp.sum(my_match * owner_before)
    rows_dp = weights.shape[2]
    hidden_units = weights.shape[3]
    model_width = tokens.shape[1]
    token_count = tokens.shape[0]
    piece = 2 * rows_dp // expert_count

    dp_count = lax.axis_size("dp")
    my_dp = lax.axis_index("dp")

    def spread(array):
        shaped = array.reshape(expert_count, piece, hidden_units)
        return lax.all_to_all(shaped, "expert", split_axis=0, concat_axis=0, tiled=True)

    def collect(array):
        return lax.all_to_all(array, "expert", split_axis=0, concat_axis=0, tiled=True)

    def regroup(array):
        return array.at[source_slot].get(mode="promise_in_bounds")

    def shift(array, step):
        ring = [(i, (i + step) % dp_count) for i in range(dp_count)]
        return lax.ppermute(array, "dp", ring)

    dense_gates = jnp.sum(
        jnp.where(routes[:, :, None] == slot_ids[None, None, :], gates[:, :, None], 0.0), axis=1
    ).T
    scales = jnp.concatenate([m_scales.reshape(-1), v_scales.reshape(-1)]).astype(jnp.float32)
    small = jnp.concatenate([dense_gates, scales.reshape(-1, token_count)])
    all_small = lax.all_gather(small, "expert", axis=0, tiled=False)
    inner = 1
    while inner * inner * 4 <= expert_count and expert_count % (inner * 2) == 0:
        inner *= 2
    outer = expert_count // inner
    lines = [[i + inner * k for k in range(outer)] for i in range(inner)]
    planes = [[inner * k + i for i in range(inner)] for k in range(outer)]

    def gather_line(array):
        return lax.all_gather(array, "expert", axis=0, tiled=True, axis_index_groups=lines)

    def gather_plane(array):
        return lax.all_gather(array, "expert", axis=0, tiled=True, axis_index_groups=planes)

    line_tokens, all_small = lax.optimization_barrier((gather_line(tokens), all_small))
    all_tokens = gather_plane(line_tokens)
    all_cotangent = gather_plane(gather_line(cotangent))

    weights_ready, all_small = lax.optimization_barrier((regroup(spread(weights)), all_small))
    gate = lax.dynamic_index_in_dim(all_small, my_expert, axis=1, keepdims=False)
    gate = gate.reshape(outer, inner, token_count).swapaxes(0, 1).reshape(-1)
    old_scales = lax.dynamic_index_in_dim(all_small, my_source, axis=0, keepdims=False)[expert_count:]
    old_scales = old_scales.reshape(2, 2 * rows_dp)
    moved_weights = collect(weights_ready)
    moved_weights, m_codes = lax.optimization_barrier((moved_weights, m_codes))
    m_spread = spread(m_codes)
    m_spread, v_codes = lax.optimization_barrier((m_spread, v_codes))
    v_spread = spread(v_codes)
    m_ready, v_spread = lax.optimization_barrier((regroup(m_spread), v_spread))
    moved_m = collect(m_ready)
    v_ready, moved_m = lax.optimization_barrier((regroup(v_spread), moved_m))
    moved_v = collect(v_ready)
    moved_m, all_cotangent = lax.optimization_barrier((moved_m, all_cotangent))

    own_rows = moved_weights.reshape(2, rows_dp, hidden_units)
    full_weights = jnp.zeros((2, dp_count * rows_dp, hidden_units), jnp.bfloat16)
    full_weights = lax.dynamic_update_slice(full_weights, own_rows, (0, my_dp * rows_dp, 0))
    for step in range(1, dp_count):
        start = (my_dp - step) % dp_count * rows_dp
        full_weights = lax.dynamic_update_slice(full_weights, shift(own_rows, step), (0, start, 0))
    gated = (gate[:, None] * all_cotangent.astype(jnp.float32)).astype(jnp.bfloat16)
    scale_model = model_width ** (-0.5)
    scale_hidden = hidden_units ** (-0.5)
    pre = jnp.dot(all_tokens, full_weights[0], preferred_element_type=jnp.float32) * scale_model
    back = jnp.dot(gated, full_weights[1], preferred_element_type=jnp.float32) * scale_hidden
    sigmoid_pre = jax.nn.sigmoid(pre)
    hidden = (pre * sigmoid_pre).astype(jnp.bfloat16)
    pre_grad = (back * sigmoid_pre * (1.0 + pre * (1.0 - sigmoid_pre))).astype(jnp.bfloat16)
    up_part = (transposed_dot(all_tokens, pre_grad) * scale_model).astype(jnp.bfloat16)
    down_part = (transposed_dot(gated, hidden) * scale_hidden).astype(jnp.bfloat16)
    part = jnp.stack([up_part, down_part])
    grads = []
    for step in range(dp_count):
        start = (my_dp + step) % dp_count * rows_dp
        mine = lax.dynamic_slice(part, (0, start, 0), (2, rows_dp, hidden_units))
        grads.append((shift(mine, step) if step else mine).reshape(2 * rows_dp, hidden_units))
    new_w, new_m, new_v, new_ms, new_vs = adam(
        grads,
        moved_weights.reshape(2 * rows_dp, hidden_units),
        moved_m.reshape(2 * rows_dp, hidden_units),
        moved_v.reshape(2 * rows_dp, hidden_units),
        old_scales[0][:, None],
        old_scales[1][:, None],
        noise.reshape(2 * rows_dp, hidden_units),
    )
    return (
        new_w.reshape(2, 1, rows_dp, hidden_units),
        new_m.reshape(2, 1, rows_dp, hidden_units),
        new_v.reshape(2, 1, rows_dp, hidden_units),
        new_ms.reshape(2, 1, rows_dp),
        new_vs.reshape(2, 1, rows_dp),
    )


def solution(mesh):
    placed = (
        P(("expert", "dp"), None),
        P(("expert", "dp"), None),
        P(("expert", "dp"), None),
        P(("expert", "dp"), None),
        P(),
        P(),
        P(None, "expert", "dp", None),
        P(None, "expert", "dp", None),
        P(None, "expert", "dp", None),
        P(None, "expert", "dp"),
        P(None, "expert", "dp"),
        P(None, "expert", "dp", None),
    )
    inner = 4
    line = mesh.shape["expert"] // inner
    in_planes = mesh.shape["dp"] == 2 and mesh.shape["expert"] == line * inner and 2 <= line <= 4
    program = functools.partial(planes_on_device, inner=inner) if in_planes else on_device
    return jax.shard_map(
        program,
        mesh=mesh,
        in_specs=placed,
        out_specs=(
            P(None, "expert", "dp", None),
            P(None, "expert", "dp", None),
            P(None, "expert", "dp", None),
            P(None, "expert", "dp"),
            P(None, "expert", "dp"),
        ),
        check_vma=False,
    )
```
